32 devices in a mesh: gx: 8 (over z, core), gy: 4 (over y, x).
Axes of the slice: x: 2, y: 2, z: 4, core: 2. Of those that a mesh axis runs over, the one named last changes fastest.
Arguments:
- bin_state: float32 [132, 64, 512], P(None, 'gx', 'gy'), may hold values from 0.05 to 2
- courant_x: float32 [64, 512], P('gx', 'gy'), may hold values from -0.4 to 0.4
- courant_y: float32 [64, 512], P('gx', 'gy'), may hold values from -0.4 to 0.4
- cloudy_order: int32 [8, 4, 8], P('gx', 'gy'), may hold values from 0 to 7, each once within a row
- block_count: int32 [4, 8], P('gy', 'gx'), may hold values from 1 to 8, 40 in all within a row
- gain_kernel: bfloat16 [10, 33, 1089], replicated, may hold values from -0.059814453 to 0.059814453
- loss_rate: bfloat16 [10, 33, 33], replicated, may hold values from 9.9658966e-05 to 0.029907227
Outputs:
- state_out: float32 [132, 64, 512], P(None, 'gx', 'gy')
The draws below stay inside these ranges and needn't reach their ends.
Inputs may be any that keep to these rules, and one draw needn't show every extreme that they name: `cloudy_order`: each device's row holds each of its 8 block numbers once. `block_count`: each row of 8 counts sums to 40, and its largest count is 8.
All inputs are finite; a program needn't handle non-finite values. No bound on the sum of `block_count` on one device may be relied on, other than what follows from the above.
Results may differ from the reference program's by a relative error of at most 0.0034.
Values may be sent and summed in bfloat16 or wider, within the bound.
No kernel may reach another device: no remote copies, remote signals or barrier semaphores. Data moves between devices by JAX's collectives and lax.ppermute only.
A program may use at most 128 MiB of HBM per device.

```python
import math
import jax
import jax.numpy as jnp
import numpy as np
from jax import lax

BINS = 33
CLASSES = 4
PAIRS = 10
COMPS = 132
LEV = 4
BLOCK = 128
CX = 8
STEPS = 2
MEANB = 5
MAXB = 8
NX = 64
NY = 128
N_GX = 8
N_GY = 4


def block_levels(stream_key, extent, split, smallest, high):
    factor_of, own = 1.0, jax.random.fold_in(stream_key, 6)
    for position, parts in split:
        heights = jnp.exp(jax.random.uniform(jax.random.fold_in(own, position), (parts,), jnp.float32, smallest / len(split), high / len(split)))
        factor_of = factor_of * jnp.repeat(heights, extent[position] // parts).reshape([-1 if axis == position else 1 for axis in range(len(extent))])
    return factor_of


def profile(count, total, bound, lean):
    portions = [(1 << 20) // math.isqrt(rank ** lean) + 1 for rank in range(2, count + 1)]
    rest, given = total - bound - (count - 1), [1] * (count - 1)
    while rest > 0:
        movable = [i for i in range(count - 1) if given[i] < bound]
        pool, remaining = sum([portions[i] for i in movable]), rest
        for i in movable:
            extra = min(bound - given[i], max(1, remaining * portions[i] // pool), rest)
            given[i] = given[i] + extra
            rest = rest - extra
    return np.array([bound] + given)


def uneven_parts(own_key, number_of, total, reach, skew):
    if number_of == 2:
        one = jax.random.randint(own_key, (), max(1, total - reach), min(reach, total - 1) + 1)
        return jnp.stack([one, total - one])
    tallies = jnp.asarray(profile(number_of, total, reach, skew), jnp.int32)
    couples = (number_of - 1) // 2
    donor, receiver = tallies[1:1 + 2 * couples:2], tallies[2:2 + 2 * couples:2]
    margin = jnp.minimum(donor - 1, reach - receiver)
    passed = jax.random.randint(jax.random.fold_in(own_key, 1), (couples,), 0, 1 << 20) % (margin + 1)
    tallies = tallies.at[1:1 + 2 * couples:2].set(donor - passed).at[2:2 + 2 * couples:2].set(receiver + passed)
    return tallies[jax.random.permutation(jax.random.fold_in(own_key, 2), number_of)]


def bell_draw(rng, extent, width, reach, kind=jnp.bfloat16):
    return jnp.clip(width * jax.random.normal(rng, extent, jnp.float32), -reach, reach).astype(kind)


def setup_inputs(seed: int = 0) -> dict:
    arg_keys = jax.random.split(jax.random.key(seed), 8)
    bin_state = jnp.clip(jnp.exp(math.log(2.0) - 3.6888794 * jax.random.uniform(arg_keys[0], (COMPS, NX, NY * LEV), jnp.float32) ** block_levels(arg_keys[0], (COMPS, NX, NY * LEV), ((1, 8), (2, 4)), -0.2, 0.2)), 0.05, 2.0)
    courant_x = jnp.clip(jax.random.uniform(arg_keys[1], (NX, NY * LEV), jnp.float32, -0.4, 0.4) * block_levels(arg_keys[1], (NX, NY * LEV), ((0, 8), (1, 4)), -0.4, 0.0), -0.4, 0.4)
    courant_y = jnp.clip(jax.random.uniform(arg_keys[2], (NX, NY * LEV), jnp.float32, -0.4, 0.4) * block_levels(arg_keys[2], (NX, NY * LEV), ((0, 8), (1, 4)), -0.4, 0.0), -0.4, 0.4)
    cloudy_order = jax.vmap(lambda own: jax.random.permutation(own, CX))(jax.random.split(arg_keys[3], N_GX * N_GY)).reshape((N_GX, N_GY, CX)).astype(jnp.int32)
    block_count = jax.vmap(lambda own: uneven_parts(own, N_GX, N_GX * MEANB, MAXB, 2))(jax.random.split(arg_keys[4], N_GY)).reshape((N_GY, N_GX)).astype(jnp.int32)
    gain_kernel = bell_draw(arg_keys[5], (PAIRS, BINS, BINS * BINS), 0.01, 0.059814453)
    loss_rate = jnp.clip(jnp.exp(jax.random.uniform(arg_keys[6], (PAIRS, BINS, BINS), jnp.float32, math.log(9.965896606445312e-05), math.log(0.029907227))), 9.965896606445312e-05, 0.029907227).astype(jnp.bfloat16)
    return {"bin_state": bin_state, "courant_x": courant_x, "courant_y": courant_y, "cloudy_order": cloudy_order, "block_count": block_count, "gain_kernel": gain_kernel, "loss_rate": loss_rate}


pair_table = ((0, 0, 1), (0, 1, 1), (0, 2, 2), (0, 3, 3), (1, 1, 1), (1, 2, 3), (1, 3, 3), (2, 2, 3), (2, 3, 3), (3, 3, 3))


def upwind(centre, minus_one, minus_two, plus_one, plus_two, courant):
    rising = (2.0 * plus_one + 3.0 * centre - 6.0 * minus_one + minus_two) / 6.0
    falling = (6.0 * plus_one - plus_two - 3.0 * centre - 2.0 * minus_one) / 6.0
    return jnp.where(courant > 0.0, rising, falling)


def transport(component, courant_x, courant_y):
    along_x = upwind(component, jnp.roll(component, 1, 0), jnp.roll(component, 2, 0), jnp.roll(component, -1, 0), jnp.roll(component, -2, 0), courant_x)
    along_y = upwind(component, jnp.roll(component, LEV, 1), jnp.roll(component, 2 * LEV, 1), jnp.roll(component, -LEV, 1), jnp.roll(component, -2 * LEV, 1), courant_y)
    return jnp.maximum(component - courant_x * along_x - courant_y * along_y, 0.0)


def collide(bin_values, gain_kernel, loss_rate):
    column_count = bin_values.shape[1]
    tendency = [jnp.zeros((BINS, column_count), jnp.float32) for member in range(CLASSES)]
    for pair_index, (former, latter, target) in enumerate(pair_table):
        former_bins = bin_values[former * BINS:(former + 1) * BINS].astype(jnp.float32)
        latter_bins = bin_values[latter * BINS:(latter + 1) * BINS].astype(jnp.float32)
        product = (former_bins[:, None, :] * latter_bins[None, :, :]).reshape(BINS * BINS, column_count)
        product = product.astype(jnp.bfloat16).astype(jnp.float32)
        kernel = gain_kernel[pair_index].astype(jnp.float32)
        rates = loss_rate[pair_index].astype(jnp.float32)
        tendency[target] = tendency[target] + jnp.dot(kernel, product, precision=lax.Precision.HIGHEST, preferred_element_type=jnp.float32)
        tendency[former] = tendency[former] - former_bins * jnp.dot(rates, latter_bins, precision=lax.Precision.HIGHEST, preferred_element_type=jnp.float32)
        tendency[latter] = tendency[latter] - latter_bins * jnp.dot(rates.T, former_bins, precision=lax.Precision.HIGHEST, preferred_element_type=jnp.float32)
    return jnp.concatenate(tendency, axis=0)


def reference(bin_state, courant_x, courant_y, cloudy_order, block_count, gain_kernel, loss_rate):
    state_now = bin_state
    serial = jnp.arange(N_GX * MEANB, dtype=jnp.int32)
    for step_index in range(STEPS):
        state_now = lax.map(lambda component: transport(component, courant_x, courant_y), state_now)
        current = state_now

        def row_tendency(row_index):
            counts_row = block_count[row_index].astype(jnp.int32)
            count_ends = jnp.cumsum(counts_row).astype(jnp.int32)
            starts = (count_ends - counts_row).astype(jnp.int32)
            sender = jnp.sum((count_ends[None, :] <= serial[:, None]).astype(jnp.int32), axis=1).astype(jnp.int32)
            within = (serial - starts[sender]).astype(jnp.int32)
            local_block = cloudy_order[sender, row_index, within].astype(jnp.int32)
            global_row = (sender * CX + local_block).astype(jnp.int32)
            row_cells = lax.dynamic_slice_in_dim(current, (row_index * BLOCK).astype(jnp.int32), BLOCK, 2)
            chosen = jnp.take(row_cells, global_row, axis=1).astype(jnp.bfloat16)
            result = collide(chosen.reshape(COMPS, N_GX * MEANB * BLOCK), gain_kernel, loss_rate).astype(jnp.bfloat16)
            result = result.reshape(COMPS, N_GX * MEANB, BLOCK)
            return jnp.zeros((COMPS, NX, BLOCK), jnp.bfloat16).at[:, global_row].set(result)

        gathered = lax.map(row_tendency, jnp.arange(N_GY, dtype=jnp.int32))
        gathered = jnp.transpose(gathered, (1, 2, 0, 3)).reshape(COMPS, NX, N_GY * BLOCK)
        state_now = state_now + gathered.astype(jnp.float32)
    return state_now
```

```python
import functools
import jax
import jax.numpy as jnp
from jax import lax
from jax.experimental import pallas as pl
from jax.experimental.pallas import tpu as pltpu
from jax.sharding import PartitionSpec as P

BINS = 33
CLASSES = 4
LEV = 4
STEPS = 2
LANES = 128
OFF = (0, 40, 80, 128)
ROWS = 168
PAD = 40
HEAD = 32
LOOK = 14

GROUPS = (
    (1, 0, ((0, 0, False), (1, 1, False))),
    (1, 1, ((4, 1, False),)),
    (2, 0, ((2, 2, False),)),
    (3, 3, ((3, 0, True), (6, 1, True), (8, 2, True), (9, 3, False))),
    (3, 2, ((5, 1, True), (7, 2, False))),
)
PAIRS = ((0, 0), (0, 1), (0, 2), (0, 3), (1, 1), (1, 2), (1, 3), (2, 2), (2, 3), (3, 3))
NG = len(GROUPS)
F32 = jnp.float32
BF16 = jnp.bfloat16


def with_halo(shard, sides, width):
    for axis, dim in sides:
        size, length = (lax.axis_size(axis), shard.shape[dim])
        up = [(i, (i + 1) % size) for i in range(size)]
        down = [(j, i) for i, j in up]
        last = lax.slice_in_dim(shard, length - width, length, axis=dim)
        leading = lax.slice_in_dim(shard, 0, width, axis=dim)
        before = lax.ppermute(last, axis, up)
        after = lax.ppermute(leading, axis, down)
        shard = jnp.concatenate([before, shard, after], axis=dim)
    return shard


def upwind(centre, minus_one, minus_two, plus_one, plus_two, courant):
    rising = (2.0 * plus_one + 3.0 * centre - 6.0 * minus_one + minus_two) / 6.0
    falling = (6.0 * plus_one - plus_two - 3.0 * centre - 2.0 * minus_one) / 6.0
    return jnp.where(courant > 0.0, rising, falling)


def transport(fields, courant_x, courant_y):
    wide_x = with_halo(fields, (("gx", 1),), 2)
    along_x = upwind(
        fields, wide_x[:, 1:-3], wide_x[:, :-4], wide_x[:, 3:-1], wide_x[:, 4:], courant_x[None]
    )
    wide_y = with_halo(fields, (("gy", 2),), 2 * LEV)
    along_y = upwind(
        fields,
        wide_y[:, :, LEV : -3 * LEV],
        wide_y[:, :, : -4 * LEV],
        wide_y[:, :, 3 * LEV : -LEV],
        wide_y[:, :, 4 * LEV :],
        courant_y[None],
    )
    return jnp.maximum(fields - courant_x[None] * along_x - courant_y[None] * along_y, 0.0)


def prepare_kernel(gain, loss, blocks, tails, losses, wide, turned, upper, last_rows):
    lane = lax.broadcasted_iota(jnp.int32, (PAD, LANES), 1)
    tiles = wide.shape[2] // LANES
    turned[...] = jnp.zeros_like(turned)
    slot_of = {}
    for _, _, members in GROUPS:
        for pair, _, second in members:
            if second:
                slot_of[pair] = len(slot_of)
    for pair in range(len(PAIRS)):
        wide[pair] = jnp.zeros((PAD, tiles * LANES), F32)
        wide[pair, :BINS, : BINS * BINS] = gain[pair].astype(F32)
        if pair in slot_of:
            for tile in range(tiles):
                part = wide[pair, :, tile * LANES : (tile + 1) * LANES]
                part = jnp.concatenate([part, jnp.zeros((LANES - PAD, LANES), F32)], axis=0)
                turned[slot_of[pair], tile * LANES : (tile + 1) * LANES, :] = part.T
    last_rows[...] = jnp.zeros_like(last_rows)
    for group, (_, _, members) in enumerate(GROUPS):
        for factor in range(BINS):
            halves = [jnp.zeros((PAD, LANES), F32), jnp.zeros((PAD, LANES), F32)]
            second_members = [m for m in members if m[2]]
            if second_members:
                rows = []
                for other in range(CLASSES - 1):
                    found = [m for m in second_members if m[1] == other]
                    if found:
                        piece = turned[slot_of[found[0][0]], pl.ds(factor, PAD, stride=BINS), :]
                        rows.append(piece)
                    else:
                        rows.append(jnp.zeros((PAD, LANES), F32))
                rows.append(jnp.zeros((LANES - 3 * PAD, LANES), F32))
                halves[0] = jnp.concatenate(rows, axis=0).T[:PAD]
            for pair, other, second in members:
                if second:
                    continue
                start = BINS * factor
                tile, inside = divmod(start, LANES)
                half, at = divmod(OFF[other], LANES)
                shift = (at - inside) % LANES
                first = wide[pair, :, tile * LANES : (tile + 1) * LANES]
                first = pltpu.roll(first, shift, 1) if shift else first
                if inside + BINS > LANES:
                    rest = wide[pair, :, (tile + 1) * LANES : (tile + 2) * LANES]
                    rest = pltpu.roll(rest, shift, 1) if shift else rest
                    first = jnp.where(lane < at + LANES - inside, first, rest)
                halves[half] = jnp.where((lane >= at) & (lane < at + BINS), first, halves[half])
            full = jnp.concatenate(halves, axis=1)
            blocks[group, factor * HEAD : (factor + 1) * HEAD, :] = full[:HEAD].astype(BF16)
            last_rows[group * PAD + factor : group * PAD + factor + 1, :] = full[HEAD : HEAD + 1]
    tails[...] = last_rows[...].astype(BF16)
    upper[...] = jnp.zeros_like(upper)
    for pair, (first, second) in enumerate(PAIRS):
        half, at = divmod(OFF[second], LANES)
        rates = jnp.concatenate(
            [loss[pair].astype(F32), jnp.zeros((BINS, LANES - BINS), F32)], axis=1
        )
        rates = pltpu.roll(rates, at, 1) if at else rates
        rows = slice(OFF[first], OFF[first] + BINS)
        span = slice(half * LANES, (half + 1) * LANES)
        upper[rows, span] = upper[rows, span] + rates
    whole = upper[...]
    losses[...] = (whole + whole.T)[: losses.shape[0]].astype(BF16)


def prepare(gain_kernel, loss_rate):
    wide = -(-BINS * BINS // LANES) * LANES
    tail = -(-NG * PAD // 16) * 16
    rows = -(-ROWS // 16) * 16
    return pl.pallas_call(
        prepare_kernel,
        out_shape=(
            jax.ShapeDtypeStruct((NG, BINS * HEAD, 2 * LANES), BF16),
            jax.ShapeDtypeStruct((tail, 2 * LANES), BF16),
            jax.ShapeDtypeStruct((rows, 2 * LANES), BF16),
        ),
        scratch_shapes=[
            pltpu.VMEM((len(PAIRS), PAD, wide), F32),
            pltpu.VMEM((4, BINS * PAD + BINS, LANES), F32),
            pltpu.VMEM((2 * LANES, 2 * LANES), F32),
            pltpu.VMEM((tail, 2 * LANES), F32),
        ],
    )(gain_kernel, loss_rate)


def collide_tiles(bins, row0, blocks, tails, losses, slots, ends, sinks, emit):
    for unit in range(2):
        right = jnp.concatenate([bins[row0 + 2 * unit], bins[row0 + 2 * unit + 1]], axis=1)
        right = jnp.concatenate(
            [right, jnp.zeros((2 * LANES - ROWS, 2 * LANES), F32)], axis=0
        ).astype(BF16)
        pltpu.matmul_push_rhs(right, 0, unit)
    for unit in range(2):
        pltpu.matmul_acc_lhs(ends[unit], tails[...], 0)
    for unit in range(2):
        pltpu.matmul_acc_lhs(sinks[unit], losses[...])
    depth = len(slots[0])
    pending, count = [], 0
    parts = {t: [[jnp.zeros((HEAD, LANES), F32) for _ in range(2)] for _ in range(2)] for t in (1, 2, 3)}

    def drain():
        target, source, factor, slot = pending.pop(0)
        for unit in range(2):
            block = pltpu.matmul_pop(slots[unit][slot])
            for half in range(2):
                scale = bins[row0 + 2 * unit + half, pl.ds(OFF[source] + factor, 1), :]
                part = block[:, half * LANES : (half + 1) * LANES]
                parts[target][unit][half] = parts[target][unit][half] + part * scale

    last = [[[jnp.zeros((PAD, LANES), F32) for _ in range(2)] for _ in range(2)] for _ in range(4)]
    for unit in range(2):
        block = pltpu.matmul_pop(ends[unit])
        for group, (target, source, _) in enumerate(GROUPS):
            for half in range(2):
                scale = bins[row0 + 2 * unit + half, OFF[source] : OFF[source] + PAD, :]
                piece = block[group * PAD : (group + 1) * PAD, half * LANES : (half + 1) * LANES]
                last[target][unit][half] = last[target][unit][half] + piece * scale
    drop = [pltpu.matmul_pop(sinks[unit]) for unit in range(2)]
    for unit in range(2):
        for half in range(2):
            row = row0 + 2 * unit + half
            for member in range(CLASSES):
                rows = slice(OFF[member], OFF[member] + PAD)
                lost = drop[unit][rows, half * LANES : (half + 1) * LANES] * bins[row, rows, :]
                if member:
                    bottom = jnp.sum(last[member][unit][half], axis=0, keepdims=True)
                    bottom = jnp.concatenate([bottom, jnp.zeros((PAD - HEAD - 1, LANES), F32)], axis=0)
                    base = jnp.concatenate([-lost[:HEAD], bottom - lost[HEAD:]], axis=0)
                else:
                    base = -lost
                emit(row, member, None, base)
    for target in (1, 2, 3):
        order = [
            (group, source, factor)
            for factor in range(BINS)
            for group, (aim, source, _) in enumerate(GROUPS)
            if aim == target
        ]
        for group, source, factor in order:
            slot = count % depth
            count += 1
            left = blocks[group, factor * HEAD : (factor + 1) * HEAD, :]
            for unit in range(2):
                pltpu.matmul_acc_lhs(slots[unit][slot], left)
            pending.append((target, source, factor, slot))
            if len(pending) > LOOK:
                drain()
        while pending:
            drain()
        for unit in range(2):
            for half in range(2):
                emit(row0 + 2 * unit + half, target, parts[target][unit][half], None)


def collide_kernel(flags, field, blocks, tails, losses, out, bins, change):
    rows_x = field.shape[1]
    flat = field.reshape(field.shape[0] * rows_x, LANES)
    flat_out = out.reshape(field.shape[0] * rows_x, LANES)
    bins[...] = jnp.zeros_like(bins)
    for row in range(rows_x):
        for member in range(CLASSES):
            part = flat[pl.ds(member * BINS * rows_x + row, BINS, stride=rows_x), :]
            bins[row, OFF[member] : OFF[member] + BINS, :] = part.astype(BF16).astype(F32)
    tail, rows = tails.shape[0], losses.shape[0]
    depth = LOOK + 2

    def inside(*refs):
        slots = (refs[:depth], refs[depth : 2 * depth])
        ends = refs[2 * depth : 2 * depth + 2]
        sinks = refs[2 * depth + 2 :]

        @pl.loop(0, rows_x // 4)
        def _(step):
            def emit(row, member, gained, base):
                top = slice(OFF[member], OFF[member] + HEAD)
                if base is not None:
                    change[row, OFF[member] : OFF[member] + PAD, :] = base
                else:
                    change[row, top, :] = change[row, top, :] + gained

            collide_tiles(bins, 4 * step, blocks, tails, losses, slots, ends, sinks, emit)

    pl.run_scoped(
        inside,
        *[pltpu.ACC(unit)((HEAD, 2 * LANES), F32) for unit in range(2) for _ in range(depth)],
        *[pltpu.ACC(unit)((tail, 2 * LANES), F32) for unit in range(2)],
        *[pltpu.ACC(unit)((rows, 2 * LANES), F32) for unit in range(2)],
    )
    for row in range(rows_x):
        cloudy = flags[row] > 0
        for member in range(CLASSES):
            span = pl.ds(member * BINS * rows_x + row, BINS, stride=rows_x)
            part = change[row, OFF[member] : OFF[member] + BINS, :].astype(BF16).astype(F32)
            flat_out[span, :] = flat[span, :] + jnp.where(cloudy, part, 0.0)


def collide(field, flags, prepared):
    vmem = pl.BlockSpec(memory_space=pltpu.VMEM)
    rows_x = field.shape[1]
    return pl.pallas_call(
        collide_kernel,
        out_shape=jax.ShapeDtypeStruct(field.shape, F32),
        in_specs=[pl.BlockSpec(memory_space=pltpu.SMEM), vmem, vmem, vmem, vmem],
        out_specs=vmem,
        scratch_shapes=[
            pltpu.VMEM((rows_x, ROWS, LANES), F32),
            pltpu.VMEM((rows_x, ROWS, LANES), F32),
        ],
    )(flags, field, *prepared)


def per_device(bin_state, courant_x, courant_y, cloudy_order, block_count, gain_kernel, loss_rate):
    state_now = bin_state
    block_rows = state_now.shape[1]
    block_order = cloudy_order[0, 0]
    own_count = block_count[0, 0]
    row_numbers = jnp.arange(block_rows, dtype=jnp.int32)
    matches = (block_order[:, None] == row_numbers[None, :]).astype(jnp.int32)
    position = jnp.sum(matches * row_numbers[:, None], axis=0)
    cloudy = (position < own_count).astype(jnp.int32)
    prepared = prepare(gain_kernel, loss_rate)
    for step_index in range(STEPS):
        state_now = transport(state_now, courant_x, courant_y)
        state_now = collide(state_now, cloudy, prepared)
    return state_now


def solution(mesh):
    placed = (
        P(None, "gx", "gy"),
        P("gx", "gy"),
        P("gx", "gy"),
        P("gx", "gy", None),
        P("gy", "gx"),
        P(),
        P(),
    )
    sharded = jax.shard_map(
        per_device, mesh=mesh, in_specs=placed, out_specs=P(None, "gx", "gy"), check_vma=False
    )

    def run(*arguments):
        with jax.sharding.use_abstract_mesh(mesh.abstract_mesh):
            return sharded(*arguments)

    return run
```

```python
import functools
import jax
import jax.numpy as jnp
from jax import lax
from jax.experimental import pallas as pl
from jax.experimental.pallas import tpu as pltpu
from jax.sharding import PartitionSpec as P

BINS = 33
CLASSES = 4
LEV = 4
STEPS = 2
LANES = 128
OFF = (0, 40, 80, 128)
ROWS = 168
PAD = 40
HEAD = 32
LOOK = 14
HALO = 2 * STEPS
GROUP = HALO * LEV
AUX = BINS
FLAG = AUX + 4
CHUNKS = tuple((OFF[member], OFF[member] + PAD) for member in range(CLASSES))
VMEM_LIMIT = 24 << 20

GROUPS = (
    (1, 0, ((0, 0, False), (1, 1, False))),
    (1, 1, ((4, 1, False),)),
    (2, 0, ((2, 2, False),)),
    (3, 3, ((3, 0, True), (6, 1, True), (8, 2, True), (9, 3, False))),
    (3, 2, ((5, 1, True), (7, 2, False))),
)
PAIRS = ((0, 0), (0, 1), (0, 2), (0, 3), (1, 1), (1, 2), (1, 3), (2, 2), (2, 3), (3, 3))
NG = len(GROUPS)
F32 = jnp.float32
BF16 = jnp.bfloat16


def prepare_kernel(gain, loss, blocks, tails, losses, wide, turned, upper, last_rows):
    lane = lax.broadcasted_iota(jnp.int32, (PAD, LANES), 1)
    tiles = wide.shape[2] // LANES
    turned[...] = jnp.zeros_like(turned)
    slot_of = {}
    for _, _, members in GROUPS:
        for pair, _, second in members:
            if second:
                slot_of[pair] = len(slot_of)
    for pair in range(len(PAIRS)):
        wide[pair] = jnp.zeros((PAD, tiles * LANES), F32)
        wide[pair, :BINS, : BINS * BINS] = gain[pair].astype(F32)
        if pair in slot_of:
            for tile in range(tiles):
                part = wide[pair, :, tile * LANES : (tile + 1) * LANES]
                part = jnp.concatenate([part, jnp.zeros((LANES - PAD, LANES), F32)], axis=0)
                turned[slot_of[pair], tile * LANES : (tile + 1) * LANES, :] = part.T
    last_rows[...] = jnp.zeros_like(last_rows)
    for group, (_, _, members) in enumerate(GROUPS):
        for factor in range(BINS):
            halves = [jnp.zeros((PAD, LANES), F32), jnp.zeros((PAD, LANES), F32)]
            second_members = [m for m in members if m[2]]
            if second_members:
                rows = []
                for other in range(CLASSES - 1):
                    found = [m for m in second_members if m[1] == other]
                    if found:
                        piece = turned[slot_of[found[0][0]], pl.ds(factor, PAD, stride=BINS), :]
                        rows.append(piece)
                    else:
                        rows.append(jnp.zeros((PAD, LANES), F32))
                rows.append(jnp.zeros((LANES - 3 * PAD, LANES), F32))
                halves[0] = jnp.concatenate(rows, axis=0).T[:PAD]
            for pair, other, second in members:
                if second:
                    continue
                start = BINS * factor
                tile, inside = divmod(start, LANES)
                half, at = divmod(OFF[other], LANES)
                shift = (at - inside) % LANES
                first = wide[pair, :, tile * LANES : (tile + 1) * LANES]
                first = pltpu.roll(first, shift, 1) if shift else first
                if inside + BINS > LANES:
                    rest = wide[pair, :, (tile + 1) * LANES : (tile + 2) * LANES]
                    rest = pltpu.roll(rest, shift, 1) if shift else rest
                    first = jnp.where(lane < at + LANES - inside, first, rest)
                halves[half] = jnp.where((lane >= at) & (lane < at + BINS), first, halves[half])
            full = jnp.concatenate(halves, axis=1)
            blocks[group, factor * HEAD : (factor + 1) * HEAD, :] = full[:HEAD].astype(BF16)
            last_rows[group * PAD + factor : group * PAD + factor + 1, :] = full[HEAD : HEAD + 1]
    tails[...] = last_rows[...].astype(BF16)
    upper[...] = jnp.zeros_like(upper)
    for pair, (first, second) in enumerate(PAIRS):
        half, at = divmod(OFF[second], LANES)
        rates = jnp.concatenate(
            [loss[pair].astype(F32), jnp.zeros((BINS, LANES - BINS), F32)], axis=1
        )
        rates = pltpu.roll(rates, at, 1) if at else rates
        rows = slice(OFF[first], OFF[first] + BINS)
        span = slice(half * LANES, (half + 1) * LANES)
        upper[rows, span] = upper[rows, span] + rates
    whole = upper[...]
    losses[...] = (whole + whole.T)[: losses.shape[0]].astype(BF16)


def prepare(gain_kernel, loss_rate):
    wide = -(-BINS * BINS // LANES) * LANES
    tail = -(-NG * PAD // 16) * 16
    rows = -(-ROWS // 16) * 16
    return pl.pallas_call(
        prepare_kernel,
        out_shape=(
            jax.ShapeDtypeStruct((NG, BINS * HEAD, 2 * LANES), BF16),
            jax.ShapeDtypeStruct((tail, 2 * LANES), BF16),
            jax.ShapeDtypeStruct((rows, 2 * LANES), BF16),
        ),
        scratch_shapes=[
            pltpu.VMEM((len(PAIRS), PAD, wide), F32),
            pltpu.VMEM((4, BINS * PAD + BINS, LANES), F32),
            pltpu.VMEM((2 * LANES, 2 * LANES), F32),
            pltpu.VMEM((tail, 2 * LANES), F32),
        ],
        compiler_params=pltpu.CompilerParams(vmem_limit_bytes=VMEM_LIMIT),
        cost_estimate=pl.CostEstimate(flops=2 * 10**9, bytes_accessed=4 << 20, transcendentals=0),
    )(gain_kernel, loss_rate)


def collide_tiles(bins, row0, blocks, tails, losses, slots, ends, sinks, emit):
    for unit in range(2):
        right = jnp.concatenate([bins[row0 + 2 * unit], bins[row0 + 2 * unit + 1]], axis=1)
        right = jnp.concatenate(
            [right, jnp.zeros((2 * LANES - ROWS, 2 * LANES), F32)], axis=0
        ).astype(BF16)
        pltpu.matmul_push_rhs(right, 0, unit)
    for unit in range(2):
        pltpu.matmul_acc_lhs(ends[unit], tails[...], 0)
    for unit in range(2):
        pltpu.matmul_acc_lhs(sinks[unit], losses[...])
    depth = len(slots[0])
    pending, count = [], 0
    parts = {t: [[jnp.zeros((HEAD, LANES), F32) for _ in range(2)] for _ in range(2)] for t in (1, 2, 3)}

    def drain():
        target, source, factor, slot = pending.pop(0)
        for unit in range(2):
            block = pltpu.matmul_pop(slots[unit][slot])
            for half in range(2):
                scale = bins[row0 + 2 * unit + half, pl.ds(OFF[source] + factor, 1), :]
                part = block[:, half * LANES : (half + 1) * LANES]
                parts[target][unit][half] = parts[target][unit][half] + part * scale

    last = [[[jnp.zeros((PAD, LANES), F32) for _ in range(2)] for _ in range(2)] for _ in range(4)]
    for unit in range(2):
        block = pltpu.matmul_pop(ends[unit])
        for group, (target, source, _) in enumerate(GROUPS):
            for half in range(2):
                scale = bins[row0 + 2 * unit + half, OFF[source] : OFF[source] + PAD, :]
                piece = block[group * PAD : (group + 1) * PAD, half * LANES : (half + 1) * LANES]
                last[target][unit][half] = last[target][unit][half] + piece * scale
    drop = [pltpu.matmul_pop(sinks[unit]) for unit in range(2)]
    for unit in range(2):
        for half in range(2):
            row = row0 + 2 * unit + half
            for member in range(CLASSES):
                rows = slice(OFF[member], OFF[member] + PAD)
                lost = drop[unit][rows, half * LANES : (half + 1) * LANES] * bins[row, rows, :]
                if member:
                    bottom = jnp.sum(last[member][unit][half], axis=0, keepdims=True)
                    bottom = jnp.concatenate([bottom, jnp.zeros((PAD - HEAD - 1, LANES), F32)], axis=0)
                    base = jnp.concatenate([-lost[:HEAD], bottom - lost[HEAD:]], axis=0)
                else:
                    base = -lost
                emit(2 * unit + half, member, None, base)
    for target in (1, 2, 3):
        order = [
            (group, source, factor)
            for factor in range(BINS)
            for group, (aim, source, _) in enumerate(GROUPS)
            if aim == target
        ]
        for group, source, factor in order:
            slot = count % depth
            count += 1
            left = blocks[group, factor * HEAD : (factor + 1) * HEAD, :]
            for unit in range(2):
                pltpu.matmul_acc_lhs(slots[unit][slot], left)
            pending.append((target, source, factor, slot))
            if len(pending) > LOOK:
                drain()
        while pending:
            drain()
        for unit in range(2):
            for half in range(2):
                emit(2 * unit + half, target, parts[target][unit][half], None)


def accumulators(depth, tail, rows):
    return (
        [pltpu.ACC(unit)((HEAD, 2 * LANES), F32) for unit in range(2) for _ in range(depth)]
        + [pltpu.ACC(unit)((tail, 2 * LANES), F32) for unit in range(2)]
        + [pltpu.ACC(unit)((rows, 2 * LANES), F32) for unit in range(2)]
    )


def settle(field, mask, change, row, place):
    def emit(index, member, gained, base):
        at = row(index)
        start = OFF[member]
        if base is not None and member:
            change[place(index), start : start + PAD, :] = base
            return
        if member:
            base = change[place(index), start : start + PAD, :]
            base = jnp.concatenate([base[:HEAD] + gained, base[HEAD:]], axis=0)
        part = jnp.where(mask[at, :1, :] > 0.5, base.astype(BF16).astype(F32), 0.0)
        span = slice(start, start + PAD)
        field[at, span, :] = field[at, span, :] + part

    return emit


def four_rows(bins, row0, matrices, refs, field, mask, change):
    depth = LOOK + 2
    slots = (refs[:depth], refs[depth : 2 * depth])
    ends, sinks = refs[2 * depth : 2 * depth + 2], refs[2 * depth + 2 :]
    emit = settle(field, mask, change, lambda index: row0 + index, lambda index: index)
    collide_tiles(bins, row0, *matrices, slots, ends, sinks, emit)


def one_row(bins, row, matrices, refs, field, mask, change):
    blocks, tails, losses = matrices
    depth = LOOK + 2
    slots = (refs[:depth], refs[depth : 2 * depth])
    end, sink = refs[2 * depth], refs[2 * depth + 3]
    right = bins[row]
    right = jnp.concatenate([right, jnp.zeros((2 * LANES - ROWS, LANES), F32)], axis=0)
    right = jnp.concatenate([right, jnp.zeros((2 * LANES, LANES), F32)], axis=1).astype(BF16)
    for unit in range(2):
        pltpu.matmul_push_rhs(right, 0, unit)
    pltpu.matmul_acc_lhs(end, tails[...], 0)
    pltpu.matmul_acc_lhs(sink, losses[...], 0)
    emit = settle(field, mask, change, lambda index: row, lambda index: 0)
    block = pltpu.matmul_pop(end)[:, :LANES]
    last = [jnp.zeros((PAD, LANES), F32) for _ in range(CLASSES)]
    for group, (target, source, _) in enumerate(GROUPS):
        scale = bins[row, OFF[source] : OFF[source] + PAD, :]
        last[target] = last[target] + block[group * PAD : (group + 1) * PAD] * scale
    drop = pltpu.matmul_pop(sink)[:, :LANES]
    for member in range(CLASSES):
        span = slice(OFF[member], OFF[member] + PAD)
        base = -drop[span] * bins[row, span, :]
        if member:
            bottom = jnp.sum(last[member], axis=0, keepdims=True)
            bottom = jnp.concatenate([bottom, jnp.zeros((PAD - HEAD - 1, LANES), F32)], axis=0)
            base = jnp.concatenate([base[:HEAD], bottom + base[HEAD:]], axis=0)
        emit(0, member, None, base)
    parts = {t: [jnp.zeros((HEAD, LANES), F32) for _ in range(2)] for t in (1, 2, 3)}
    pending, count = [], 0

    def drain():
        target, source, factor, unit, slot = pending.pop(0)
        part = pltpu.matmul_pop(slots[unit][slot])[:, :LANES]
        scale = bins[row, OFF[source] + factor : OFF[source] + factor + 1, :]
        parts[target][unit] = parts[target][unit] + part * scale

    for target in (1, 2, 3):
        order = [
            (group, source, factor)
            for factor in range(BINS)
            for group, (aim, source, _) in enumerate(GROUPS)
            if aim == target
        ]
        for group, source, factor in order:
            unit, slot = count % 2, (count // 2) % len(slots[0])
            count += 1
            left = blocks[group, factor * HEAD : (factor + 1) * HEAD, :]
            pltpu.matmul_acc_lhs(slots[unit][slot], left)
            pending.append((target, source, factor, unit, slot))
            if len(pending) > 2 * LOOK:
                drain()
        while pending:
            drain()
        emit(0, target, parts[target][0] + parts[target][1], None)


def weights(tile, row):
    out, centre = [], 1.0
    for axis in range(2):
        pair = tile[row, AUX + 2 * axis : AUX + 2 * axis + 2, :]
        speed = (pair[:1] + pair[1:]) * (1.0 / 6.0)
        rising, falling = jnp.maximum(speed, 0.0), jnp.minimum(speed, 0.0)
        centre = centre - 3.0 * (rising - falling)
        out.append(
            (
                6.0 * rising + 2.0 * falling,
                -rising,
                -2.0 * rising - 6.0 * falling,
                falling,
            )
        )
    return centre, out


def advance(centre, along_x, along_y, coefficients):
    middle, (for_x, for_y) = coefficients
    total = middle * centre
    for values, factors in ((along_x, for_x), (along_y, for_y)):
        for value, factor in zip(values, factors):
            total = total + factor * value
    return jnp.maximum(total, 0.0)


def shifted(value, amount):
    amount = amount % LANES
    return pltpu.roll(value, amount, 1) if amount else value


def beside(centre, edge, lane):
    return (
        shifted(jnp.where(lane >= LANES - LEV, edge, centre), LEV),
        shifted(jnp.where(lane >= LANES - 2 * LEV, edge, centre), 2 * LEV),
        shifted(jnp.where(lane < LEV, edge, centre), -LEV),
        shifted(jnp.where(lane < 2 * LEV, edge, centre), -2 * LEV),
    )


def lanes():
    return lax.broadcasted_iota(jnp.int32, (PAD, LANES), 1)


def put(field, bins, row, span, value):
    field[row, span, :] = value
    bins[row, span, :] = value.astype(BF16).astype(F32)


def clear_gap(*arrays):
    gap = slice(OFF[2] + PAD, OFF[3])
    for array in arrays:
        for row in range(array.shape[0]):
            array[row, gap, :] = jnp.zeros((OFF[3] - OFF[2] - PAD, LANES), F32)


def stage_kernel(order, count, state, courant_x, courant_y, rows, edges, low, high):
    rows_x = state.shape[1]
    flat = state.reshape(state.shape[0] * rows_x, LANES)
    spare = jnp.zeros((PAD - BINS, LANES), F32)
    for row in range(rows_x):
        cloudy = jnp.int32(0)
        for place in range(rows_x):
            hit = (order[0, 0, place] == row) & (place < count[0, 0])
            cloudy = cloudy | hit.astype(jnp.int32)
        for member in range(CLASSES):
            part = flat[pl.ds(member * BINS * rows_x + row, BINS, stride=rows_x), :]
            rows[row, OFF[member] : OFF[member] + BINS, :] = part
            rows[row, OFF[member] + BINS : OFF[member] + PAD, :] = spare
        for axis, courant in enumerate((courant_x, courant_y)):
            speed = courant[row : row + 1, :]
            upper = speed.astype(BF16).astype(F32)
            rows[row, AUX + 2 * axis : AUX + 2 * axis + 1, :] = upper
            rows[row, AUX + 2 * axis + 1 : AUX + 2 * axis + 2, :] = speed - upper
        rows[row, FLAG : FLAG + 1, :] = jnp.full((1, LANES), cloudy.astype(F32), F32)
    clear_gap(rows, edges)
    owner = lanes() // GROUP
    for start, stop in CHUNKS:
        left = jnp.zeros((PAD, LANES), F32)
        right = left
        for row in range(rows_x):
            value = rows[row, start:stop, :]
            left = jnp.where(owner == row, shifted(value, GROUP * row), left)
            right = jnp.where(owner == row, shifted(value, GROUP * (row + 1)), right)
        edges[0, start:stop, :] = left
        edges[1, start:stop, :] = right
    low[...] = edges[0].astype(BF16)
    high[...] = edges[1].astype(BF16)


def widen_kernel(rows, before, after, around, to_right, to_left):
    rows_x = rows.shape[0]
    inner = lax.broadcasted_iota(jnp.int32, (ROWS, LANES), 1) % GROUP < GROUP // 2
    near = jnp.where(
        inner,
        shifted(before[...].astype(F32), -GROUP // 2),
        shifted(after[...].astype(F32), GROUP // 2),
    )
    around[0] = near
    for index in range(HALO):
        to_right[index] = rows[rows_x - HALO + index].astype(BF16)
        to_left[index] = rows[index].astype(BF16)
    to_right[HALO] = near.astype(BF16)
    to_left[HALO] = near.astype(BF16)


def inner_kernel(rows, around, blocks, tails, losses, out, bins, change, mask):
    rows_x = rows.shape[0]
    lane = lanes()
    clear_gap(out, bins)
    for index in range(rows_x - HALO):
        row = index + HALO // 2
        coefficients = weights(rows, row)
        mask[index] = jnp.broadcast_to(rows[row, FLAG : FLAG + 1, :], mask.shape[1:])
        for start, stop in CHUNKS:
            span = slice(start, stop)
            centre = rows[row, span, :]
            along_x = [rows[row + d, span, :] for d in (-1, -2, 1, 2)]
            edge = shifted(around[0, span, :], -GROUP * row - GROUP // 2)
            value = advance(centre, along_x, beside(centre, edge, lane), coefficients)
            put(out, bins, index, span, value)
    matrices = (blocks, tails, losses)
    pl.run_scoped(
        lambda *refs: four_rows(bins, 0, matrices, refs, out, mask, change),
        *accumulators(LOOK + 2, tails.shape[0], losses.shape[0]),
    )


def outer_kernel(
    rows, edges, before, after, around, from_left, from_right, middle, blocks, tails, losses,
    out, left, right, field, bins, change, mask, second,
):
    rows_x = rows.shape[0]
    lane = lanes()
    outside = rows_x + HALO
    for index in range(HALO + 1):
        left[index] = from_left[index].astype(F32)
        right[index] = from_right[index].astype(F32)
    clear_gap(field, bins, second)

    def column(x):
        if x < 0:
            return left, x + HALO
        if x >= rows_x:
            return right, x - rows_x
        return rows, x

    def edge_of(x, span):
        if x < 0:
            return shifted(left[HALO, span, :], -GROUP * (x + rows_x) - GROUP // 2)
        if x >= rows_x:
            return shifted(right[HALO, span, :], -GROUP * (x - rows_x) - GROUP // 2)
        return shifted(around[0, span, :], -GROUP * x - GROUP // 2)

    reach = HALO // 2
    for x in list(range(-reach, reach)) + list(range(rows_x - reach, rows_x + reach)):
        tile, row = column(x)
        coefficients = weights(tile, row)
        mask[x + reach] = jnp.broadcast_to(tile[row, FLAG : FLAG + 1, :], mask.shape[1:])
        for start, stop in CHUNKS:
            span = slice(start, stop)
            centre = tile[row, span, :]
            along_x = []
            for d in (-1, -2, 1, 2):
                other, at = column(x + d)
                along_x.append(other[at, span, :])
            value = advance(
                centre, along_x, beside(centre, edge_of(x, span), lane), coefficients
            )
            put(field, bins, x + reach, span, value)
    coefficients = weights(around, 0)
    mask[outside] = jnp.broadcast_to(around[0, FLAG : FLAG + 1, :], mask.shape[1:])
    inside = lane % GROUP
    half = GROUP // 2
    for start, stop in CHUNKS:
        span = slice(start, stop)
        lower, upper = before[span, :].astype(F32), after[span, :].astype(F32)
        first, last = edges[0, span, :], edges[1, span, :]
        centre = around[0, span, :]
        along_y = (
            jnp.where(
                inside < half + LEV,
                shifted(jnp.where(inside < half + LEV, lower, last), -LEV),
                shifted(upper, half + LEV),
            ),
            jnp.where(inside < half, lower, last),
            jnp.where(
                inside < LEV,
                shifted(lower, -half - LEV),
                shifted(jnp.where(inside < LEV, first, upper), LEV),
            ),
            jnp.where(inside < half, first, upper),
        )
        beyond = jnp.where(lane >= LANES // 2, left[HALO, span, :], right[HALO, span, :])
        along_x = (
            shifted(jnp.where(lane >= LANES - GROUP, beyond, centre), GROUP),
            shifted(jnp.where(lane >= LANES - 2 * GROUP, beyond, centre), 2 * GROUP),
            shifted(jnp.where(lane < GROUP, beyond, centre), -GROUP),
            shifted(jnp.where(lane < 2 * GROUP, beyond, centre), -2 * GROUP),
        )
        put(field, bins, outside, span, advance(centre, along_x, along_y, coefficients))
    for index in range(rows_x - HALO):
        field[index + HALO] = middle[index]
        row = index + reach
        mask[index + HALO] = jnp.broadcast_to(rows[row, FLAG : FLAG + 1, :], mask.shape[1:])
    matrices = (blocks, tails, losses)

    def collisions(*refs):
        one_row(bins, outside, matrices, refs, field, mask, change)

        @pl.loop(0, 2)
        def _(step):
            four_rows(bins, rows_x * step, matrices, refs, field, mask, change)

        for x in range(rows_x):
            coefficients = weights(rows, x)
            for start, stop in CHUNKS:
                span = slice(start, stop)
                centre = field[x + reach, span, :]
                along_x = [field[x + reach + d, span, :] for d in (-1, -2, 1, 2)]
                edge = shifted(field[outside, span, :], -GROUP * x - GROUP // 2)
                value = advance(centre, along_x, beside(centre, edge, lane), coefficients)
                put(second, bins, x + reach, span, value)

        @pl.loop(0, rows_x // 4)
        def _(step):
            four_rows(bins, reach + 4 * step, matrices, refs, second, mask, change)

    pl.run_scoped(collisions, *accumulators(LOOK + 2, tails.shape[0], losses.shape[0]))
    flat = out.reshape(out.shape[0] * rows_x, LANES)
    for x in range(rows_x):
        for member in range(CLASSES):
            span = pl.ds(member * BINS * rows_x + x, BINS, stride=rows_x)
            flat[span, :] = second[x + reach, OFF[member] : OFF[member] + BINS, :]


def call(kernel, outs, scratch, *arguments, scalars=0, flops=0):
    vmem = pl.BlockSpec(memory_space=pltpu.VMEM)
    smem = pl.BlockSpec(memory_space=pltpu.SMEM)
    shapes = tuple(jax.ShapeDtypeStruct(shape, dtype) for shape, dtype in outs)
    moved = sum(a.size * a.dtype.itemsize for a in arguments)
    return pl.pallas_call(
        kernel,
        out_shape=shapes,
        in_specs=[smem] * scalars + [vmem] * (len(arguments) - scalars),
        out_specs=tuple(vmem for _ in shapes),
        scratch_shapes=[pltpu.VMEM(shape, F32) for shape in scratch],
        compiler_params=pltpu.CompilerParams(vmem_limit_bytes=VMEM_LIMIT),
        cost_estimate=pl.CostEstimate(flops=flops, bytes_accessed=moved, transcendentals=0),
    )(*arguments)


def exchange(axis, upward, downward):
    size = lax.axis_size(axis)
    up = [(i, (i + 1) % size) for i in range(size)]
    down = [(j, i) for i, j in up]
    return lax.ppermute(upward, axis, up), lax.ppermute(downward, axis, down)


def per_device(bin_state, courant_x, courant_y, cloudy_order, block_count, gain_kernel, loss_rate):
    rows_x = bin_state.shape[1]
    tile = (ROWS, LANES)
    rows, edges, low, high = call(
        stage_kernel,
        [((rows_x, *tile), F32), ((2, *tile), F32), (tile, BF16), (tile, BF16)],
        [],
        cloudy_order, block_count, bin_state, courant_x, courant_y,
        scalars=2,
    )
    before, after = exchange("gy", high, low)
    matrices = prepare(gain_kernel, loss_rate)
    around, to_right, to_left = call(
        widen_kernel,
        [((1, *tile), F32), ((HALO + 1, *tile), BF16), ((HALO + 1, *tile), BF16)],
        [],
        rows, before, after,
    )
    from_left, from_right = exchange("gx", to_right, to_left)
    inner = rows_x - HALO
    (middle,) = call(
        inner_kernel,
        [((inner, *tile), F32)],
        [(inner, *tile), (4, *tile), (inner, 8, LANES)],
        rows, around, *matrices,
        flops=5 * 10**9,
    )
    total = rows_x + HALO + 1
    (out,) = call(
        outer_kernel,
        [(bin_state.shape, F32)],
        [
            (HALO + 1, *tile),
            (HALO + 1, *tile),
            (total, *tile),
            (total, *tile),
            (4, *tile),
            (total, 8, LANES),
            (total, *tile),
        ],
        rows, edges, before, after, around, from_left, from_right, middle, *matrices,
        flops=20 * 10**9,
    )
    return out


def solution(mesh):
    placed = (
        P(None, "gx", "gy"),
        P("gx", "gy"),
        P("gx", "gy"),
        P("gx", "gy", None),
        P("gy", "gx"),
        P(),
        P(),
    )
    sharded = jax.shard_map(
        per_device, mesh=mesh, in_specs=placed, out_specs=P(None, "gx", "gy"), check_vma=False
    )

    def run(*arguments):
        with jax.sharding.use_abstract_mesh(mesh.abstract_mesh):
            return sharded(*arguments)

    return run
```

```python
import functools
import jax
import jax.numpy as jnp
from jax import lax
from jax.experimental import pallas as pl
from jax.experimental.pallas import tpu as pltpu
from jax.sharding import PartitionSpec as P

BINS = 33
CLASSES = 4
LEV = 4
STEPS = 2
LANES = 128
SUBLANES = 8
OFF = (0, 40, 80, 128)
ROWS = 176
PAD = 40
HEAD = 32
LOOK = 14
HALO = 2 * STEPS
GROUP = HALO * LEV
AUX = BINS
FLAG = AUX + 4
EDGE = 2 * LANES - GROUP
CHUNKS = tuple((OFF[member], OFF[member] + PAD) for member in range(CLASSES))
VMEM_LIMIT = 24 << 20

GROUPS = (
    (1, 0, ((0, 0, False), (1, 1, False))),
    (1, 1, ((4, 1, False),)),
    (2, 0, ((2, 2, False),)),
    (3, 3, ((3, 0, True), (6, 1, True), (8, 2, True), (9, 3, False))),
    (3, 2, ((5, 1, True), (7, 2, False))),
)
PAIRS = ((0, 0), (0, 1), (0, 2), (0, 3), (1, 1), (1, 2), (1, 3), (2, 2), (2, 3), (3, 3))
NG = len(GROUPS)
F32 = jnp.float32
BF16 = jnp.bfloat16


def prepare_kernel(gain, loss, blocks, tails, losses, moves, wide, turned, upper, last_rows):
    lane = lax.broadcasted_iota(jnp.int32, (PAD, LANES), 1)
    tiles = wide.shape[2] // LANES
    turned[...] = jnp.zeros_like(turned)
    slot_of = {}
    for _, _, members in GROUPS:
        for pair, _, second in members:
            if second:
                slot_of[pair] = len(slot_of)
    for pair in range(len(PAIRS)):
        wide[pair] = jnp.zeros((PAD, tiles * LANES), F32)
        wide[pair, :BINS, : BINS * BINS] = gain[pair].astype(F32)
        if pair in slot_of:
            for tile in range(tiles):
                part = wide[pair, :, tile * LANES : (tile + 1) * LANES]
                part = jnp.concatenate([part, jnp.zeros((LANES - PAD, LANES), F32)], axis=0)
                turned[slot_of[pair], tile * LANES : (tile + 1) * LANES, :] = part.T
    last_rows[...] = jnp.zeros_like(last_rows)
    for group, (_, _, members) in enumerate(GROUPS):
        for factor in range(BINS):
            halves = [jnp.zeros((PAD, LANES), F32), jnp.zeros((PAD, LANES), F32)]
            second_members = [m for m in members if m[2]]
            if second_members:
                rows = []
                for other in range(CLASSES - 1):
                    found = [m for m in second_members if m[1] == other]
                    if found:
                        piece = turned[slot_of[found[0][0]], pl.ds(factor, PAD, stride=BINS), :]
                        rows.append(piece)
                    else:
                        rows.append(jnp.zeros((PAD, LANES), F32))
                rows.append(jnp.zeros((LANES - 3 * PAD, LANES), F32))
                halves[0] = jnp.concatenate(rows, axis=0).T[:PAD]
            for pair, other, second in members:
                if second:
                    continue
                start = BINS * factor
                tile, inside = divmod(start, LANES)
                half, at = divmod(OFF[other], LANES)
                shift = (at - inside) % LANES
                first = wide[pair, :, tile * LANES : (tile + 1) * LANES]
                first = pltpu.roll(first, shift, 1) if shift else first
                if inside + BINS > LANES:
                    rest = wide[pair, :, (tile + 1) * LANES : (tile + 2) * LANES]
                    rest = pltpu.roll(rest, shift, 1) if shift else rest
                    first = jnp.where(lane < at + LANES - inside, first, rest)
                halves[half] = jnp.where((lane >= at) & (lane < at + BINS), first, halves[half])
            full = jnp.concatenate(halves, axis=1)
            blocks[group, factor * HEAD : (factor + 1) * HEAD, :] = full[:HEAD].astype(BF16)
            last_rows[group * PAD + factor : group * PAD + factor + 1, :] = full[HEAD : HEAD + 1]
    tails[...] = last_rows[...].astype(BF16)
    upper[...] = jnp.zeros_like(upper)
    for pair, (first, second) in enumerate(PAIRS):
        half, at = divmod(OFF[second], LANES)
        rates = jnp.concatenate(
            [loss[pair].astype(F32), jnp.zeros((BINS, LANES - BINS), F32)], axis=1
        )
        rates = pltpu.roll(rates, at, 1) if at else rates
        rows = slice(OFF[first], OFF[first] + BINS)
        span = slice(half * LANES, (half + 1) * LANES)
        upper[rows, span] = upper[rows, span] + rates
    whole = upper[...]
    losses[...] = (whole + whole.T)[: losses.shape[0]].astype(BF16)
    fill_moves(moves)


def fill_moves(moves):
    moves[...] = jnp.zeros_like(moves)
    for part, step in enumerate((LEV, 2 * LEV)):
        source = lax.broadcasted_iota(jnp.int32, (LANES, LANES), 0)
        target = lax.broadcasted_iota(jnp.int32, (LANES, LANES), 1)
        moves[part, :LANES, :LANES] = jnp.where(source == target - step, 1.0, 0.0).astype(BF16)
        moves[part, :LANES, LANES:] = jnp.where(source == target + step, 1.0, 0.0).astype(BF16)
        source, target = source[:GROUP], target[:GROUP]
        half = GROUP // 2
        low = (target < step) & (source == target + half - step)
        high = (target >= LANES - step) & (source == target - (LANES - step) + half)
        rows = slice(EDGE, EDGE + GROUP)
        moves[part, rows, :LANES] = jnp.where(low, 1.0, 0.0).astype(BF16)
        moves[part, rows, LANES:] = jnp.where(high, 1.0, 0.0).astype(BF16)


def prepare(gain_kernel, loss_rate):
    wide = -(-BINS * BINS // LANES) * LANES
    tail = -(-NG * PAD // 16) * 16
    rows = -(-ROWS // 16) * 16
    return pl.pallas_call(
        prepare_kernel,
        out_shape=(
            jax.ShapeDtypeStruct((NG, BINS * HEAD, 2 * LANES), BF16),
            jax.ShapeDtypeStruct((tail, 2 * LANES), BF16),
            jax.ShapeDtypeStruct((rows, 2 * LANES), BF16),
            jax.ShapeDtypeStruct((2, EDGE + LANES, 2 * LANES), BF16),
        ),
        scratch_shapes=[
            pltpu.VMEM((len(PAIRS), PAD, wide), F32),
            pltpu.VMEM((4, BINS * PAD + BINS, LANES), F32),
            pltpu.VMEM((2 * LANES, 2 * LANES), F32),
            pltpu.VMEM((tail, 2 * LANES), F32),
        ],
        compiler_params=pltpu.CompilerParams(vmem_limit_bytes=VMEM_LIMIT),
        cost_estimate=pl.CostEstimate(flops=2 * 10**9, bytes_accessed=4 << 20, transcendentals=0),
    )(gain_kernel, loss_rate)


def collide_tiles(bins, row0, blocks, tails, losses, slots, ends, sinks, emit):
    for unit in range(2):
        right = jnp.concatenate([bins[row0 + 2 * unit], bins[row0 + 2 * unit + 1]], axis=1)
        right = jnp.concatenate(
            [right, jnp.zeros((2 * LANES - ROWS, 2 * LANES), F32)], axis=0
        ).astype(BF16)
        pltpu.matmul_push_rhs(right, 0, unit)
    for unit in range(2):
        pltpu.matmul_acc_lhs(ends[unit], tails[...], 0)
    for unit in range(2):
        pltpu.matmul_acc_lhs(sinks[unit], losses[...])
    depth = len(slots[0])
    pending, count = [], 0
    parts = {t: [[jnp.zeros((HEAD, LANES), F32) for _ in range(2)] for _ in range(2)] for t in (1, 2, 3)}

    def drain():
        target, source, factor, slot = pending.pop(0)
        for unit in range(2):
            block = pltpu.matmul_pop(slots[unit][slot])
            for half in range(2):
                scale = bins[row0 + 2 * unit + half, pl.ds(OFF[source] + factor, 1), :]
                part = block[:, half * LANES : (half + 1) * LANES]
                parts[target][unit][half] = parts[target][unit][half] + part * scale

    last = [[[jnp.zeros((PAD, LANES), F32) for _ in range(2)] for _ in range(2)] for _ in range(4)]
    for unit in range(2):
        block = pltpu.matmul_pop(ends[unit])
        for group, (target, source, _) in enumerate(GROUPS):
            for half in range(2):
                scale = bins[row0 + 2 * unit + half, OFF[source] : OFF[source] + PAD, :]
                piece = block[group * PAD : (group + 1) * PAD, half * LANES : (half + 1) * LANES]
                last[target][unit][half] = last[target][unit][half] + piece * scale
    drop = [pltpu.matmul_pop(sinks[unit]) for unit in range(2)]
    for unit in range(2):
        for half in range(2):
            row = row0 + 2 * unit + half
            for member in range(CLASSES):
                rows = slice(OFF[member], OFF[member] + PAD)
                lost = drop[unit][rows, half * LANES : (half + 1) * LANES] * bins[row, rows, :]
                if member:
                    bottom = jnp.sum(last[member][unit][half], axis=0, keepdims=True)
                    bottom = jnp.concatenate([bottom, jnp.zeros((PAD - HEAD - 1, LANES), F32)], axis=0)
                    base = jnp.concatenate([-lost[:HEAD], bottom - lost[HEAD:]], axis=0)
                else:
                    base = -lost
                emit(2 * unit + half, member, None, base)
    for target in (1, 2, 3):
        order = [
            (group, source, factor)
            for factor in range(BINS)
            for group, (aim, source, _) in enumerate(GROUPS)
            if aim == target
        ]
        for group, source, factor in order:
            slot = count % depth
            count += 1
            left = blocks[group, factor * HEAD : (factor + 1) * HEAD, :]
            for unit in range(2):
                pltpu.matmul_acc_lhs(slots[unit][slot], left)
            pending.append((target, source, factor, slot))
            if len(pending) > LOOK:
                drain()
        while pending:
            drain()
        for unit in range(2):
            for half in range(2):
                emit(2 * unit + half, target, parts[target][unit][half], None)


def accumulators(depth, tail, rows):
    return (
        [pltpu.ACC(unit)((HEAD, 2 * LANES), F32) for unit in range(2) for _ in range(depth)]
        + [pltpu.ACC(unit)((tail, 2 * LANES), F32) for unit in range(2)]
        + [pltpu.ACC(unit)((rows, 2 * LANES), F32) for unit in range(2)]
    )


def settle(field, mask, change, row, place):
    def emit(index, member, gained, base):
        at = row(index)
        start = OFF[member]
        if base is not None and member:
            change[place(index), start : start + PAD, :] = base
            return
        if member:
            base = change[place(index), start : start + PAD, :]
            base = jnp.concatenate([base[:HEAD] + gained, base[HEAD:]], axis=0)
        part = jnp.where(mask[at, :1, :] > 0.5, base.astype(BF16).astype(F32), 0.0)
        span = slice(start, start + PAD)
        field[at, span, :] = field[at, span, :] + part

    return emit


def four_rows(bins, row0, matrices, refs, field, mask, change):
    depth = LOOK + 2
    slots = (refs[:depth], refs[depth : 2 * depth])
    ends, sinks = refs[2 * depth : 2 * depth + 2], refs[2 * depth + 2 :]
    emit = settle(field, mask, change, lambda index: row0 + index, lambda index: index)
    collide_tiles(bins, row0, *matrices, slots, ends, sinks, emit)


def one_row(bins, row, matrices, refs, field, mask, change):
    blocks, tails, losses = matrices
    depth = LOOK + 2
    slots = (refs[:depth], refs[depth : 2 * depth])
    end, sink = refs[2 * depth], refs[2 * depth + 3]
    right = bins[row]
    right = jnp.concatenate([right, jnp.zeros((2 * LANES - ROWS, LANES), F32)], axis=0)
    right = jnp.concatenate([right, jnp.zeros((2 * LANES, LANES), F32)], axis=1).astype(BF16)
    for unit in range(2):
        pltpu.matmul_push_rhs(right, 0, unit)
    pltpu.matmul_acc_lhs(end, tails[...], 0)
    pltpu.matmul_acc_lhs(sink, losses[...], 0)
    emit = settle(field, mask, change, lambda index: row, lambda index: 0)
    block = pltpu.matmul_pop(end)[:, :LANES]
    last = [jnp.zeros((PAD, LANES), F32) for _ in range(CLASSES)]
    for group, (target, source, _) in enumerate(GROUPS):
        scale = bins[row, OFF[source] : OFF[source] + PAD, :]
        last[target] = last[target] + block[group * PAD : (group + 1) * PAD] * scale
    drop = pltpu.matmul_pop(sink)[:, :LANES]
    for member in range(CLASSES):
        span = slice(OFF[member], OFF[member] + PAD)
        base = -drop[span] * bins[row, span, :]
        if member:
            bottom = jnp.sum(last[member], axis=0, keepdims=True)
            bottom = jnp.concatenate([bottom, jnp.zeros((PAD - HEAD - 1, LANES), F32)], axis=0)
            base = jnp.concatenate([base[:HEAD], bottom + base[HEAD:]], axis=0)
        emit(0, member, None, base)
    parts = {t: [jnp.zeros((HEAD, LANES), F32) for _ in range(2)] for t in (1, 2, 3)}
    pending, count = [], 0

    def drain():
        target, source, factor, unit, slot = pending.pop(0)
        part = pltpu.matmul_pop(slots[unit][slot])[:, :LANES]
        scale = bins[row, OFF[source] + factor : OFF[source] + factor + 1, :]
        parts[target][unit] = parts[target][unit] + part * scale

    for target in (1, 2, 3):
        order = [
            (group, source, factor)
            for factor in range(BINS)
            for group, (aim, source, _) in enumerate(GROUPS)
            if aim == target
        ]
        for group, source, factor in order:
            unit, slot = count % 2, (count // 2) % len(slots[0])
            count += 1
            left = blocks[group, factor * HEAD : (factor + 1) * HEAD, :]
            pltpu.matmul_acc_lhs(slots[unit][slot], left)
            pending.append((target, source, factor, unit, slot))
            if len(pending) > 2 * LOOK:
                drain()
        while pending:
            drain()
        emit(0, target, parts[target][0] + parts[target][1], None)


def weights(tile, row):
    out, centre = [], 1.0
    for axis in range(2):
        first, second = (
            jnp.broadcast_to(tile[row, pl.ds(AUX + 2 * axis + part, 1), :], (SUBLANES, LANES))
            for part in range(2)
        )
        speed = (first + second) * (1.0 / 6.0)
        rising, falling = jnp.maximum(speed, 0.0), jnp.minimum(speed, 0.0)
        centre = centre - 3.0 * (rising - falling)
        out.append(
            (
                6.0 * rising + 2.0 * falling,
                -rising,
                -2.0 * rising - 6.0 * falling,
                falling,
            )
        )
    return centre, out


def cells(value):
    return value.reshape(value.shape[0] // SUBLANES, SUBLANES, LANES)


def advance(centre, along_x, along_y, coefficients):
    middle, (for_x, for_y) = coefficients
    total = middle * centre
    for values, factors in ((along_x, for_x), (along_y, for_y)):
        for value, factor in zip(values, factors):
            total = total + factor * value
    return jnp.maximum(total, 0.0)


def shifted(value, amount):
    amount = amount % LANES
    return pltpu.roll(value, amount, value.ndim - 1) if amount else value


def travel(jobs, moves, refs, finish):
    def issue(number, job):
        row, outside, place = job
        left = jnp.concatenate([row().astype(BF16), outside().astype(BF16)], axis=1)
        for unit in range(2):
            start = EDGE - GROUP * place
            right = [moves[unit, :LANES, :], moves[unit, start : start + LANES, :]]
            pltpu.matmul_push_rhs(jnp.concatenate(right, axis=0), number % 2, unit)
            pltpu.matmul_acc_lhs(refs[2 * (number % 2) + unit], left, number % 2)

    for number in range(len(jobs) + 1):
        if number < len(jobs):
            issue(number, jobs[number])
        if number:
            one, two = (pltpu.matmul_pop(refs[2 * ((number - 1) % 2) + unit]) for unit in range(2))
            finish(number - 1, (one[:, :LANES], two[:, :LANES], one[:, LANES:], two[:, LANES:]))


def travellers():
    return [pltpu.ACC(unit)((ROWS, 2 * LANES), F32) for _ in range(2) for unit in range(2)]


def lanes():
    return lax.broadcasted_iota(jnp.int32, (SUBLANES, LANES), 1)


def put(field, bins, row, span, value):
    value = value.reshape(PAD, LANES)
    field[row, span, :] = value
    bins[row, span, :] = value.astype(BF16).astype(F32)


def clear_gap(*arrays):
    for start, stop in ((OFF[2] + PAD, OFF[3]), (OFF[3] + PAD, ROWS)):
        for array in arrays:
            for row in range(array.shape[0]):
                array[row, start:stop, :] = jnp.zeros((stop - start, LANES), F32)


def stage_kernel(
    order, count, state_hbm, courant_x_hbm, courant_y_hbm, gain_hbm, loss_hbm,
    rows, edges, low, high, gain, loss, state, courant_x, courant_y, arrived,
):
    rows_x = state.shape[1]
    flat = state.reshape(state.shape[0] * rows_x, LANES)
    pieces = [
        (state_hbm.at[pl.ds(member * BINS, BINS)], state.at[pl.ds(member * BINS, BINS)])
        for member in range(CLASSES)
    ]
    pieces += [(courant_x_hbm, courant_x), (courant_y_hbm, courant_y)]
    pieces += [(gain_hbm, gain), (loss_hbm, loss)]
    copies = [
        pltpu.make_async_copy(source, target, arrived.at[number])
        for number, (source, target) in enumerate(pieces)
    ]
    for copy in copies:
        copy.start()
    for copy in copies[:-2]:
        copy.wait()
    spare = jnp.zeros((PAD - BINS, LANES), F32)
    for row in range(rows_x):
        cloudy = jnp.int32(0)
        for place in range(rows_x):
            hit = (order[0, 0, place] == row) & (place < count[0, 0])
            cloudy = cloudy | hit.astype(jnp.int32)
        for member in range(CLASSES):
            part = flat[pl.ds(member * BINS * rows_x + row, BINS, stride=rows_x), :]
            rows[row, OFF[member] : OFF[member] + BINS, :] = part
            rows[row, OFF[member] + BINS : OFF[member] + PAD, :] = spare
        for axis, courant in enumerate((courant_x, courant_y)):
            speed = courant[row : row + 1, :]
            upper = speed.astype(BF16).astype(F32)
            rows[row, AUX + 2 * axis : AUX + 2 * axis + 1, :] = upper
            rows[row, AUX + 2 * axis + 1 : AUX + 2 * axis + 2, :] = speed - upper
        rows[row, FLAG : FLAG + 1, :] = jnp.full((1, LANES), cloudy.astype(F32), F32)
    clear_gap(rows, edges)
    owner = lanes() // GROUP
    for start, stop in CHUNKS:
        left = jnp.zeros((PAD // SUBLANES, SUBLANES, LANES), F32)
        right = left
        for row in range(rows_x):
            value = cells(rows[row, start:stop, :])
            left = jnp.where(owner == row, shifted(value, GROUP * row), left)
            right = jnp.where(owner == row, shifted(value, GROUP * (row + 1)), right)
        edges[0, start:stop, :] = left.reshape(PAD, LANES)
        edges[1, start:stop, :] = right.reshape(PAD, LANES)
    low[...] = edges[0].astype(BF16)
    high[...] = edges[1].astype(BF16)
    for copy in copies[-2:]:
        copy.wait()


def widen_kernel(rows, before, after, around, to_right, to_left):
    rows_x = rows.shape[0]
    inner = lax.broadcasted_iota(jnp.int32, (ROWS, LANES), 1) % GROUP < GROUP // 2
    near = jnp.where(
        inner,
        shifted(before[...].astype(F32), -GROUP // 2),
        shifted(after[...].astype(F32), GROUP // 2),
    )
    around[0] = near
    for index in range(HALO):
        to_right[index] = rows[rows_x - HALO + index].astype(BF16)
        to_left[index] = rows[index].astype(BF16)
    to_right[HALO] = near.astype(BF16)
    to_left[HALO] = near.astype(BF16)


def inner_kernel(rows, around, moves, blocks, tails, losses, out, bins, change, mask):
    rows_x = rows.shape[0]
    clear_gap(out, bins)
    places = [index + HALO // 2 for index in range(rows_x - HALO)]

    def finish(index, along_y):
        row = places[index]
        coefficients = weights(rows, row)
        mask[index] = jnp.broadcast_to(rows[row, FLAG : FLAG + 1, :], mask.shape[1:])
        for start, stop in CHUNKS:
            span = slice(start, stop)
            centre = cells(rows[row, span, :])
            along_x = [cells(rows[row + d, span, :]) for d in (-1, -2, 1, 2)]
            beside = [cells(value[span]) for value in along_y]
            put(out, bins, index, span, advance(centre, along_x, beside, coefficients))

    jobs = [(lambda row=row: rows[row], lambda: around[0], row) for row in places]
    pl.run_scoped(lambda *refs: travel(jobs, moves, refs, finish), *travellers())
    matrices = (blocks, tails, losses)
    pl.run_scoped(
        lambda *refs: four_rows(bins, 0, matrices, refs, out, mask, change),
        *accumulators(LOOK + 2, tails.shape[0], losses.shape[0]),
    )


def outer_kernel(
    rows, edges, before, after, around, from_left, from_right, middle, moves, blocks, tails, losses,
    out, left, right, field, bins, change, mask, second,
):
    rows_x = rows.shape[0]
    lane = lanes()
    outside = rows_x + HALO
    for index in range(HALO + 1):
        left[index] = from_left[index].astype(F32)
        right[index] = from_right[index].astype(F32)
    clear_gap(field, bins, second)

    def column(x):
        if x < 0:
            return left, x + HALO
        if x >= rows_x:
            return right, x - rows_x
        return rows, x

    def outer_columns(x):
        if x < 0:
            return (lambda: left[HALO]), x + rows_x
        if x >= rows_x:
            return (lambda: right[HALO]), x - rows_x
        return (lambda: around[0]), x

    reach = HALO // 2
    places = list(range(-reach, reach)) + list(range(rows_x - reach, rows_x + reach))

    def job(x):
        tile, row = column(x)
        return (lambda: tile[row], *outer_columns(x))

    def first_step(index, beside):
        x = places[index]
        tile, row = column(x)
        coefficients = weights(tile, row)
        mask[x + reach] = jnp.broadcast_to(tile[row, FLAG : FLAG + 1, :], mask.shape[1:])
        for start, stop in CHUNKS:
            span = slice(start, stop)
            centre = cells(tile[row, span, :])
            along_x = []
            for d in (-1, -2, 1, 2):
                other, at = column(x + d)
                along_x.append(cells(other[at, span, :]))
            along_y = [cells(value[span]) for value in beside]
            put(field, bins, x + reach, span, advance(centre, along_x, along_y, coefficients))

    jobs = [job(x) for x in places]
    pl.run_scoped(lambda *refs: travel(jobs, moves, refs, first_step), *travellers())
    coefficients = weights(around, 0)
    mask[outside] = jnp.broadcast_to(around[0, FLAG : FLAG + 1, :], mask.shape[1:])
    inside = lane % GROUP
    half = GROUP // 2
    for start, stop in CHUNKS:
        span = slice(start, stop)
        lower, upper = cells(before[span, :].astype(F32)), cells(after[span, :].astype(F32))
        first, last = cells(edges[0, span, :]), cells(edges[1, span, :])
        centre = cells(around[0, span, :])
        along_y = (
            jnp.where(
                inside < half + LEV,
                shifted(jnp.where(inside < half + LEV, lower, last), -LEV),
                shifted(upper, half + LEV),
            ),
            jnp.where(inside < half, lower, last),
            jnp.where(
                inside < LEV,
                shifted(lower, -half - LEV),
                shifted(jnp.where(inside < LEV, first, upper), LEV),
            ),
            jnp.where(inside < half, first, upper),
        )
        beyond = jnp.where(
            lane >= LANES // 2, cells(left[HALO, span, :]), cells(right[HALO, span, :])
        )
        along_x = (
            shifted(jnp.where(lane >= LANES - GROUP, beyond, centre), GROUP),
            shifted(jnp.where(lane >= LANES - 2 * GROUP, beyond, centre), 2 * GROUP),
            shifted(jnp.where(lane < GROUP, beyond, centre), -GROUP),
            shifted(jnp.where(lane < 2 * GROUP, beyond, centre), -2 * GROUP),
        )
        put(field, bins, outside, span, advance(centre, along_x, along_y, coefficients))
    for index in range(rows_x - HALO):
        field[index + HALO] = middle[index]
        row = index + reach
        mask[index + HALO] = jnp.broadcast_to(rows[row, FLAG : FLAG + 1, :], mask.shape[1:])
    matrices = (blocks, tails, losses)

    def first_collisions(*refs):
        one_row(bins, outside, matrices, refs, field, mask, change)

        @pl.loop(0, 2)
        def _(step):
            four_rows(bins, rows_x * step, matrices, refs, field, mask, change)

    def second_step(x, beside):
        coefficients = weights(rows, x)
        for start, stop in CHUNKS:
            span = slice(start, stop)
            centre = cells(field[x + reach, span, :])
            along_x = [cells(field[x + reach + d, span, :]) for d in (-1, -2, 1, 2)]
            along_y = [cells(value[span]) for value in beside]
            put(second, bins, x + reach, span, advance(centre, along_x, along_y, coefficients))

    def second_collisions(*refs):
        @pl.loop(0, rows_x // 4)
        def _(step):
            four_rows(bins, reach + 4 * step, matrices, refs, second, mask, change)

    shapes = accumulators(LOOK + 2, tails.shape[0], losses.shape[0])
    pl.run_scoped(first_collisions, *shapes)
    later = [(lambda x=x: field[x + reach], lambda: field[outside], x) for x in range(rows_x)]
    pl.run_scoped(lambda *refs: travel(later, moves, refs, second_step), *travellers())
    pl.run_scoped(second_collisions, *shapes)
    flat = out.reshape(out.shape[0] * rows_x, LANES)
    for x in range(rows_x):
        for member in range(CLASSES):
            span = pl.ds(member * BINS * rows_x + x, BINS, stride=rows_x)
            flat[span, :] = second[x + reach, OFF[member] : OFF[member] + BINS, :]


def call(kernel, outs, scratch, *arguments, scalars=0, direct=0, flops=0):
    vmem = pl.BlockSpec(memory_space=pltpu.VMEM)
    smem = pl.BlockSpec(memory_space=pltpu.SMEM)
    hbm = pl.BlockSpec(memory_space=pltpu.HBM)
    shapes = tuple(jax.ShapeDtypeStruct(shape, dtype) for shape, dtype in outs)
    moved = sum(a.size * a.dtype.itemsize for a in arguments)
    staged = len(arguments) - scalars - direct
    waits = [pltpu.SemaphoreType.DMA((direct + CLASSES - 1,))] if direct else []
    return pl.pallas_call(
        kernel,
        out_shape=shapes,
        in_specs=[smem] * scalars + [hbm] * direct + [vmem] * staged,
        out_specs=tuple(vmem for _ in shapes),
        scratch_shapes=[pltpu.VMEM(shape, F32) for shape in scratch] + waits,
        compiler_params=pltpu.CompilerParams(vmem_limit_bytes=VMEM_LIMIT),
        cost_estimate=pl.CostEstimate(flops=flops, bytes_accessed=moved, transcendentals=0),
    )(*arguments)


def exchange(axis, upward, downward):
    size = lax.axis_size(axis)
    up = [(i, (i + 1) % size) for i in range(size)]
    down = [(j, i) for i, j in up]
    return lax.ppermute(upward, axis, up), lax.ppermute(downward, axis, down)


def per_device(bin_state, courant_x, courant_y, cloudy_order, block_count, gain_kernel, loss_rate):
    rows_x = bin_state.shape[1]
    tile = (ROWS, LANES)
    rows, edges, low, high, gain, loss = call(
        stage_kernel,
        [
            ((rows_x, *tile), F32),
            ((2, *tile), F32),
            (tile, BF16),
            (tile, BF16),
            (gain_kernel.shape, BF16),
            (loss_rate.shape, BF16),
        ],
        [bin_state.shape, courant_x.shape, courant_y.shape],
        cloudy_order, block_count, bin_state, courant_x, courant_y, gain_kernel, loss_rate,
        scalars=2, direct=5,
    )
    before, after = exchange("gy", high, low)
    *matrices, moves = prepare(gain, loss)
    around, to_right, to_left = call(
        widen_kernel,
        [((1, *tile), F32), ((HALO + 1, *tile), BF16), ((HALO + 1, *tile), BF16)],
        [],
        rows, before, after,
    )
    from_left, from_right = exchange("gx", to_right, to_left)
    inner = rows_x - HALO
    (middle,) = call(
        inner_kernel,
        [((inner, *tile), F32)],
        [(inner, *tile), (4, *tile), (inner, 8, LANES)],
        rows, around, moves, *matrices,
        flops=5 * 10**9,
    )
    total = rows_x + HALO + 1
    (out,) = call(
        outer_kernel,
        [(bin_state.shape, F32)],
        [
            (HALO + 1, *tile),
            (HALO + 1, *tile),
            (total, *tile),
            (total, *tile),
            (4, *tile),
            (total, 8, LANES),
            (total, *tile),
        ],
        rows, edges, before, after, around, from_left, from_right, middle, moves, *matrices,
        flops=20 * 10**9,
    )
    return out


def solution(mesh):
    placed = (
        P(None, "gx", "gy"),
        P("gx", "gy"),
        P("gx", "gy"),
        P("gx", "gy", None),
        P("gy", "gx"),
        P(),
        P(),
    )
    sharded = jax.shard_map(
        per_device, mesh=mesh, in_specs=placed, out_specs=P(None, "gx", "gy"), check_vma=False
    )

    def run(*arguments):
        with jax.sharding.use_abstract_mesh(mesh.abstract_mesh):
            return sharded(*arguments)

    return run
```

```python
import functools
import jax
import jax.numpy as jnp
from jax import lax
from jax.experimental import pallas as pl
from jax.experimental.pallas import tpu as pltpu
from jax.sharding import PartitionSpec as P

BINS = 33
CLASSES = 4
LEV = 4
STEPS = 2
LANES = 128
SUBLANES = 8
OFF = (0, 40, 80, 128)
ROWS = 176
PAD = 40
HEAD = 32
LOOK = 14
HALO = 2 * STEPS
GROUP = HALO * LEV
AUX = BINS
FLAG = AUX + 4
EDGE = 2 * LANES - GROUP
CHUNKS = tuple((OFF[member], OFF[member] + PAD) for member in range(CLASSES))
VMEM_LIMIT = 24 << 20

GROUPS = (
    (1, 0, ((0, 0, False), (1, 1, False))),
    (1, 1, ((4, 1, False),)),
    (2, 0, ((2, 2, False),)),
    (3, 3, ((3, 0, True), (6, 1, True), (8, 2, True), (9, 3, False))),
    (3, 2, ((5, 1, True), (7, 2, False))),
)
PAIRS = ((0, 0), (0, 1), (0, 2), (0, 3), (1, 1), (1, 2), (1, 3), (2, 2), (2, 3), (3, 3))
NG = len(GROUPS)
F32 = jnp.float32
BF16 = jnp.bfloat16


def prepare_kernel(gain, loss, blocks, tails, losses, moves, wide, turned, upper, last_rows):
    lane = lax.broadcasted_iota(jnp.int32, (PAD, LANES), 1)
    tiles = wide.shape[2] // LANES
    turned[...] = jnp.zeros_like(turned)
    slot_of = {}
    for _, _, members in GROUPS:
        for pair, _, second in members:
            if second:
                slot_of[pair] = len(slot_of)
    for pair in range(len(PAIRS)):
        wide[pair] = jnp.zeros((PAD, tiles * LANES), F32)
        wide[pair, :BINS, : BINS * BINS] = gain[pair].astype(F32)
        if pair in slot_of:
            for tile in range(tiles):
                part = wide[pair, :, tile * LANES : (tile + 1) * LANES]
                part = jnp.concatenate([part, jnp.zeros((LANES - PAD, LANES), F32)], axis=0)
                turned[slot_of[pair], tile * LANES : (tile + 1) * LANES, :] = part.T
    last_rows[...] = jnp.zeros_like(last_rows)
    for group, (_, _, members) in enumerate(GROUPS):
        for factor in range(BINS):
            halves = [jnp.zeros((PAD, LANES), F32), jnp.zeros((PAD, LANES), F32)]
            second_members = [m for m in members if m[2]]
            if second_members:
                rows = []
                for other in range(CLASSES - 1):
                    found = [m for m in second_members if m[1] == other]
                    if found:
                        piece = turned[slot_of[found[0][0]], pl.ds(factor, PAD, stride=BINS), :]
                        rows.append(piece)
                    else:
                        rows.append(jnp.zeros((PAD, LANES), F32))
                rows.append(jnp.zeros((LANES - 3 * PAD, LANES), F32))
                halves[0] = jnp.concatenate(rows, axis=0).T[:PAD]
            for pair, other, second in members:
                if second:
                    continue
                start = BINS * factor
                tile, inside = divmod(start, LANES)
                half, at = divmod(OFF[other], LANES)
                shift = (at - inside) % LANES
                first = wide[pair, :, tile * LANES : (tile + 1) * LANES]
                first = pltpu.roll(first, shift, 1) if shift else first
                if inside + BINS > LANES:
                    rest = wide[pair, :, (tile + 1) * LANES : (tile + 2) * LANES]
                    rest = pltpu.roll(rest, shift, 1) if shift else rest
                    first = jnp.where(lane < at + LANES - inside, first, rest)
                halves[half] = jnp.where((lane >= at) & (lane < at + BINS), first, halves[half])
            full = jnp.concatenate(halves, axis=1)
            blocks[group, factor * HEAD : (factor + 1) * HEAD, :] = full[:HEAD].astype(BF16)
            last_rows[group * PAD + factor : group * PAD + factor + 1, :] = full[HEAD : HEAD + 1]
    tails[...] = last_rows[...].astype(BF16)
    upper[...] = jnp.zeros_like(upper)
    for pair, (first, second) in enumerate(PAIRS):
        half, at = divmod(OFF[second], LANES)
        rates = jnp.concatenate(
            [loss[pair].astype(F32), jnp.zeros((BINS, LANES - BINS), F32)], axis=1
        )
        rates = pltpu.roll(rates, at, 1) if at else rates
        rows = slice(OFF[first], OFF[first] + BINS)
        span = slice(half * LANES, (half + 1) * LANES)
        upper[rows, span] = upper[rows, span] + rates
    whole = upper[...]
    losses[...] = (whole + whole.T)[: losses.shape[0]].astype(BF16)
    fill_moves(moves)


def fill_moves(moves):
    moves[...] = jnp.zeros_like(moves)
    for part, step in enumerate((LEV, 2 * LEV)):
        source = lax.broadcasted_iota(jnp.int32, (LANES, LANES), 0)
        target = lax.broadcasted_iota(jnp.int32, (LANES, LANES), 1)
        moves[part, :LANES, :LANES] = jnp.where(source == target - step, 1.0, 0.0).astype(BF16)
        moves[part, :LANES, LANES:] = jnp.where(source == target + step, 1.0, 0.0).astype(BF16)
        source, target = source[:GROUP], target[:GROUP]
        half = GROUP // 2
        low = (target < step) & (source == target + half - step)
        high = (target >= LANES - step) & (source == target - (LANES - step) + half)
        rows = slice(EDGE, EDGE + GROUP)
        moves[part, rows, :LANES] = jnp.where(low, 1.0, 0.0).astype(BF16)
        moves[part, rows, LANES:] = jnp.where(high, 1.0, 0.0).astype(BF16)


def prepare(gain_kernel, loss_rate):
    wide = -(-BINS * BINS // LANES) * LANES
    tail = -(-NG * PAD // 16) * 16
    rows = -(-ROWS // 16) * 16
    return pl.pallas_call(
        prepare_kernel,
        out_shape=(
            jax.ShapeDtypeStruct((NG, BINS * HEAD, 2 * LANES), BF16),
            jax.ShapeDtypeStruct((tail, 2 * LANES), BF16),
            jax.ShapeDtypeStruct((rows, 2 * LANES), BF16),
            jax.ShapeDtypeStruct((2, EDGE + LANES, 2 * LANES), BF16),
        ),
        scratch_shapes=[
            pltpu.VMEM((len(PAIRS), PAD, wide), F32),
            pltpu.VMEM((4, BINS * PAD + BINS, LANES), F32),
            pltpu.VMEM((2 * LANES, 2 * LANES), F32),
            pltpu.VMEM((tail, 2 * LANES), F32),
        ],
        compiler_params=pltpu.CompilerParams(vmem_limit_bytes=VMEM_LIMIT),
        cost_estimate=pl.CostEstimate(flops=2 * 10**9, bytes_accessed=4 << 20, transcendentals=0),
    )(gain_kernel, loss_rate)


def collide_tiles(bins, row0, blocks, tails, losses, slots, ends, sinks, emit):
    for unit in range(2):
        right = jnp.concatenate([bins[row0 + 2 * unit], bins[row0 + 2 * unit + 1]], axis=1)
        right = jnp.concatenate(
            [right, jnp.zeros((2 * LANES - ROWS, 2 * LANES), F32)], axis=0
        ).astype(BF16)
        pltpu.matmul_push_rhs(right, 0, unit)
    for unit in range(2):
        pltpu.matmul_acc_lhs(ends[unit], tails[...], 0)
    for unit in range(2):
        pltpu.matmul_acc_lhs(sinks[unit], losses[...])
    depth = len(slots[0])
    pending, count = [], 0
    parts = {t: [[jnp.zeros((HEAD, LANES), F32) for _ in range(2)] for _ in range(2)] for t in (1, 2, 3)}

    def drain():
        target, source, factor, slot = pending.pop(0)
        for unit in range(2):
            block = pltpu.matmul_pop(slots[unit][slot])
            for half in range(2):
                scale = bins[row0 + 2 * unit + half, pl.ds(OFF[source] + factor, 1), :]
                part = block[:, half * LANES : (half + 1) * LANES]
                parts[target][unit][half] = parts[target][unit][half] + part * scale

    last = [[[jnp.zeros((PAD, LANES), F32) for _ in range(2)] for _ in range(2)] for _ in range(4)]
    for unit in range(2):
        block = pltpu.matmul_pop(ends[unit])
        for group, (target, source, _) in enumerate(GROUPS):
            for half in range(2):
                scale = bins[row0 + 2 * unit + half, OFF[source] : OFF[source] + PAD, :]
                piece = block[group * PAD : (group + 1) * PAD, half * LANES : (half + 1) * LANES]
                last[target][unit][half] = last[target][unit][half] + piece * scale
    drop = [pltpu.matmul_pop(sinks[unit]) for unit in range(2)]
    for unit in range(2):
        for half in range(2):
            row = row0 + 2 * unit + half
            for member in range(CLASSES):
                rows = slice(OFF[member], OFF[member] + PAD)
                lost = drop[unit][rows, half * LANES : (half + 1) * LANES] * bins[row, rows, :]
                if member:
                    bottom = jnp.sum(last[member][unit][half], axis=0, keepdims=True)
                    bottom = jnp.concatenate([bottom, jnp.zeros((PAD - HEAD - 1, LANES), F32)], axis=0)
                    base = jnp.concatenate([-lost[:HEAD], bottom - lost[HEAD:]], axis=0)
                else:
                    base = -lost
                emit(2 * unit + half, member, None, base)
    for target in (1, 2, 3):
        order = [
            (group, source, factor)
            for factor in range(BINS)
            for group, (aim, source, _) in enumerate(GROUPS)
            if aim == target
        ]
        for group, source, factor in order:
            slot = count % depth
            count += 1
            left = blocks[group, factor * HEAD : (factor + 1) * HEAD, :]
            for unit in range(2):
                pltpu.matmul_acc_lhs(slots[unit][slot], left)
            pending.append((target, source, factor, slot))
            if len(pending) > LOOK:
                drain()
        while pending:
            drain()
        for unit in range(2):
            for half in range(2):
                emit(2 * unit + half, target, parts[target][unit][half], None)


def accumulators(depth, tail, rows):
    return (
        [pltpu.ACC(unit)((HEAD, 2 * LANES), F32) for unit in range(2) for _ in range(depth)]
        + [pltpu.ACC(unit)((tail, 2 * LANES), F32) for unit in range(2)]
        + [pltpu.ACC(unit)((rows, 2 * LANES), F32) for unit in range(2)]
    )


def settle(field, mask, change, row, place):
    def emit(index, member, gained, base):
        at = row(index)
        start = OFF[member]
        if base is not None and member:
            change[place(index), start : start + PAD, :] = base
            return
        if member:
            base = change[place(index), start : start + PAD, :]
            base = jnp.concatenate([base[:HEAD] + gained, base[HEAD:]], axis=0)
        part = jnp.where(mask[at, :1, :] > 0.5, base.astype(BF16).astype(F32), 0.0)
        span = slice(start, start + PAD)
        field[at, span, :] = field[at, span, :] + part

    return emit


def four_rows(bins, row0, matrices, refs, field, mask, change):
    depth = LOOK + 2
    slots = (refs[:depth], refs[depth : 2 * depth])
    ends, sinks = refs[2 * depth : 2 * depth + 2], refs[2 * depth + 2 :]
    emit = settle(field, mask, change, lambda index: row0 + index, lambda index: index)
    collide_tiles(bins, row0, *matrices, slots, ends, sinks, emit)


def one_row(bins, row, matrices, refs, field, mask, change):
    blocks, tails, losses = matrices
    depth = LOOK + 2
    slots = (refs[:depth], refs[depth : 2 * depth])
    end, sink = refs[2 * depth], refs[2 * depth + 3]
    right = bins[row]
    right = jnp.concatenate([right, jnp.zeros((2 * LANES - ROWS, LANES), F32)], axis=0)
    right = jnp.concatenate([right, jnp.zeros((2 * LANES, LANES), F32)], axis=1).astype(BF16)
    for unit in range(2):
        pltpu.matmul_push_rhs(right, 0, unit)
    pltpu.matmul_acc_lhs(end, tails[...], 0)
    pltpu.matmul_acc_lhs(sink, losses[...], 0)
    emit = settle(field, mask, change, lambda index: row, lambda index: 0)
    block = pltpu.matmul_pop(end)[:, :LANES]
    last = [jnp.zeros((PAD, LANES), F32) for _ in range(CLASSES)]
    for group, (target, source, _) in enumerate(GROUPS):
        scale = bins[row, OFF[source] : OFF[source] + PAD, :]
        last[target] = last[target] + block[group * PAD : (group + 1) * PAD] * scale
    drop = pltpu.matmul_pop(sink)[:, :LANES]
    for member in range(CLASSES):
        span = slice(OFF[member], OFF[member] + PAD)
        base = -drop[span] * bins[row, span, :]
        if member:
            bottom = jnp.sum(last[member], axis=0, keepdims=True)
            bottom = jnp.concatenate([bottom, jnp.zeros((PAD - HEAD - 1, LANES), F32)], axis=0)
            base = jnp.concatenate([base[:HEAD], bottom + base[HEAD:]], axis=0)
        emit(0, member, None, base)
    parts = {t: [jnp.zeros((HEAD, LANES), F32) for _ in range(2)] for t in (1, 2, 3)}
    pending, count = [], 0

    def drain():
        target, source, factor, unit, slot = pending.pop(0)
        part = pltpu.matmul_pop(slots[unit][slot])[:, :LANES]
        scale = bins[row, OFF[source] + factor : OFF[source] + factor + 1, :]
        parts[target][unit] = parts[target][unit] + part * scale

    for target in (1, 2, 3):
        order = [
            (group, source, factor)
            for factor in range(BINS)
            for group, (aim, source, _) in enumerate(GROUPS)
            if aim == target
        ]
        for group, source, factor in order:
            unit, slot = count % 2, (count // 2) % len(slots[0])
            count += 1
            left = blocks[group, factor * HEAD : (factor + 1) * HEAD, :]
            pltpu.matmul_acc_lhs(slots[unit][slot], left)
            pending.append((target, source, factor, unit, slot))
            if len(pending) > 2 * LOOK:
                drain()
        while pending:
            drain()
        emit(0, target, parts[target][0] + parts[target][1], None)


def weights(tile, row):
    out, centre = [], 1.0
    for axis in range(2):
        first, second = (
            jnp.broadcast_to(tile[row, pl.ds(AUX + 2 * axis + part, 1), :], (SUBLANES, LANES))
            for part in range(2)
        )
        speed = (first + second) * (1.0 / 6.0)
        rising, falling = jnp.maximum(speed, 0.0), jnp.minimum(speed, 0.0)
        centre = centre - 3.0 * (rising - falling)
        out.append(
            (
                6.0 * rising + 2.0 * falling,
                -rising,
                -2.0 * rising - 6.0 * falling,
                falling,
            )
        )
    return centre, out


def cells(value):
    return value.reshape(value.shape[0] // SUBLANES, SUBLANES, LANES)


def advance(centre, along_x, along_y, coefficients):
    middle, (for_x, for_y) = coefficients
    total = middle * centre
    for values, factors in ((along_x, for_x), (along_y, for_y)):
        for value, factor in zip(values, factors):
            total = total + factor * value
    return jnp.maximum(total, 0.0)


def shifted(value, amount):
    amount = amount % LANES
    return pltpu.roll(value, amount, value.ndim - 1) if amount else value


def travel(jobs, moves, refs, finish):
    def issue(number, job):
        row, outside, place = job
        left = jnp.concatenate([row().astype(BF16), outside().astype(BF16)], axis=1)
        for unit in range(2):
            start = EDGE - GROUP * place
            right = [moves[unit, :LANES, :], moves[unit, start : start + LANES, :]]
            pltpu.matmul_push_rhs(jnp.concatenate(right, axis=0), number % 2, unit)
            pltpu.matmul_acc_lhs(refs[2 * (number % 2) + unit], left, number % 2)

    for number in range(len(jobs) + 1):
        if number < len(jobs):
            issue(number, jobs[number])
        if number:
            one, two = (pltpu.matmul_pop(refs[2 * ((number - 1) % 2) + unit]) for unit in range(2))
            finish(number - 1, (one[:, :LANES], two[:, :LANES], one[:, LANES:], two[:, LANES:]))


def travellers():
    return [pltpu.ACC(unit)((ROWS, 2 * LANES), F32) for _ in range(2) for unit in range(2)]


def lanes():
    return lax.broadcasted_iota(jnp.int32, (SUBLANES, LANES), 1)


def put(field, bins, row, span, value):
    value = value.reshape(PAD, LANES)
    field[row, span, :] = value
    bins[row, span, :] = value.astype(BF16).astype(F32)


def clear_gap(*arrays):
    for start, stop in ((OFF[2] + PAD, OFF[3]), (OFF[3] + PAD, ROWS)):
        for array in arrays:
            for row in range(array.shape[0]):
                array[row, start:stop, :] = jnp.zeros((stop - start, LANES), F32)


def stage_kernel(
    count, order_hbm, state_hbm, courant_x_hbm, courant_y_hbm, gain_hbm, loss_hbm,
    rows, edges, low, high, gain, loss, state, courant_x, courant_y, order, arrived,
):
    rows_x = state.shape[1]
    flat = state.reshape(state.shape[0] * rows_x, LANES)
    pieces = [
        (state_hbm.at[pl.ds(member * BINS, BINS)], state.at[pl.ds(member * BINS, BINS)])
        for member in range(CLASSES)
    ]
    pieces += [(courant_x_hbm, courant_x), (courant_y_hbm, courant_y)]
    pieces += [(order_hbm, order)]
    pieces += [(gain_hbm, gain), (loss_hbm, loss)]
    copies = [
        pltpu.make_async_copy(source, target, arrived.at[number])
        for number, (source, target) in enumerate(pieces)
    ]
    for copy in copies:
        copy.start()
    for copy in copies[:-2]:
        copy.wait()
    spare = jnp.zeros((PAD - BINS, LANES), F32)
    for row in range(rows_x):
        cloudy = jnp.int32(0)
        for place in range(rows_x):
            hit = (order[0, 0, place] == row) & (place < count[0, 0])
            cloudy = cloudy | hit.astype(jnp.int32)
        for member in range(CLASSES):
            part = flat[pl.ds(member * BINS * rows_x + row, BINS, stride=rows_x), :]
            rows[row, OFF[member] : OFF[member] + BINS, :] = part
            rows[row, OFF[member] + BINS : OFF[member] + PAD, :] = spare
        for axis, courant in enumerate((courant_x, courant_y)):
            speed = courant[row : row + 1, :]
            upper = speed.astype(BF16).astype(F32)
            rows[row, AUX + 2 * axis : AUX + 2 * axis + 1, :] = upper
            rows[row, AUX + 2 * axis + 1 : AUX + 2 * axis + 2, :] = speed - upper
        rows[row, FLAG : FLAG + 1, :] = jnp.full((1, LANES), cloudy.astype(F32), F32)
    clear_gap(rows, edges)
    owner = lanes() // GROUP
    for start, stop in CHUNKS:
        left = jnp.zeros((PAD // SUBLANES, SUBLANES, LANES), F32)
        right = left
        for row in range(rows_x):
            value = cells(rows[row, start:stop, :])
            left = jnp.where(owner == row, shifted(value, GROUP * row), left)
            right = jnp.where(owner == row, shifted(value, GROUP * (row + 1)), right)
        edges[0, start:stop, :] = left.reshape(PAD, LANES)
        edges[1, start:stop, :] = right.reshape(PAD, LANES)
    low[...] = edges[0].astype(BF16)
    high[...] = edges[1].astype(BF16)
    for copy in copies[-2:]:
        copy.wait()


def widen_kernel(rows, before, after, around, to_right, to_left):
    rows_x = rows.shape[0]
    inner = lax.broadcasted_iota(jnp.int32, (ROWS, LANES), 1) % GROUP < GROUP // 2
    near = jnp.where(
        inner,
        shifted(before[...].astype(F32), -GROUP // 2),
        shifted(after[...].astype(F32), GROUP // 2),
    )
    around[0] = near
    for index in range(HALO):
        to_right[index] = rows[rows_x - HALO + index].astype(BF16)
        to_left[index] = rows[index].astype(BF16)
    to_right[HALO] = near.astype(BF16)
    to_left[HALO] = near.astype(BF16)


def inner_kernel(rows, around, moves, blocks, tails, losses, out, bins, change, mask):
    rows_x = rows.shape[0]
    clear_gap(out, bins)
    places = [index + HALO // 2 for index in range(rows_x - HALO)]

    def finish(index, along_y):
        row = places[index]
        coefficients = weights(rows, row)
        mask[index] = jnp.broadcast_to(rows[row, FLAG : FLAG + 1, :], mask.shape[1:])
        for start, stop in CHUNKS:
            span = slice(start, stop)
            centre = cells(rows[row, span, :])
            along_x = [cells(rows[row + d, span, :]) for d in (-1, -2, 1, 2)]
            beside = [cells(value[span]) for value in along_y]
            put(out, bins, index, span, advance(centre, along_x, beside, coefficients))

    jobs = [(lambda row=row: rows[row], lambda: around[0], row) for row in places]
    pl.run_scoped(lambda *refs: travel(jobs, moves, refs, finish), *travellers())
    matrices = (blocks, tails, losses)
    pl.run_scoped(
        lambda *refs: four_rows(bins, 0, matrices, refs, out, mask, change),
        *accumulators(LOOK + 2, tails.shape[0], losses.shape[0]),
    )


def outer_kernel(
    rows, edges, before, after, around, from_left, from_right, middle, moves, blocks, tails, losses,
    out, left, right, field, bins, change, mask, second,
):
    rows_x = rows.shape[0]
    lane = lanes()
    outside = rows_x + HALO
    for index in range(HALO + 1):
        left[index] = from_left[index].astype(F32)
        right[index] = from_right[index].astype(F32)
    clear_gap(field, bins, second)

    def column(x):
        if x < 0:
            return left, x + HALO
        if x >= rows_x:
            return right, x - rows_x
        return rows, x

    def outer_columns(x):
        if x < 0:
            return (lambda: left[HALO]), x + rows_x
        if x >= rows_x:
            return (lambda: right[HALO]), x - rows_x
        return (lambda: around[0]), x

    reach = HALO // 2
    places = list(range(-reach, reach)) + list(range(rows_x - reach, rows_x + reach))

    def job(x):
        tile, row = column(x)
        return (lambda: tile[row], *outer_columns(x))

    def first_step(index, beside):
        x = places[index]
        tile, row = column(x)
        coefficients = weights(tile, row)
        mask[x + reach] = jnp.broadcast_to(tile[row, FLAG : FLAG + 1, :], mask.shape[1:])
        for start, stop in CHUNKS:
            span = slice(start, stop)
            centre = cells(tile[row, span, :])
            along_x = []
            for d in (-1, -2, 1, 2):
                other, at = column(x + d)
                along_x.append(cells(other[at, span, :]))
            along_y = [cells(value[span]) for value in beside]
            put(field, bins, x + reach, span, advance(centre, along_x, along_y, coefficients))

    jobs = [job(x) for x in places]
    pl.run_scoped(lambda *refs: travel(jobs, moves, refs, first_step), *travellers())
    coefficients = weights(around, 0)
    mask[outside] = jnp.broadcast_to(around[0, FLAG : FLAG + 1, :], mask.shape[1:])
    inside = lane % GROUP
    half = GROUP // 2
    for start, stop in CHUNKS:
        span = slice(start, stop)
        lower, upper = cells(before[span, :].astype(F32)), cells(after[span, :].astype(F32))
        first, last = cells(edges[0, span, :]), cells(edges[1, span, :])
        centre = cells(around[0, span, :])
        along_y = (
            jnp.where(
                inside < half + LEV,
                shifted(jnp.where(inside < half + LEV, lower, last), -LEV),
                shifted(upper, half + LEV),
            ),
            jnp.where(inside < half, lower, last),
            jnp.where(
                inside < LEV,
                shifted(lower, -half - LEV),
                shifted(jnp.where(inside < LEV, first, upper), LEV),
            ),
            jnp.where(inside < half, first, upper),
        )
        beyond = jnp.where(
            lane >= LANES // 2, cells(left[HALO, span, :]), cells(right[HALO, span, :])
        )
        along_x = (
            shifted(jnp.where(lane >= LANES - GROUP, beyond, centre), GROUP),
            shifted(jnp.where(lane >= LANES - 2 * GROUP, beyond, centre), 2 * GROUP),
            shifted(jnp.where(lane < GROUP, beyond, centre), -GROUP),
            shifted(jnp.where(lane < 2 * GROUP, beyond, centre), -2 * GROUP),
        )
        put(field, bins, outside, span, advance(centre, along_x, along_y, coefficients))
    for index in range(rows_x - HALO):
        field[index + HALO] = middle[index]
        row = index + reach
        mask[index + HALO] = jnp.broadcast_to(rows[row, FLAG : FLAG + 1, :], mask.shape[1:])
    matrices = (blocks, tails, losses)

    def first_collisions(*refs):
        one_row(bins, outside, matrices, refs, field, mask, change)

        @pl.loop(0, 2)
        def _(step):
            four_rows(bins, rows_x * step, matrices, refs, field, mask, change)

    def second_step(x, beside):
        coefficients = weights(rows, x)
        for start, stop in CHUNKS:
            span = slice(start, stop)
            centre = cells(field[x + reach, span, :])
            along_x = [cells(field[x + reach + d, span, :]) for d in (-1, -2, 1, 2)]
            along_y = [cells(value[span]) for value in beside]
            put(second, bins, x + reach, span, advance(centre, along_x, along_y, coefficients))

    def second_collisions(*refs):
        @pl.loop(0, rows_x // 4)
        def _(step):
            four_rows(bins, reach + 4 * step, matrices, refs, second, mask, change)

    shapes = accumulators(LOOK + 2, tails.shape[0], losses.shape[0])
    pl.run_scoped(first_collisions, *shapes)
    later = [(lambda x=x: field[x + reach], lambda: field[outside], x) for x in range(rows_x)]
    pl.run_scoped(lambda *refs: travel(later, moves, refs, second_step), *travellers())
    pl.run_scoped(second_collisions, *shapes)
    flat = out.reshape(out.shape[0] * rows_x, LANES)
    for x in range(rows_x):
        for member in range(CLASSES):
            span = pl.ds(member * BINS * rows_x + x, BINS, stride=rows_x)
            flat[span, :] = second[x + reach, OFF[member] : OFF[member] + BINS, :]


def call(kernel, outs, scratch, *arguments, scalars=0, direct=0, flops=0):
    smem = pl.BlockSpec(memory_space=pltpu.SMEM)
    vmem = pl.BlockSpec(memory_space=pltpu.VMEM)
    hbm = pl.BlockSpec(memory_space=pltpu.HBM)
    shapes = tuple(jax.ShapeDtypeStruct(shape, dtype) for shape, dtype in outs)
    moved = sum(a.size * a.dtype.itemsize for a in arguments)
    own = [pltpu.VMEM(piece, F32) if isinstance(piece, tuple) else piece for piece in scratch]
    staged = scalars + direct
    held = [pltpu.with_memory_space_constraint(a, pltpu.HBM) for a in arguments[scalars:staged]]
    return pl.pallas_call(
        kernel,
        out_shape=shapes,
        in_specs=[smem] * scalars + [hbm] * direct + [vmem] * (len(arguments) - staged),
        out_specs=tuple(vmem for _ in shapes),
        scratch_shapes=own,
        compiler_params=pltpu.CompilerParams(vmem_limit_bytes=VMEM_LIMIT),
        cost_estimate=pl.CostEstimate(flops=flops, bytes_accessed=moved, transcendentals=0),
    )(*arguments[:scalars], *held, *arguments[staged:])


def exchange(axis, upward, downward):
    size = lax.axis_size(axis)
    up = [(i, (i + 1) % size) for i in range(size)]
    down = [(j, i) for i, j in up]
    return lax.ppermute(upward, axis, up), lax.ppermute(downward, axis, down)


def per_device(bin_state, courant_x, courant_y, cloudy_order, block_count, gain_kernel, loss_rate):
    rows_x = bin_state.shape[1]
    tile = (ROWS, LANES)
    rows, edges, low, high, gain, loss = call(
        stage_kernel,
        [
            ((rows_x, *tile), F32),
            ((2, *tile), F32),
            (tile, BF16),
            (tile, BF16),
            (gain_kernel.shape, BF16),
            (loss_rate.shape, BF16),
        ],
        [
            bin_state.shape,
            courant_x.shape,
            courant_y.shape,
            pltpu.SMEM(cloudy_order.shape, jnp.int32),
            pltpu.SemaphoreType.DMA((CLASSES + 5,)),
        ],
        block_count, cloudy_order, bin_state, courant_x, courant_y, gain_kernel, loss_rate,
        scalars=1, direct=6,
    )
    before, after = exchange("gy", high, low)
    *matrices, moves = prepare(gain, loss)
    around, to_right, to_left = call(
        widen_kernel,
        [((1, *tile), F32), ((HALO + 1, *tile), BF16), ((HALO + 1, *tile), BF16)],
        [],
        rows, before, after,
    )
    from_left, from_right = exchange("gx", to_right, to_left)
    inner = rows_x - HALO
    (middle,) = call(
        inner_kernel,
        [((inner, *tile), F32)],
        [(inner, *tile), (4, *tile), (inner, 8, LANES)],
        rows, around, moves, *matrices,
        flops=5 * 10**9,
    )
    total = rows_x + HALO + 1
    (out,) = call(
        outer_kernel,
        [(bin_state.shape, F32)],
        [
            (HALO + 1, *tile),
            (HALO + 1, *tile),
            (total, *tile),
            (total, *tile),
            (4, *tile),
            (total, 8, LANES),
            (total, *tile),
        ],
        rows, edges, before, after, around, from_left, from_right, middle, moves, *matrices,
        flops=20 * 10**9,
    )
    return out


def solution(mesh):
    placed = (
        P(None, "gx", "gy"),
        P("gx", "gy"),
        P("gx", "gy"),
        P("gx", "gy", None),
        P("gy", "gx"),
        P(),
        P(),
    )
    sharded = jax.shard_map(
        per_device, mesh=mesh, in_specs=placed, out_specs=P(None, "gx", "gy"), check_vma=False
    )

    def run(*arguments):
        with jax.sharding.use_abstract_mesh(mesh.abstract_mesh):
            return sharded(*arguments)

    return run
```

```python
import functools
import jax
import jax.numpy as jnp
from jax import lax
from jax.experimental import pallas as pl
from jax.experimental.pallas import tpu as pltpu
from jax.sharding import PartitionSpec as P

BINS = 33
CLASSES = 4
LEV = 4
STEPS = 2
LANES = 128
SUBLANES = 8
OFF = (0, 40, 80, 128)
ROWS = 176
PAD = 40
HEAD = 32
LOOK = 14
HALO = 2 * STEPS
GROUP = HALO * LEV
AUX = BINS
FLAG = AUX + 4
EDGE = 2 * LANES - GROUP
DENSE = (0, BINS + 5, 2 * BINS + 5, 3 * BINS + 5)
SENT = DENSE[3] + PAD
REACH = HALO // 2
CORNER = REACH * GROUP
CHUNKS = tuple((OFF[member], OFF[member] + PAD) for member in range(CLASSES))
VMEM_LIMIT = 24 << 20

GROUPS = (
    (1, 0, ((0, 0, False), (1, 1, False))),
    (1, 1, ((4, 1, False),)),
    (2, 0, ((2, 2, False),)),
    (3, 3, ((3, 0, True), (6, 1, True), (8, 2, True), (9, 3, False))),
    (3, 2, ((5, 1, True), (7, 2, False))),
)
PAIRS = ((0, 0), (0, 1), (0, 2), (0, 3), (1, 1), (1, 2), (1, 3), (2, 2), (2, 3), (3, 3))
NG = len(GROUPS)
F32 = jnp.float32
BF16 = jnp.bfloat16


def prepare_kernel(gain, loss, blocks, tails, losses, moves, wide, turned, upper, last_rows):
    lane = lax.broadcasted_iota(jnp.int32, (PAD, LANES), 1)
    tiles = wide.shape[2] // LANES
    turned[...] = jnp.zeros_like(turned)
    slot_of = {}
    for _, _, members in GROUPS:
        for pair, _, second in members:
            if second:
                slot_of[pair] = len(slot_of)
    for pair in range(len(PAIRS)):
        wide[pair] = jnp.zeros((PAD, tiles * LANES), F32)
        wide[pair, :BINS, : BINS * BINS] = gain[pair].astype(F32)
        if pair in slot_of:
            for tile in range(tiles):
                part = wide[pair, :, tile * LANES : (tile + 1) * LANES]
                part = jnp.concatenate([part, jnp.zeros((LANES - PAD, LANES), F32)], axis=0)
                turned[slot_of[pair], tile * LANES : (tile + 1) * LANES, :] = part.T
    last_rows[...] = jnp.zeros_like(last_rows)
    for group, (_, _, members) in enumerate(GROUPS):
        for factor in range(BINS):
            halves = [jnp.zeros((PAD, LANES), F32), jnp.zeros((PAD, LANES), F32)]
            second_members = [m for m in members if m[2]]
            if second_members:
                rows = []
                for other in range(CLASSES - 1):
                    found = [m for m in second_members if m[1] == other]
                    if found:
                        piece = turned[slot_of[found[0][0]], pl.ds(factor, PAD, stride=BINS), :]
                        rows.append(piece)
                    else:
                        rows.append(jnp.zeros((PAD, LANES), F32))
                rows.append(jnp.zeros((LANES - 3 * PAD, LANES), F32))
                halves[0] = jnp.concatenate(rows, axis=0).T[:PAD]
            for pair, other, second in members:
                if second:
                    continue
                start = BINS * factor
                tile, inside = divmod(start, LANES)
                half, at = divmod(OFF[other], LANES)
                shift = (at - inside) % LANES
                first = wide[pair, :, tile * LANES : (tile + 1) * LANES]
                first = pltpu.roll(first, shift, 1) if shift else first
                if inside + BINS > LANES:
                    rest = wide[pair, :, (tile + 1) * LANES : (tile + 2) * LANES]
                    rest = pltpu.roll(rest, shift, 1) if shift else rest
                    first = jnp.where(lane < at + LANES - inside, first, rest)
                halves[half] = jnp.where((lane >= at) & (lane < at + BINS), first, halves[half])
            full = jnp.concatenate(halves, axis=1)
            blocks[group, factor * HEAD : (factor + 1) * HEAD, :] = full[:HEAD].astype(BF16)
            last_rows[group * PAD + factor : group * PAD + factor + 1, :] = full[HEAD : HEAD + 1]
    tails[...] = last_rows[...].astype(BF16)
    upper[...] = jnp.zeros_like(upper)
    for pair, (first, second) in enumerate(PAIRS):
        half, at = divmod(OFF[second], LANES)
        rates = jnp.concatenate(
            [loss[pair].astype(F32), jnp.zeros((BINS, LANES - BINS), F32)], axis=1
        )
        rates = pltpu.roll(rates, at, 1) if at else rates
        rows = slice(OFF[first], OFF[first] + BINS)
        span = slice(half * LANES, (half + 1) * LANES)
        upper[rows, span] = upper[rows, span] + rates
    whole = upper[...]
    losses[...] = (whole + whole.T)[: losses.shape[0]].astype(BF16)
    fill_moves(moves)


def fill_moves(moves):
    moves[...] = jnp.zeros_like(moves)
    for part, step in enumerate((LEV, 2 * LEV)):
        source = lax.broadcasted_iota(jnp.int32, (LANES, LANES), 0)
        target = lax.broadcasted_iota(jnp.int32, (LANES, LANES), 1)
        moves[part, :LANES, :LANES] = jnp.where(source == target - step, 1.0, 0.0).astype(BF16)
        moves[part, :LANES, LANES:] = jnp.where(source == target + step, 1.0, 0.0).astype(BF16)
        source, target = source[:GROUP], target[:GROUP]
        half = GROUP // 2
        low = (target < step) & (source == target + half - step)
        high = (target >= LANES - step) & (source == target - (LANES - step) + half)
        rows = slice(EDGE, EDGE + GROUP)
        moves[part, rows, :LANES] = jnp.where(low, 1.0, 0.0).astype(BF16)
        moves[part, rows, LANES:] = jnp.where(high, 1.0, 0.0).astype(BF16)


def prepare(gain_kernel, loss_rate):
    wide = -(-BINS * BINS // LANES) * LANES
    tail = -(-NG * PAD // 16) * 16
    rows = -(-ROWS // 16) * 16
    return pl.pallas_call(
        prepare_kernel,
        out_shape=(
            jax.ShapeDtypeStruct((NG, BINS * HEAD, 2 * LANES), BF16),
            jax.ShapeDtypeStruct((tail, 2 * LANES), BF16),
            jax.ShapeDtypeStruct((rows, 2 * LANES), BF16),
            jax.ShapeDtypeStruct((2, EDGE + LANES, 2 * LANES), BF16),
        ),
        scratch_shapes=[
            pltpu.VMEM((len(PAIRS), PAD, wide), F32),
            pltpu.VMEM((4, BINS * PAD + BINS, LANES), F32),
            pltpu.VMEM((2 * LANES, 2 * LANES), F32),
            pltpu.VMEM((tail, 2 * LANES), F32),
        ],
        compiler_params=pltpu.CompilerParams(vmem_limit_bytes=VMEM_LIMIT),
        cost_estimate=pl.CostEstimate(flops=2 * 10**9, bytes_accessed=4 << 20, transcendentals=0),
    )(gain_kernel, loss_rate)


def collide_tiles(bins, row0, blocks, tails, losses, slots, ends, sinks, emit):
    for unit in range(2):
        right = jnp.concatenate([bins[row0 + 2 * unit], bins[row0 + 2 * unit + 1]], axis=1)
        right = jnp.concatenate(
            [right, jnp.zeros((2 * LANES - ROWS, 2 * LANES), F32)], axis=0
        ).astype(BF16)
        pltpu.matmul_push_rhs(right, 0, unit)
    for unit in range(2):
        pltpu.matmul_acc_lhs(ends[unit], tails[...], 0)
    for unit in range(2):
        pltpu.matmul_acc_lhs(sinks[unit], losses[...])
    depth = len(slots[0])
    pending, count = [], 0
    parts = {t: [[jnp.zeros((HEAD, LANES), F32) for _ in range(2)] for _ in range(2)] for t in (1, 2, 3)}

    def drain():
        target, source, factor, slot = pending.pop(0)
        for unit in range(2):
            block = pltpu.matmul_pop(slots[unit][slot])
            for half in range(2):
                scale = bins[row0 + 2 * unit + half, pl.ds(OFF[source] + factor, 1), :]
                part = block[:, half * LANES : (half + 1) * LANES]
                parts[target][unit][half] = parts[target][unit][half] + part * scale

    last = [[[jnp.zeros((PAD, LANES), F32) for _ in range(2)] for _ in range(2)] for _ in range(4)]
    for unit in range(2):
        block = pltpu.matmul_pop(ends[unit])
        for group, (target, source, _) in enumerate(GROUPS):
            for half in range(2):
                scale = bins[row0 + 2 * unit + half, OFF[source] : OFF[source] + PAD, :]
                piece = block[group * PAD : (group + 1) * PAD, half * LANES : (half + 1) * LANES]
                last[target][unit][half] = last[target][unit][half] + piece * scale
    drop = [pltpu.matmul_pop(sinks[unit]) for unit in range(2)]
    for unit in range(2):
        for half in range(2):
            row = row0 + 2 * unit + half
            for member in range(CLASSES):
                rows = slice(OFF[member], OFF[member] + PAD)
                lost = drop[unit][rows, half * LANES : (half + 1) * LANES] * bins[row, rows, :]
                if member:
                    bottom = jnp.sum(last[member][unit][half], axis=0, keepdims=True)
                    bottom = jnp.concatenate([bottom, jnp.zeros((PAD - HEAD - 1, LANES), F32)], axis=0)
                    base = jnp.concatenate([-lost[:HEAD], bottom - lost[HEAD:]], axis=0)
                else:
                    base = -lost
                emit(2 * unit + half, member, None, base)
    for target in (1, 2, 3):
        order = [
            (group, source, factor)
            for factor in range(BINS)
            for group, (aim, source, _) in enumerate(GROUPS)
            if aim == target
        ]
        for group, source, factor in order:
            slot = count % depth
            count += 1
            left = blocks[group, factor * HEAD : (factor + 1) * HEAD, :]
            for unit in range(2):
                pltpu.matmul_acc_lhs(slots[unit][slot], left)
            pending.append((target, source, factor, slot))
            if len(pending) > LOOK:
                drain()
        while pending:
            drain()
        for unit in range(2):
            for half in range(2):
                emit(2 * unit + half, target, parts[target][unit][half], None)


def accumulators(depth, tail, rows):
    return (
        [pltpu.ACC(unit)((HEAD, 2 * LANES), F32) for unit in range(2) for _ in range(depth)]
        + [pltpu.ACC(unit)((tail, 2 * LANES), F32) for unit in range(2)]
        + [pltpu.ACC(unit)((rows, 2 * LANES), F32) for unit in range(2)]
    )


def settle(field, mask, change, row, place):
    def emit(index, member, gained, base):
        at = row(index)
        start = OFF[member]
        if base is not None and member:
            change[place(index), start : start + PAD, :] = base
            return
        if member:
            base = change[place(index), start : start + PAD, :]
            base = jnp.concatenate([base[:HEAD] + gained, base[HEAD:]], axis=0)
        part = jnp.where(mask[at, :1, :] > 0.5, base.astype(BF16).astype(F32), 0.0)
        span = slice(start, start + PAD)
        field[at, span, :] = field[at, span, :] + part

    return emit


def four_rows(bins, row0, matrices, refs, field, mask, change):
    depth = LOOK + 2
    slots = (refs[:depth], refs[depth : 2 * depth])
    ends, sinks = refs[2 * depth : 2 * depth + 2], refs[2 * depth + 2 :]
    emit = settle(field, mask, change, lambda index: row0 + index, lambda index: index)
    collide_tiles(bins, row0, *matrices, slots, ends, sinks, emit)


def one_row(bins, row, matrices, refs, field, mask, change):
    blocks, tails, losses = matrices
    depth = LOOK + 2
    slots = (refs[:depth], refs[depth : 2 * depth])
    end, sink = refs[2 * depth], refs[2 * depth + 3]
    right = bins[row]
    right = jnp.concatenate([right, jnp.zeros((2 * LANES - ROWS, LANES), F32)], axis=0)
    right = jnp.concatenate([right, jnp.zeros((2 * LANES, LANES), F32)], axis=1).astype(BF16)
    for unit in range(2):
        pltpu.matmul_push_rhs(right, 0, unit)
    pltpu.matmul_acc_lhs(end, tails[...], 0)
    pltpu.matmul_acc_lhs(sink, losses[...], 0)
    emit = settle(field, mask, change, lambda index: row, lambda index: 0)
    block = pltpu.matmul_pop(end)[:, :LANES]
    last = [jnp.zeros((PAD, LANES), F32) for _ in range(CLASSES)]
    for group, (target, source, _) in enumerate(GROUPS):
        scale = bins[row, OFF[source] : OFF[source] + PAD, :]
        last[target] = last[target] + block[group * PAD : (group + 1) * PAD] * scale
    drop = pltpu.matmul_pop(sink)[:, :LANES]
    for member in range(CLASSES):
        span = slice(OFF[member], OFF[member] + PAD)
        base = -drop[span] * bins[row, span, :]
        if member:
            bottom = jnp.sum(last[member], axis=0, keepdims=True)
            bottom = jnp.concatenate([bottom, jnp.zeros((PAD - HEAD - 1, LANES), F32)], axis=0)
            base = jnp.concatenate([base[:HEAD], bottom + base[HEAD:]], axis=0)
        emit(0, member, None, base)
    parts = {t: [jnp.zeros((HEAD, LANES), F32) for _ in range(2)] for t in (1, 2, 3)}
    pending, count = [], 0

    def drain():
        target, source, factor, unit, slot = pending.pop(0)
        part = pltpu.matmul_pop(slots[unit][slot])[:, :LANES]
        scale = bins[row, OFF[source] + factor : OFF[source] + factor + 1, :]
        parts[target][unit] = parts[target][unit] + part * scale

    for target in (1, 2, 3):
        order = [
            (group, source, factor)
            for factor in range(BINS)
            for group, (aim, source, _) in enumerate(GROUPS)
            if aim == target
        ]
        for group, source, factor in order:
            unit, slot = count % 2, (count // 2) % len(slots[0])
            count += 1
            left = blocks[group, factor * HEAD : (factor + 1) * HEAD, :]
            pltpu.matmul_acc_lhs(slots[unit][slot], left)
            pending.append((target, source, factor, unit, slot))
            if len(pending) > 2 * LOOK:
                drain()
        while pending:
            drain()
        emit(0, target, parts[target][0] + parts[target][1], None)


def weights(tile, row):
    out, centre = [], 1.0
    for axis in range(2):
        first, second = (
            jnp.broadcast_to(tile[row, pl.ds(AUX + 2 * axis + part, 1), :], (SUBLANES, LANES))
            for part in range(2)
        )
        speed = (first + second) * (1.0 / 6.0)
        rising, falling = jnp.maximum(speed, 0.0), jnp.minimum(speed, 0.0)
        centre = centre - 3.0 * (rising - falling)
        out.append(
            (
                6.0 * rising + 2.0 * falling,
                -rising,
                -2.0 * rising - 6.0 * falling,
                falling,
            )
        )
    return centre, out


def cells(value):
    return value.reshape(value.shape[0] // SUBLANES, SUBLANES, LANES)


def advance(centre, along_x, along_y, coefficients):
    middle, (for_x, for_y) = coefficients
    total = middle * centre
    for values, factors in ((along_x, for_x), (along_y, for_y)):
        for value, factor in zip(values, factors):
            total = total + factor * value
    return jnp.maximum(total, 0.0)


def shifted(value, amount):
    amount = amount % LANES
    return pltpu.roll(value, amount, value.ndim - 1) if amount else value


def travel(jobs, moves, refs, finish):
    def issue(number, job):
        row, outside, place = job
        left = jnp.concatenate([row().astype(BF16), outside().astype(BF16)], axis=1)
        for unit in range(2):
            start = EDGE - GROUP * place
            right = [moves[unit, :LANES, :], moves[unit, start : start + LANES, :]]
            pltpu.matmul_push_rhs(jnp.concatenate(right, axis=0), number % 2, unit)
            pltpu.matmul_acc_lhs(refs[2 * (number % 2) + unit], left, number % 2)

    for number in range(len(jobs) + 1):
        if number < len(jobs):
            issue(number, jobs[number])
        if number:
            one, two = (pltpu.matmul_pop(refs[2 * ((number - 1) % 2) + unit]) for unit in range(2))
            finish(number - 1, (one[:, :LANES], two[:, :LANES], one[:, LANES:], two[:, LANES:]))


def travellers():
    return [pltpu.ACC(unit)((ROWS, 2 * LANES), F32) for _ in range(2) for unit in range(2)]


def lanes():
    return lax.broadcasted_iota(jnp.int32, (SUBLANES, LANES), 1)


def put(field, bins, row, span, value):
    value = value.reshape(PAD, LANES)
    field[row, span, :] = value
    bins[row, span, :] = value.astype(BF16).astype(F32)


def clear_gap(*arrays):
    for start, stop in ((OFF[2] + PAD, OFF[3]), (OFF[3] + PAD, ROWS)):
        for array in arrays:
            for row in range(array.shape[0]):
                array[row, start:stop, :] = jnp.zeros((stop - start, LANES), F32)


def stage_kernel(
    count, order_hbm, state_hbm, courant_x_hbm, courant_y_hbm, gain_hbm, loss_hbm,
    rows, edges, low, high, gain, loss, state, courant_x, courant_y, order, arrived,
):
    rows_x = state.shape[1]
    flat = state.reshape(state.shape[0] * rows_x, LANES)
    pieces = [
        (state_hbm.at[pl.ds(member * BINS, BINS)], state.at[pl.ds(member * BINS, BINS)])
        for member in range(CLASSES)
    ]
    pieces += [(courant_x_hbm, courant_x), (courant_y_hbm, courant_y)]
    pieces += [(order_hbm, order)]
    pieces += [(gain_hbm, gain), (loss_hbm, loss)]
    copies = [
        pltpu.make_async_copy(source, target, arrived.at[number])
        for number, (source, target) in enumerate(pieces)
    ]
    for copy in copies:
        copy.start()
    for copy in copies[:-2]:
        copy.wait()
    spare = jnp.zeros((PAD - BINS, LANES), F32)
    for row in range(rows_x):
        cloudy = jnp.int32(0)
        for place in range(rows_x):
            hit = (order[0, 0, place] == row) & (place < count[0, 0])
            cloudy = cloudy | hit.astype(jnp.int32)
        for member in range(CLASSES):
            part = flat[pl.ds(member * BINS * rows_x + row, BINS, stride=rows_x), :]
            rows[row, OFF[member] : OFF[member] + BINS, :] = part
            rows[row, OFF[member] + BINS : OFF[member] + PAD, :] = spare
        for axis, courant in enumerate((courant_x, courant_y)):
            speed = courant[row : row + 1, :]
            upper = speed.astype(BF16).astype(F32)
            rows[row, AUX + 2 * axis : AUX + 2 * axis + 1, :] = upper
            rows[row, AUX + 2 * axis + 1 : AUX + 2 * axis + 2, :] = speed - upper
        rows[row, FLAG : FLAG + 1, :] = jnp.full((1, LANES), cloudy.astype(F32), F32)
    clear_gap(rows, edges)
    owner = lanes() // GROUP
    for start, stop in CHUNKS:
        left = jnp.zeros((PAD // SUBLANES, SUBLANES, LANES), F32)
        right = left
        for row in range(rows_x):
            value = cells(rows[row, start:stop, :])
            left = jnp.where(owner == row, shifted(value, GROUP * row), left)
            right = jnp.where(owner == row, shifted(value, GROUP * (row + 1)), right)
        edges[0, start:stop, :] = left.reshape(PAD, LANES)
        edges[1, start:stop, :] = right.reshape(PAD, LANES)
    low[...] = edges[0].astype(BF16)
    high[...] = edges[1].astype(BF16)
    for copy in copies[-2:]:
        copy.wait()


def pack_kernel(rows, packed, dense):
    for row in range(rows.shape[0]):
        for (start, stop), first in zip(CHUNKS, DENSE):
            dense[row, first : first + PAD, :] = rows[row, start:stop, :]
        packed[row] = dense[row].astype(BF16)


def widen_kernel(packed, before, after, around, to_right, to_left):
    rows_x = packed.shape[0]
    inner = lanes() % GROUP < GROUP // 2
    block = lanes() // CORNER
    corners = [None, None]
    for member, (start, stop) in enumerate(CHUNKS):
        near = jnp.where(
            inner,
            shifted(cells(before[start:stop].astype(F32)), -GROUP // 2),
            shifted(cells(after[start:stop].astype(F32)), GROUP // 2),
        )
        around[0, start:stop, :] = near.reshape(PAD, LANES)
        for side, first in enumerate((LANES - CORNER, 0)):
            moved = shifted(near, CORNER * member - first)
            old = corners[side]
            corners[side] = moved if old is None else jnp.where(block == member, moved, old)
    clear_gap(around)
    for index in range(HALO):
        span = slice(index * SENT, (index + 1) * SENT)
        to_right[span, :] = packed[rows_x - HALO + index]
        to_left[span, :] = packed[index]
    for target, corner in zip((to_right, to_left), corners):
        target[HALO * SENT :, :] = corner.reshape(PAD, LANES).astype(BF16)


def unpack(sent, tiles, dense, first_lane):
    for index in range(HALO):
        dense[index] = sent[index * SENT : (index + 1) * SENT, :].astype(F32)
        for (start, stop), first in zip(CHUNKS, DENSE):
            tiles[index, start:stop, :] = dense[index, first : first + PAD, :]
    corner = cells(sent[HALO * SENT :, :].astype(F32))
    for member, (start, stop) in enumerate(CHUNKS):
        moved = shifted(corner, first_lane - CORNER * member)
        tiles[HALO, start:stop, :] = moved.reshape(PAD, LANES)


def inner_kernel(rows, around, moves, blocks, tails, losses, out, bins, change, mask):
    rows_x = rows.shape[0]
    clear_gap(out, bins)
    places = [index + HALO // 2 for index in range(rows_x - HALO)]

    def finish(index, along_y):
        row = places[index]
        coefficients = weights(rows, row)
        mask[index] = jnp.broadcast_to(rows[row, FLAG : FLAG + 1, :], mask.shape[1:])
        for start, stop in CHUNKS:
            span = slice(start, stop)
            centre = cells(rows[row, span, :])
            along_x = [cells(rows[row + d, span, :]) for d in (-1, -2, 1, 2)]
            beside = [cells(value[span]) for value in along_y]
            put(out, bins, index, span, advance(centre, along_x, beside, coefficients))

    jobs = [(lambda row=row: rows[row], lambda: around[0], row) for row in places]
    pl.run_scoped(lambda *refs: travel(jobs, moves, refs, finish), *travellers())
    matrices = (blocks, tails, losses)
    pl.run_scoped(
        lambda *refs: four_rows(bins, 0, matrices, refs, out, mask, change),
        *accumulators(LOOK + 2, tails.shape[0], losses.shape[0]),
    )


def outer_kernel(
    rows, edges, before, after, around, from_left, from_right, middle, moves, blocks, tails, losses,
    out_hbm, left, right, field, bins, change, mask, second, dense, out, sent,
):
    rows_x = rows.shape[0]
    lane = lanes()
    outside = rows_x + HALO
    unpack(from_left, left, dense, LANES - CORNER)
    unpack(from_right, right, dense, 0)
    clear_gap(field, bins, second, left, right)

    def column(x):
        if x < 0:
            return left, x + HALO
        if x >= rows_x:
            return right, x - rows_x
        return rows, x

    def outer_columns(x):
        if x < 0:
            return (lambda: left[HALO]), x + rows_x
        if x >= rows_x:
            return (lambda: right[HALO]), x - rows_x
        return (lambda: around[0]), x

    reach = HALO // 2
    places = list(range(-reach, reach)) + list(range(rows_x - reach, rows_x + reach))

    def job(x):
        tile, row = column(x)
        return (lambda: tile[row], *outer_columns(x))

    def first_step(index, beside):
        x = places[index]
        tile, row = column(x)
        coefficients = weights(tile, row)
        mask[x + reach] = jnp.broadcast_to(tile[row, FLAG : FLAG + 1, :], mask.shape[1:])
        for start, stop in CHUNKS:
            span = slice(start, stop)
            centre = cells(tile[row, span, :])
            along_x = []
            for d in (-1, -2, 1, 2):
                other, at = column(x + d)
                along_x.append(cells(other[at, span, :]))
            along_y = [cells(value[span]) for value in beside]
            put(field, bins, x + reach, span, advance(centre, along_x, along_y, coefficients))

    jobs = [job(x) for x in places]
    pl.run_scoped(lambda *refs: travel(jobs, moves, refs, first_step), *travellers())
    coefficients = weights(around, 0)
    mask[outside] = jnp.broadcast_to(around[0, FLAG : FLAG + 1, :], mask.shape[1:])
    inside = lane % GROUP
    half = GROUP // 2
    for start, stop in CHUNKS:
        span = slice(start, stop)
        lower, upper = cells(before[span, :].astype(F32)), cells(after[span, :].astype(F32))
        first, last = cells(edges[0, span, :]), cells(edges[1, span, :])
        centre = cells(around[0, span, :])
        along_y = (
            jnp.where(
                inside < half + LEV,
                shifted(jnp.where(inside < half + LEV, lower, last), -LEV),
                shifted(upper, half + LEV),
            ),
            jnp.where(inside < half, lower, last),
            jnp.where(
                inside < LEV,
                shifted(lower, -half - LEV),
                shifted(jnp.where(inside < LEV, first, upper), LEV),
            ),
            jnp.where(inside < half, first, upper),
        )
        beyond = jnp.where(
            lane >= LANES // 2, cells(left[HALO, span, :]), cells(right[HALO, span, :])
        )
        along_x = (
            shifted(jnp.where(lane >= LANES - GROUP, beyond, centre), GROUP),
            shifted(jnp.where(lane >= LANES - 2 * GROUP, beyond, centre), 2 * GROUP),
            shifted(jnp.where(lane < GROUP, beyond, centre), -GROUP),
            shifted(jnp.where(lane < 2 * GROUP, beyond, centre), -2 * GROUP),
        )
        put(field, bins, outside, span, advance(centre, along_x, along_y, coefficients))
    for index in range(rows_x - HALO):
        field[index + HALO] = middle[index]
        row = index + reach
        mask[index + HALO] = jnp.broadcast_to(rows[row, FLAG : FLAG + 1, :], mask.shape[1:])
    matrices = (blocks, tails, losses)

    def first_collisions(*refs):
        one_row(bins, outside, matrices, refs, field, mask, change)

        @pl.loop(0, 2)
        def _(step):
            four_rows(bins, rows_x * step, matrices, refs, field, mask, change)

    def second_step(x, beside):
        coefficients = weights(rows, x)
        for start, stop in CHUNKS:
            span = slice(start, stop)
            centre = cells(field[x + reach, span, :])
            along_x = [cells(field[x + reach + d, span, :]) for d in (-1, -2, 1, 2)]
            along_y = [cells(value[span]) for value in beside]
            put(second, bins, x + reach, span, advance(centre, along_x, along_y, coefficients))

    def second_collisions(*refs):
        @pl.loop(0, rows_x // 4)
        def _(step):
            four_rows(bins, reach + 4 * step, matrices, refs, second, mask, change)

    shapes = accumulators(LOOK + 2, tails.shape[0], losses.shape[0])
    pl.run_scoped(first_collisions, *shapes)
    later = [(lambda x=x: field[x + reach], lambda: field[outside], x) for x in range(rows_x)]
    pl.run_scoped(lambda *refs: travel(later, moves, refs, second_step), *travellers())
    pl.run_scoped(second_collisions, *shapes)
    flat = out.reshape(out.shape[0] * rows_x, LANES)
    copies = []
    for member in range(CLASSES):
        for x in range(rows_x):
            span = pl.ds(member * BINS * rows_x + x, BINS, stride=rows_x)
            flat[span, :] = second[x + reach, OFF[member] : OFF[member] + BINS, :]
        part = pl.ds(member * BINS, BINS)
        copies.append(pltpu.make_async_copy(out.at[part], out_hbm.at[part], sent.at[member]))
        copies[-1].start()
    for copy in copies:
        copy.wait()


def call(kernel, outs, scratch, *arguments, scalars=0, direct=0, flops=0, stored=False):
    smem = pl.BlockSpec(memory_space=pltpu.SMEM)
    vmem = pl.BlockSpec(memory_space=pltpu.VMEM)
    hbm = pl.BlockSpec(memory_space=pltpu.HBM)
    shapes = tuple(jax.ShapeDtypeStruct(shape, dtype) for shape, dtype in outs)
    moved = sum(a.size * a.dtype.itemsize for a in arguments)
    own = [pltpu.VMEM(piece, F32) if isinstance(piece, tuple) else piece for piece in scratch]
    staged = scalars + direct
    held = [pltpu.with_memory_space_constraint(a, pltpu.HBM) for a in arguments[scalars:staged]]
    return pl.pallas_call(
        kernel,
        out_shape=shapes,
        in_specs=[smem] * scalars + [hbm] * direct + [vmem] * (len(arguments) - staged),
        out_specs=tuple(hbm if stored else vmem for _ in shapes),
        scratch_shapes=own,
        compiler_params=pltpu.CompilerParams(vmem_limit_bytes=VMEM_LIMIT),
        cost_estimate=pl.CostEstimate(flops=flops, bytes_accessed=moved, transcendentals=0),
    )(*arguments[:scalars], *held, *arguments[staged:])


def exchange(axis, upward, downward):
    size = lax.axis_size(axis)
    up = [(i, (i + 1) % size) for i in range(size)]
    down = [(j, i) for i, j in up]
    return lax.ppermute(upward, axis, up), lax.ppermute(downward, axis, down)


def per_device(bin_state, courant_x, courant_y, cloudy_order, block_count, gain_kernel, loss_rate):
    rows_x = bin_state.shape[1]
    tile = (ROWS, LANES)
    rows, edges, low, high, gain, loss = call(
        stage_kernel,
        [
            ((rows_x, *tile), F32),
            ((2, *tile), F32),
            (tile, BF16),
            (tile, BF16),
            (gain_kernel.shape, BF16),
            (loss_rate.shape, BF16),
        ],
        [
            bin_state.shape,
            courant_x.shape,
            courant_y.shape,
            pltpu.SMEM(cloudy_order.shape, jnp.int32),
            pltpu.SemaphoreType.DMA((CLASSES + 5,)),
        ],
        block_count, cloudy_order, bin_state, courant_x, courant_y, gain_kernel, loss_rate,
        scalars=1, direct=6,
    )
    before, after = exchange("gy", high, low)
    *matrices, moves = prepare(gain, loss)
    (packed,) = call(
        pack_kernel,
        [((rows_x, SENT, LANES), BF16)],
        [(rows_x, SENT, LANES)],
        rows,
    )
    message = ((HALO * SENT + PAD, LANES), BF16)
    around, to_right, to_left = call(
        widen_kernel,
        [((1, *tile), F32), message, message],
        [],
        packed, before, after,
    )
    from_left, from_right = exchange("gx", to_right, to_left)
    inner = rows_x - HALO
    (middle,) = call(
        inner_kernel,
        [((inner, *tile), F32)],
        [(inner, *tile), (4, *tile), (inner, 8, LANES)],
        rows, around, moves, *matrices,
        flops=5 * 10**9,
    )
    total = rows_x + HALO + 1
    (out,) = call(
        outer_kernel,
        [(bin_state.shape, F32)],
        [
            (HALO + 1, *tile),
            (HALO + 1, *tile),
            (total, *tile),
            (total, *tile),
            (4, *tile),
            (total, 8, LANES),
            (total, *tile),
            (HALO, SENT, LANES),
            bin_state.shape,
            pltpu.SemaphoreType.DMA((CLASSES,)),
        ],
        rows, edges, before, after, around, from_left, from_right, middle, moves, *matrices,
        flops=20 * 10**9,
        stored=True,
    )
    return out


def solution(mesh):
    placed = (
        P(None, "gx", "gy"),
        P("gx", "gy"),
        P("gx", "gy"),
        P("gx", "gy", None),
        P("gy", "gx"),
        P(),
        P(),
    )
    sharded = jax.shard_map(
        per_device, mesh=mesh, in_specs=placed, out_specs=P(None, "gx", "gy"), check_vma=False
    )

    def run(*arguments):
        with jax.sharding.use_abstract_mesh(mesh.abstract_mesh):
            return sharded(*arguments)

    return run
```

```python
import functools
import jax
import jax.numpy as jnp
from jax import lax
from jax.experimental import pallas as pl
from jax.experimental.pallas import tpu as pltpu
from jax.sharding import PartitionSpec as P

BINS = 33
CLASSES = 4
LEV = 4
STEPS = 2
LANES = 128
SUBLANES = 8
OFF = (0, 40, 80, 128)
ROWS = 176
PAD = 40
HEAD = 32
LOOK = 14
HALO = 2 * STEPS
GROUP = HALO * LEV
AUX = BINS
FLAG = AUX + 4
EDGE = 2 * LANES - GROUP
DENSE = (0, BINS + 5, 2 * BINS + 5, 3 * BINS + 5)
SENT = DENSE[3] + PAD
REACH = HALO // 2
CORNER = REACH * GROUP
CHUNKS = tuple((OFF[member], OFF[member] + PAD) for member in range(CLASSES))
VMEM_LIMIT = 24 << 20

GROUPS = (
    (1, 0, ((0, 0, False), (1, 1, False))),
    (1, 1, ((4, 1, False),)),
    (2, 0, ((2, 2, False),)),
    (3, 3, ((3, 0, True), (6, 1, True), (8, 2, True), (9, 3, False))),
    (3, 2, ((5, 1, True), (7, 2, False))),
)
PAIRS = ((0, 0), (0, 1), (0, 2), (0, 3), (1, 1), (1, 2), (1, 3), (2, 2), (2, 3), (3, 3))
NG = len(GROUPS)
F32 = jnp.float32
BF16 = jnp.bfloat16
F8 = jnp.float8_e4m3fn
FINE = ((0, 80, 40, False), (1, 0, 40, False), (2, 0, -80, True), (4, -40, -80, True))
GAIN_SCALE = 4096.0
PEAK = 256.0
LOOK8 = 18
TOGETHER = 3


def prepare_kernel(gain, loss, blocks, tails, losses, moves, wide, turned, upper, last_rows):
    lane = lax.broadcasted_iota(jnp.int32, (PAD, LANES), 1)
    tiles = wide.shape[2] // LANES
    turned[...] = jnp.zeros_like(turned)
    slot_of = {}
    for _, _, members in GROUPS:
        for pair, _, second in members:
            if second:
                slot_of[pair] = len(slot_of)
    for pair in range(len(PAIRS)):
        wide[pair] = jnp.zeros((PAD, tiles * LANES), F32)
        wide[pair, :BINS, : BINS * BINS] = gain[pair].astype(F32)
        if pair in slot_of:
            for tile in range(tiles):
                part = wide[pair, :, tile * LANES : (tile + 1) * LANES]
                part = jnp.concatenate([part, jnp.zeros((LANES - PAD, LANES), F32)], axis=0)
                turned[slot_of[pair], tile * LANES : (tile + 1) * LANES, :] = part.T
    last_rows[...] = jnp.zeros_like(last_rows)
    for group, (_, _, members) in enumerate(GROUPS):
        for factor in range(BINS):
            halves = [jnp.zeros((PAD, LANES), F32), jnp.zeros((PAD, LANES), F32)]
            second_members = [m for m in members if m[2]]
            if second_members:
                rows = []
                for other in range(CLASSES - 1):
                    found = [m for m in second_members if m[1] == other]
                    if found:
                        piece = turned[slot_of[found[0][0]], pl.ds(factor, PAD, stride=BINS), :]
                        rows.append(piece)
                    else:
                        rows.append(jnp.zeros((PAD, LANES), F32))
                rows.append(jnp.zeros((LANES - 3 * PAD, LANES), F32))
                halves[0] = jnp.concatenate(rows, axis=0).T[:PAD]
            for pair, other, second in members:
                if second:
                    continue
                start = BINS * factor
                tile, inside = divmod(start, LANES)
                half, at = divmod(OFF[other], LANES)
                shift = (at - inside) % LANES
                first = wide[pair, :, tile * LANES : (tile + 1) * LANES]
                first = pltpu.roll(first, shift, 1) if shift else first
                if inside + BINS > LANES:
                    rest = wide[pair, :, (tile + 1) * LANES : (tile + 2) * LANES]
                    rest = pltpu.roll(rest, shift, 1) if shift else rest
                    first = jnp.where(lane < at + LANES - inside, first, rest)
                halves[half] = jnp.where((lane >= at) & (lane < at + BINS), first, halves[half])
            full = jnp.concatenate(halves, axis=1)
            blocks[group, factor * HEAD : (factor + 1) * HEAD, :] = full[:HEAD].astype(BF16)
            last_rows[group * PAD + factor : group * PAD + factor + 1, :] = full[HEAD : HEAD + 1]
    tails[...] = last_rows[...].astype(BF16)
    upper[...] = jnp.zeros_like(upper)
    for pair, (first, second) in enumerate(PAIRS):
        half, at = divmod(OFF[second], LANES)
        rates = jnp.concatenate(
            [loss[pair].astype(F32), jnp.zeros((BINS, LANES - BINS), F32)], axis=1
        )
        rates = pltpu.roll(rates, at, 1) if at else rates
        rows = slice(OFF[first], OFF[first] + BINS)
        span = slice(half * LANES, (half + 1) * LANES)
        upper[rows, span] = upper[rows, span] + rates
    whole = upper[...]
    losses[...] = (whole + whole.T)[: losses.shape[0]].astype(BF16)
    fill_moves(moves)


def fill_moves(moves):
    moves[...] = jnp.zeros_like(moves)
    for part, step in enumerate((LEV, 2 * LEV)):
        source = lax.broadcasted_iota(jnp.int32, (LANES, LANES), 0)
        target = lax.broadcasted_iota(jnp.int32, (LANES, LANES), 1)
        moves[part, :LANES, :LANES] = jnp.where(source == target - step, 1.0, 0.0).astype(BF16)
        moves[part, :LANES, LANES:] = jnp.where(source == target + step, 1.0, 0.0).astype(BF16)
        source, target = source[:GROUP], target[:GROUP]
        half = GROUP // 2
        low = (target < step) & (source == target + half - step)
        high = (target >= LANES - step) & (source == target - (LANES - step) + half)
        rows = slice(EDGE, EDGE + GROUP)
        moves[part, rows, :LANES] = jnp.where(low, 1.0, 0.0).astype(BF16)
        moves[part, rows, LANES:] = jnp.where(high, 1.0, 0.0).astype(BF16)


def prepare(gain_kernel, loss_rate):
    wide = -(-BINS * BINS // LANES) * LANES
    tail = -(-NG * PAD // 16) * 16
    rows = -(-ROWS // 16) * 16
    return pl.pallas_call(
        prepare_kernel,
        out_shape=(
            jax.ShapeDtypeStruct((NG, BINS * HEAD, 2 * LANES), BF16),
            jax.ShapeDtypeStruct((tail, 2 * LANES), BF16),
            jax.ShapeDtypeStruct((rows, 2 * LANES), BF16),
            jax.ShapeDtypeStruct((2, EDGE + LANES, 2 * LANES), BF16),
        ),
        scratch_shapes=[
            pltpu.VMEM((len(PAIRS), PAD, wide), F32),
            pltpu.VMEM((4, BINS * PAD + BINS, LANES), F32),
            pltpu.VMEM((2 * LANES, 2 * LANES), F32),
            pltpu.VMEM((tail, 2 * LANES), F32),
        ],
        compiler_params=pltpu.CompilerParams(vmem_limit_bytes=VMEM_LIMIT),
        cost_estimate=pl.CostEstimate(flops=2 * 10**9, bytes_accessed=4 << 20, transcendentals=0),
    )(gain_kernel, loss_rate)


def collide_tiles(bins, row0, blocks, tails, losses, slots, ends, sinks, emit):
    for unit in range(2):
        right = jnp.concatenate([bins[row0 + 2 * unit], bins[row0 + 2 * unit + 1]], axis=1)
        right = jnp.concatenate(
            [right, jnp.zeros((2 * LANES - ROWS, 2 * LANES), F32)], axis=0
        ).astype(BF16)
        pltpu.matmul_push_rhs(right, 0, unit)
    for unit in range(2):
        pltpu.matmul_acc_lhs(ends[unit], tails[...], 0)
    for unit in range(2):
        pltpu.matmul_acc_lhs(sinks[unit], losses[...])
    depth = len(slots[0])
    pending, count = [], 0
    parts = {t: [[jnp.zeros((HEAD, LANES), F32) for _ in range(2)] for _ in range(2)] for t in (1, 2, 3)}

    def drain():
        target, source, factor, slot = pending.pop(0)
        for unit in range(2):
            block = pltpu.matmul_pop(slots[unit][slot])
            for half in range(2):
                scale = bins[row0 + 2 * unit + half, pl.ds(OFF[source] + factor, 1), :]
                part = block[:, half * LANES : (half + 1) * LANES]
                parts[target][unit][half] = parts[target][unit][half] + part * scale

    last = [[[jnp.zeros((PAD, LANES), F32) for _ in range(2)] for _ in range(2)] for _ in range(4)]
    for unit in range(2):
        block = pltpu.matmul_pop(ends[unit])
        for group, (target, source, _) in enumerate(GROUPS):
            for half in range(2):
                scale = bins[row0 + 2 * unit + half, OFF[source] : OFF[source] + PAD, :]
                piece = block[group * PAD : (group + 1) * PAD, half * LANES : (half + 1) * LANES]
                last[target][unit][half] = last[target][unit][half] + piece * scale
    drop = [pltpu.matmul_pop(sinks[unit]) for unit in range(2)]
    for unit in range(2):
        for half in range(2):
            row = row0 + 2 * unit + half
            for member in range(CLASSES):
                rows = slice(OFF[member], OFF[member] + PAD)
                lost = drop[unit][rows, half * LANES : (half + 1) * LANES] * bins[row, rows, :]
                if member:
                    bottom = jnp.sum(last[member][unit][half], axis=0, keepdims=True)
                    bottom = jnp.concatenate([bottom, jnp.zeros((PAD - HEAD - 1, LANES), F32)], axis=0)
                    base = jnp.concatenate([-lost[:HEAD], bottom - lost[HEAD:]], axis=0)
                else:
                    base = -lost
                emit(2 * unit + half, member, None, base)
    for target in (1, 2, 3):
        order = [
            (group, source, factor)
            for factor in range(BINS)
            for group, (aim, source, _) in enumerate(GROUPS)
            if aim == target
        ]
        for group, source, factor in order:
            slot = count % depth
            count += 1
            left = blocks[group, factor * HEAD : (factor + 1) * HEAD, :]
            for unit in range(2):
                pltpu.matmul_acc_lhs(slots[unit][slot], left)
            pending.append((target, source, factor, slot))
            if len(pending) > LOOK:
                drain()
        while pending:
            drain()
        for unit in range(2):
            for half in range(2):
                emit(2 * unit + half, target, parts[target][unit][half], None)


def collide_fine(bins, row0, blocks, tails, losses, fine, scale, slots, ends, sinks, emit):
    for unit in range(2):
        right = jnp.concatenate([bins[row0 + 2 * unit], bins[row0 + 2 * unit + 1]], axis=1)
        right = jnp.concatenate(
            [right, jnp.zeros((2 * LANES - ROWS, 2 * LANES), F32)], axis=0
        ).astype(BF16)
        pltpu.matmul_push_rhs(right, 0, unit)
    for unit in range(2):
        pltpu.matmul_acc_lhs(ends[unit], tails[...], 0)
    for unit in range(2):
        pltpu.matmul_acc_lhs(sinks[unit], losses[...])
    for unit in range(2):
        pltpu.matmul_push_rhs(fine_bins(bins, row0, unit, scale, True), 1, unit)
    last = [[[jnp.zeros((PAD, LANES), F32) for _ in range(2)] for _ in range(2)] for _ in range(4)]
    for unit in range(2):
        block = pltpu.matmul_pop(ends[unit])
        for group, (target, source, _) in enumerate(GROUPS):
            for half in range(2):
                factor = bins[row0 + 2 * unit + half, OFF[source] : OFF[source] + PAD, :]
                piece = block[group * PAD : (group + 1) * PAD, half * LANES : (half + 1) * LANES]
                last[target][unit][half] = last[target][unit][half] + piece * factor
    drop = [pltpu.matmul_pop(sinks[unit]) for unit in range(2)]
    for unit in range(2):
        for half in range(2):
            row = row0 + 2 * unit + half
            for member in range(CLASSES):
                rows = slice(OFF[member], OFF[member] + PAD)
                lost = drop[unit][rows, half * LANES : (half + 1) * LANES] * bins[row, rows, :]
                if member:
                    bottom = jnp.sum(last[member][unit][half], axis=0, keepdims=True)
                    bottom = jnp.concatenate([bottom, jnp.zeros((PAD - HEAD - 1, LANES), F32)], axis=0)
                    base = jnp.concatenate([-lost[:HEAD], bottom - lost[HEAD:]], axis=0)
                else:
                    base = -lost
                emit(2 * unit + half, member, None, base)
    down = 1.0 / (scale * GAIN_SCALE)
    place = {group: index for index, (group, *_) in enumerate(FINE)}
    stages = (
        ((3,), None),
        ((4,), 1),
        ((2,), None),
        ((0, 1), 0),
    )
    depth = len(slots[0])
    sums = [
        [[jnp.zeros((HEAD, LANES), F32) for _ in range(2)] for _ in range(2)] for _ in stages
    ]
    left_over = [BINS * len(groups) for groups, _ in stages]
    pending, count = [], 0

    def drain():
        stage, source, factor, slot = pending.pop(0)
        for unit in range(2):
            block = pltpu.matmul_pop(slots[unit][slot])
            for half in range(2):
                scaled = bins[row0 + 2 * unit + half, pl.ds(OFF[source] + factor, 1), :]
                part = block[:, half * LANES : (half + 1) * LANES]
                sums[stage][unit][half] = sums[stage][unit][half] + part * scaled
        left_over[stage] -= 1
        if left_over[stage] or not stage:
            return
        target = (None, 3, 2, 1)[stage]
        for unit in range(2):
            for half in range(2):
                total = sums[stage][unit][half] * down
                if target == 3:
                    total = total + sums[0][unit][half]
                emit(2 * unit + half, target, total, None)

    for stage, (groups, staged) in enumerate(stages):
        for factor in range(BINS):
            for group in groups:
                slot = count % depth
                count += 1
                rows = slice(factor * HEAD, (factor + 1) * HEAD)
                left = fine[place[group], rows, :] if group in place else blocks[group, rows, :]
                for unit in range(2):
                    pltpu.matmul_acc_lhs(slots[unit][slot], left, staged)
                if staged == 1:
                    for unit in range(2):
                        right = fine_bins(bins, row0, unit, scale, False)
                        pltpu.matmul_push_rhs(right, 0, unit)
                staged = None
                pending.append((stage, GROUPS[group][1], factor, slot))
                if len(pending) > LOOK8:
                    drain()
    while pending:
        drain()


def accumulators(depth, tail, rows):
    return (
        [pltpu.ACC(unit)((HEAD, 2 * LANES), F32) for unit in range(2) for _ in range(depth)]
        + [pltpu.ACC(unit)((tail, 2 * LANES), F32) for unit in range(2)]
        + [pltpu.ACC(unit)((rows, 2 * LANES), F32) for unit in range(2)]
    )


def settle(field, mask, change, row, place):
    def emit(index, member, gained, base):
        at = row(index)
        start = OFF[member]
        if base is not None and member:
            change[place(index), start : start + PAD, :] = base
            return
        if member:
            base = change[place(index), start : start + PAD, :]
            base = jnp.concatenate([base[:HEAD] + gained, base[HEAD:]], axis=0)
        part = jnp.where(mask[at, :1, :] > 0.5, base.astype(BF16).astype(F32), 0.0)
        span = slice(start, start + PAD)
        field[at, span, :] = field[at, span, :] + part

    return emit


def four_rows(bins, row0, matrices, refs, field, mask, change, fine=None, scale=None):
    depth = LOOK + 2 if fine is None else LOOK8 + 2
    slots = (refs[:depth], refs[depth : 2 * depth])
    ends, sinks = refs[2 * depth : 2 * depth + 2], refs[2 * depth + 2 :]
    emit = settle(field, mask, change, lambda index: row0 + index, lambda index: index)
    if fine is None:
        collide_tiles(bins, row0, *matrices, slots, ends, sinks, emit)
    else:
        collide_fine(bins, row0, *matrices, fine, scale, slots, ends, sinks, emit)


def one_row(bins, row, matrices, refs, field, mask, change):
    blocks, tails, losses = matrices
    depth = LOOK + 2
    slots = (refs[:depth], refs[depth : 2 * depth])
    end, sink = refs[2 * depth], refs[2 * depth + 3]
    right = bins[row]
    right = jnp.concatenate([right, jnp.zeros((2 * LANES - ROWS, LANES), F32)], axis=0)
    right = jnp.concatenate([right, jnp.zeros((2 * LANES, LANES), F32)], axis=1).astype(BF16)
    for unit in range(2):
        pltpu.matmul_push_rhs(right, 0, unit)
    pltpu.matmul_acc_lhs(end, tails[...], 0)
    pltpu.matmul_acc_lhs(sink, losses[...], 0)
    emit = settle(field, mask, change, lambda index: row, lambda index: 0)
    block = pltpu.matmul_pop(end)[:, :LANES]
    last = [jnp.zeros((PAD, LANES), F32) for _ in range(CLASSES)]
    for group, (target, source, _) in enumerate(GROUPS):
        scale = bins[row, OFF[source] : OFF[source] + PAD, :]
        last[target] = last[target] + block[group * PAD : (group + 1) * PAD] * scale
    drop = pltpu.matmul_pop(sink)[:, :LANES]
    for member in range(CLASSES):
        span = slice(OFF[member], OFF[member] + PAD)
        base = -drop[span] * bins[row, span, :]
        if member:
            bottom = jnp.sum(last[member], axis=0, keepdims=True)
            bottom = jnp.concatenate([bottom, jnp.zeros((PAD - HEAD - 1, LANES), F32)], axis=0)
            base = jnp.concatenate([base[:HEAD], bottom + base[HEAD:]], axis=0)
        emit(0, member, None, base)
    parts = {t: [jnp.zeros((HEAD, LANES), F32) for _ in range(2)] for t in (1, 2, 3)}
    pending, count = [], 0

    def drain():
        target, source, factor, unit, slot = pending.pop(0)
        part = pltpu.matmul_pop(slots[unit][slot])[:, :LANES]
        scale = bins[row, OFF[source] + factor : OFF[source] + factor + 1, :]
        parts[target][unit] = parts[target][unit] + part * scale

    for target in (1, 2, 3):
        order = [
            (group, source, factor)
            for factor in range(BINS)
            for group, (aim, source, _) in enumerate(GROUPS)
            if aim == target
        ]
        for group, source, factor in order:
            unit, slot = count % 2, (count // 2) % len(slots[0])
            count += 1
            left = blocks[group, factor * HEAD : (factor + 1) * HEAD, :]
            pltpu.matmul_acc_lhs(slots[unit][slot], left)
            pending.append((target, source, factor, unit, slot))
            if len(pending) > 2 * LOOK:
                drain()
        while pending:
            drain()
        emit(0, target, parts[target][0] + parts[target][1], None)


def weights(tile, row):
    out, centre = [], 1.0
    for axis in range(2):
        first, second = (
            jnp.broadcast_to(tile[row, pl.ds(AUX + 2 * axis + part, 1), :], (SUBLANES, LANES))
            for part in range(2)
        )
        speed = (first + second) * (1.0 / 6.0)
        rising, falling = jnp.maximum(speed, 0.0), jnp.minimum(speed, 0.0)
        centre = centre - 3.0 * (rising - falling)
        out.append(
            (
                6.0 * rising + 2.0 * falling,
                -rising,
                -2.0 * rising - 6.0 * falling,
                falling,
            )
        )
    return centre, out


def cells(value):
    return value.reshape(value.shape[0] // SUBLANES, SUBLANES, LANES)


def advance(centre, along_x, along_y, coefficients):
    middle, (for_x, for_y) = coefficients
    total = middle * centre
    for values, factors in ((along_x, for_x), (along_y, for_y)):
        for value, factor in zip(values, factors):
            total = total + factor * value
    return jnp.maximum(total, 0.0)


def shifted(value, amount):
    amount = amount % LANES
    return pltpu.roll(value, amount, value.ndim - 1) if amount else value


def travel(jobs, moves, refs, finish):
    def issue(number, job):
        row, outside, place = job
        left = jnp.concatenate([row().astype(BF16), outside().astype(BF16)], axis=1)
        for unit in range(2):
            start = EDGE - GROUP * place
            right = [moves[unit, :LANES, :], moves[unit, start : start + LANES, :]]
            pltpu.matmul_push_rhs(jnp.concatenate(right, axis=0), number % 2, unit)
            pltpu.matmul_acc_lhs(refs[2 * (number % 2) + unit], left, number % 2)

    for number in range(len(jobs) + 1):
        if number < len(jobs):
            issue(number, jobs[number])
        if number:
            one, two = (pltpu.matmul_pop(refs[2 * ((number - 1) % 2) + unit]) for unit in range(2))
            finish(number - 1, (one[:, :LANES], two[:, :LANES], one[:, LANES:], two[:, LANES:]))


def travellers():
    return [pltpu.ACC(unit)((ROWS, 2 * LANES), F32) for _ in range(2) for unit in range(2)]


def lanes():
    return lax.broadcasted_iota(jnp.int32, (SUBLANES, LANES), 1)


def put(field, bins, row, span, value, peak=None):
    if peak is not None:
        peak[...] = jnp.maximum(peak[...], jnp.max(value, axis=0))
    value = value.reshape(PAD, LANES)
    field[row, span, :] = value
    bins[row, span, :] = value.astype(BF16).astype(F32)


def clear_gap(*arrays):
    for start, stop in ((OFF[2] + PAD, OFF[3]), (OFF[3] + PAD, ROWS)):
        for array in arrays:
            for row in range(array.shape[0]):
                array[row, start:stop, :] = jnp.zeros((stop - start, LANES), F32)


def stage_kernel(
    count, order_hbm, state_hbm, courant_x_hbm, courant_y_hbm, gain_hbm, loss_hbm,
    rows, edges, low, high, gain, loss, state, courant_x, courant_y, order, arrived,
):
    rows_x = state.shape[1]
    flat = state.reshape(state.shape[0] * rows_x, LANES)
    pieces = [
        (state_hbm.at[pl.ds(member * BINS, BINS)], state.at[pl.ds(member * BINS, BINS)])
        for member in range(CLASSES)
    ]
    pieces += [(courant_x_hbm, courant_x), (courant_y_hbm, courant_y)]
    pieces += [(order_hbm, order)]
    pieces += [(gain_hbm, gain), (loss_hbm, loss)]
    copies = [
        pltpu.make_async_copy(source, target, arrived.at[number])
        for number, (source, target) in enumerate(pieces)
    ]
    for copy in copies:
        copy.start()
    for copy in copies[:-2]:
        copy.wait()
    spare = jnp.zeros((PAD - BINS, LANES), F32)
    for row in range(rows_x):
        cloudy = jnp.int32(0)
        for place in range(rows_x):
            hit = (order[0, 0, place] == row) & (place < count[0, 0])
            cloudy = cloudy | hit.astype(jnp.int32)
        for member in range(CLASSES):
            part = flat[pl.ds(member * BINS * rows_x + row, BINS, stride=rows_x), :]
            rows[row, OFF[member] : OFF[member] + BINS, :] = part
            rows[row, OFF[member] + BINS : OFF[member] + PAD, :] = spare
        for axis, courant in enumerate((courant_x, courant_y)):
            speed = courant[row : row + 1, :]
            upper = speed.astype(BF16).astype(F32)
            rows[row, AUX + 2 * axis : AUX + 2 * axis + 1, :] = upper
            rows[row, AUX + 2 * axis + 1 : AUX + 2 * axis + 2, :] = speed - upper
        rows[row, FLAG : FLAG + 1, :] = jnp.full((1, LANES), cloudy.astype(F32), F32)
    clear_gap(rows, edges)
    owner = lanes() // GROUP
    for start, stop in CHUNKS:
        left = jnp.zeros((PAD // SUBLANES, SUBLANES, LANES), F32)
        right = left
        for row in range(rows_x):
            value = cells(rows[row, start:stop, :])
            left = jnp.where(owner == row, shifted(value, GROUP * row), left)
            right = jnp.where(owner == row, shifted(value, GROUP * (row + 1)), right)
        edges[0, start:stop, :] = left.reshape(PAD, LANES)
        edges[1, start:stop, :] = right.reshape(PAD, LANES)
    low[...] = edges[0].astype(BF16)
    high[...] = edges[1].astype(BF16)
    for copy in copies[-2:]:
        copy.wait()


def pack_kernel(rows, packed, dense):
    for row in range(rows.shape[0]):
        for (start, stop), first in zip(CHUNKS, DENSE):
            dense[row, first : first + PAD, :] = rows[row, start:stop, :]
        packed[row] = dense[row].astype(BF16)


def widen_kernel(packed, before, after, around, to_right, to_left):
    rows_x = packed.shape[0]
    inner = lanes() % GROUP < GROUP // 2
    block = lanes() // CORNER
    corners = [None, None]
    for member, (start, stop) in enumerate(CHUNKS):
        near = jnp.where(
            inner,
            shifted(cells(before[start:stop].astype(F32)), -GROUP // 2),
            shifted(cells(after[start:stop].astype(F32)), GROUP // 2),
        )
        around[0, start:stop, :] = near.reshape(PAD, LANES)
        for side, first in enumerate((LANES - CORNER, 0)):
            moved = shifted(near, CORNER * member - first)
            old = corners[side]
            corners[side] = moved if old is None else jnp.where(block == member, moved, old)
    clear_gap(around)
    for index in range(HALO):
        span = slice(index * SENT, (index + 1) * SENT)
        to_right[span, :] = packed[rows_x - HALO + index]
        to_left[span, :] = packed[index]
    for target, corner in zip((to_right, to_left), corners):
        target[HALO * SENT :, :] = corner.reshape(PAD, LANES).astype(BF16)


def unpack(sent, tiles, dense, first_lane):
    for index in range(HALO):
        dense[index] = sent[index * SENT : (index + 1) * SENT, :].astype(F32)
        for (start, stop), first in zip(CHUNKS, DENSE):
            tiles[index, start:stop, :] = dense[index, first : first + PAD, :]
    corner = cells(sent[HALO * SENT :, :].astype(F32))
    for member, (start, stop) in enumerate(CHUNKS):
        moved = shifted(corner, first_lane - CORNER * member)
        tiles[HALO, start:stop, :] = moved.reshape(PAD, LANES)


def split_gains(blocks, fine):
    lane = lax.broadcasted_iota(jnp.int32, (HEAD, LANES), 1)

    @pl.loop(0, BINS // TOGETHER)
    def _(step):
        for part in range(TOGETHER):
            start = pl.multiple_of((step * TOGETHER + part) * HEAD, HEAD)
            rows = pl.ds(start, HEAD)
            for index, (group, first, second, high) in enumerate(FINE):
                gain = blocks[group, rows, :LANES].astype(F32) * GAIN_SCALE
                upper = gain.astype(F8).astype(F32)
                rest = gain - upper
                kept = lane >= PAD if high else lane < 2 * PAD
                left = jnp.where(kept, upper, shifted(upper, first)) if first else upper
                right = jnp.where(kept, rest, shifted(upper, second))
                fine[index, rows, :] = jnp.concatenate([left, right], axis=1).astype(F8)


def fine_bins(bins, row0, unit, scale, high):
    parts = []
    for member in (1, 2) if high else (0, 1):
        span = slice(OFF[member], OFF[member] + PAD)
        value = jnp.concatenate(
            [bins[row0 + 2 * unit, span, :], bins[row0 + 2 * unit + 1, span, :]], axis=1
        )
        value = value * scale
        upper = value.astype(F8).astype(F32)
        parts.append((upper, value - upper))
    (one, one_rest), (two, two_rest) = parts
    gap = jnp.zeros((LANES - 3 * PAD, 2 * LANES), F32)
    if high:
        order = [one_rest, one, two, gap, two_rest, one, two, gap]
    else:
        order = [one, two, one_rest, gap, one, two, two_rest, gap]
    return jnp.concatenate(order, axis=0).astype(F8)


def scale_of(peak):
    top, scale = jnp.max(peak[...]), jnp.float32(2.0**-40)
    for power in (64, 32, 16, 8, 4, 2, 1):
        larger = scale * jnp.float32(2.0**power)
        scale = jnp.where(top * larger <= PEAK, larger, scale)
    return scale


def inner_kernel(rows, around, moves, blocks, tails, losses, out, fine, bins, change, mask):
    split_gains(blocks, fine)
    rows_x = rows.shape[0]
    clear_gap(out, bins)
    places = [index + HALO // 2 for index in range(rows_x - HALO)]

    def finish(index, along_y):
        row = places[index]
        coefficients = weights(rows, row)
        mask[index] = jnp.broadcast_to(rows[row, FLAG : FLAG + 1, :], mask.shape[1:])
        for start, stop in CHUNKS:
            span = slice(start, stop)
            centre = cells(rows[row, span, :])
            along_x = [cells(rows[row + d, span, :]) for d in (-1, -2, 1, 2)]
            beside = [cells(value[span]) for value in along_y]
            put(out, bins, index, span, advance(centre, along_x, beside, coefficients))

    jobs = [(lambda row=row: rows[row], lambda: around[0], row) for row in places]
    pl.run_scoped(lambda *refs: travel(jobs, moves, refs, finish), *travellers())
    matrices = (blocks, tails, losses)
    pl.run_scoped(
        lambda *refs: four_rows(bins, 0, matrices, refs, out, mask, change),
        *accumulators(LOOK + 2, tails.shape[0], losses.shape[0]),
    )


def outer_kernel(
    rows, edges, before, after, around, from_left, from_right, middle, moves, fine, blocks, tails, losses,
    out_hbm, left, right, field, bins, change, mask, second, dense, out, peak, sent,
):
    rows_x = rows.shape[0]
    lane = lanes()
    outside = rows_x + HALO
    unpack(from_left, left, dense, LANES - CORNER)
    unpack(from_right, right, dense, 0)
    clear_gap(field, bins, second, left, right)

    def column(x):
        if x < 0:
            return left, x + HALO
        if x >= rows_x:
            return right, x - rows_x
        return rows, x

    def outer_columns(x):
        if x < 0:
            return (lambda: left[HALO]), x + rows_x
        if x >= rows_x:
            return (lambda: right[HALO]), x - rows_x
        return (lambda: around[0]), x

    reach = HALO // 2
    places = list(range(-reach, reach)) + list(range(rows_x - reach, rows_x + reach))

    def job(x):
        tile, row = column(x)
        return (lambda: tile[row], *outer_columns(x))

    def first_step(index, beside):
        x = places[index]
        tile, row = column(x)
        coefficients = weights(tile, row)
        mask[x + reach] = jnp.broadcast_to(tile[row, FLAG : FLAG + 1, :], mask.shape[1:])
        for start, stop in CHUNKS:
            span = slice(start, stop)
            centre = cells(tile[row, span, :])
            along_x = []
            for d in (-1, -2, 1, 2):
                other, at = column(x + d)
                along_x.append(cells(other[at, span, :]))
            along_y = [cells(value[span]) for value in beside]
            put(field, bins, x + reach, span, advance(centre, along_x, along_y, coefficients), peak)

    peak[...] = jnp.zeros_like(peak)
    jobs = [job(x) for x in places]
    pl.run_scoped(lambda *refs: travel(jobs, moves, refs, first_step), *travellers())
    coefficients = weights(around, 0)
    mask[outside] = jnp.broadcast_to(around[0, FLAG : FLAG + 1, :], mask.shape[1:])
    inside = lane % GROUP
    half = GROUP // 2
    for start, stop in CHUNKS:
        span = slice(start, stop)
        lower, upper = cells(before[span, :].astype(F32)), cells(after[span, :].astype(F32))
        first, last = cells(edges[0, span, :]), cells(edges[1, span, :])
        centre = cells(around[0, span, :])
        along_y = (
            jnp.where(
                inside < half + LEV,
                shifted(jnp.where(inside < half + LEV, lower, last), -LEV),
                shifted(upper, half + LEV),
            ),
            jnp.where(inside < half, lower, last),
            jnp.where(
                inside < LEV,
                shifted(lower, -half - LEV),
                shifted(jnp.where(inside < LEV, first, upper), LEV),
            ),
            jnp.where(inside < half, first, upper),
        )
        beyond = jnp.where(
            lane >= LANES // 2, cells(left[HALO, span, :]), cells(right[HALO, span, :])
        )
        along_x = (
            shifted(jnp.where(lane >= LANES - GROUP, beyond, centre), GROUP),
            shifted(jnp.where(lane >= LANES - 2 * GROUP, beyond, centre), 2 * GROUP),
            shifted(jnp.where(lane < GROUP, beyond, centre), -GROUP),
            shifted(jnp.where(lane < 2 * GROUP, beyond, centre), -2 * GROUP),
        )
        put(field, bins, outside, span, advance(centre, along_x, along_y, coefficients))
    for index in range(rows_x - HALO):
        field[index + HALO] = middle[index]
        row = index + reach
        mask[index + HALO] = jnp.broadcast_to(rows[row, FLAG : FLAG + 1, :], mask.shape[1:])
    matrices = (blocks, tails, losses)

    def last_row(*refs):
        one_row(bins, outside, matrices, refs, field, mask, change)

    def first_collisions(*refs):
        scale = scale_of(peak)

        @pl.loop(0, 2)
        def _(step):
            four_rows(bins, rows_x * step, matrices, refs, field, mask, change, fine, scale)

    def second_step(x, beside):
        coefficients = weights(rows, x)
        for start, stop in CHUNKS:
            span = slice(start, stop)
            centre = cells(field[x + reach, span, :])
            along_x = [cells(field[x + reach + d, span, :]) for d in (-1, -2, 1, 2)]
            along_y = [cells(value[span]) for value in beside]
            put(second, bins, x + reach, span, advance(centre, along_x, along_y, coefficients), peak)

    def second_collisions(*refs):
        scale = scale_of(peak)

        @pl.loop(0, rows_x // 4)
        def _(step):
            row0 = reach + 4 * step
            four_rows(bins, row0, matrices, refs, second, mask, change, fine, scale)

    sizes = (tails.shape[0], losses.shape[0])
    pl.run_scoped(last_row, *accumulators(LOOK + 2, *sizes))
    shapes = accumulators(LOOK8 + 2, *sizes)
    pl.run_scoped(first_collisions, *shapes)
    peak[...] = jnp.zeros_like(peak)
    later = [(lambda x=x: field[x + reach], lambda: field[outside], x) for x in range(rows_x)]
    pl.run_scoped(lambda *refs: travel(later, moves, refs, second_step), *travellers())
    pl.run_scoped(second_collisions, *shapes)
    flat = out.reshape(out.shape[0] * rows_x, LANES)
    copies = []
    for member in range(CLASSES):
        for x in range(rows_x):
            span = pl.ds(member * BINS * rows_x + x, BINS, stride=rows_x)
            flat[span, :] = second[x + reach, OFF[member] : OFF[member] + BINS, :]
        part = pl.ds(member * BINS, BINS)
        copies.append(pltpu.make_async_copy(out.at[part], out_hbm.at[part], sent.at[member]))
        copies[-1].start()
    for copy in copies:
        copy.wait()


def call(kernel, outs, scratch, *arguments, scalars=0, direct=0, flops=0, stored=False):
    smem = pl.BlockSpec(memory_space=pltpu.SMEM)
    vmem = pl.BlockSpec(memory_space=pltpu.VMEM)
    hbm = pl.BlockSpec(memory_space=pltpu.HBM)
    shapes = tuple(jax.ShapeDtypeStruct(shape, dtype) for shape, dtype in outs)
    moved = sum(a.size * a.dtype.itemsize for a in arguments)
    own = [pltpu.VMEM(piece, F32) if isinstance(piece, tuple) else piece for piece in scratch]
    staged = scalars + direct
    held = [pltpu.with_memory_space_constraint(a, pltpu.HBM) for a in arguments[scalars:staged]]
    return pl.pallas_call(
        kernel,
        out_shape=shapes,
        in_specs=[smem] * scalars + [hbm] * direct + [vmem] * (len(arguments) - staged),
        out_specs=tuple(hbm if stored else vmem for _ in shapes),
        scratch_shapes=own,
        compiler_params=pltpu.CompilerParams(vmem_limit_bytes=VMEM_LIMIT),
        cost_estimate=pl.CostEstimate(flops=flops, bytes_accessed=moved, transcendentals=0),
    )(*arguments[:scalars], *held, *arguments[staged:])


def exchange(axis, upward, downward):
    size = lax.axis_size(axis)
    up = [(i, (i + 1) % size) for i in range(size)]
    down = [(j, i) for i, j in up]
    return lax.ppermute(upward, axis, up), lax.ppermute(downward, axis, down)


def per_device(bin_state, courant_x, courant_y, cloudy_order, block_count, gain_kernel, loss_rate):
    rows_x = bin_state.shape[1]
    tile = (ROWS, LANES)
    rows, edges, low, high, gain, loss = call(
        stage_kernel,
        [
            ((rows_x, *tile), F32),
            ((2, *tile), F32),
            (tile, BF16),
            (tile, BF16),
            (gain_kernel.shape, BF16),
            (loss_rate.shape, BF16),
        ],
        [
            bin_state.shape,
            courant_x.shape,
            courant_y.shape,
            pltpu.SMEM(cloudy_order.shape, jnp.int32),
            pltpu.SemaphoreType.DMA((CLASSES + 5,)),
        ],
        block_count, cloudy_order, bin_state, courant_x, courant_y, gain_kernel, loss_rate,
        scalars=1, direct=6,
    )
    before, after = exchange("gy", high, low)
    *matrices, moves = prepare(gain, loss)
    (packed,) = call(
        pack_kernel,
        [((rows_x, SENT, LANES), BF16)],
        [(rows_x, SENT, LANES)],
        rows,
    )
    message = ((HALO * SENT + PAD, LANES), BF16)
    around, to_right, to_left = call(
        widen_kernel,
        [((1, *tile), F32), message, message],
        [],
        packed, before, after,
    )
    from_left, from_right = exchange("gx", to_right, to_left)
    inner = rows_x - HALO
    middle, fine = call(
        inner_kernel,
        [((inner, *tile), F32), ((len(FINE), BINS * HEAD, 2 * LANES), F8)],
        [(inner, *tile), (4, *tile), (inner, 8, LANES)],
        rows, around, moves, *matrices,
        flops=5 * 10**9,
    )
    total = rows_x + HALO + 1
    (out,) = call(
        outer_kernel,
        [(bin_state.shape, F32)],
        [
            (HALO + 1, *tile),
            (HALO + 1, *tile),
            (total, *tile),
            (total, *tile),
            (4, *tile),
            (total, 8, LANES),
            (total, *tile),
            (HALO, SENT, LANES),
            bin_state.shape,
            (SUBLANES, LANES),
            pltpu.SemaphoreType.DMA((CLASSES,)),
        ],
        rows, edges, before, after, around, from_left, from_right, middle, moves, fine, *matrices,
        flops=20 * 10**9,
        stored=True,
    )
    return out


def solution(mesh):
    placed = (
        P(None, "gx", "gy"),
        P("gx", "gy"),
        P("gx", "gy"),
        P("gx", "gy", None),
        P("gy", "gx"),
        P(),
        P(),
    )
    sharded = jax.shard_map(
        per_device, mesh=mesh, in_specs=placed, out_specs=P(None, "gx", "gy"), check_vma=False
    )

    def run(*arguments):
        with jax.sharding.use_abstract_mesh(mesh.abstract_mesh):
            return sharded(*arguments)

    return run
```

```python
import functools
import jax
import jax.numpy as jnp
from jax import lax
from jax.experimental import pallas as pl
from jax.experimental.pallas import tpu as pltpu
from jax.sharding import PartitionSpec as P

BINS = 33
CLASSES = 4
LEV = 4
STEPS = 2
LANES = 128
SUBLANES = 8
OFF = (0, 40, 80, 128)
ROWS = 176
PAD = 40
HEAD = 32
LOOK = 14
HALO = 2 * STEPS
GROUP = HALO * LEV
AUX = BINS
FLAG = AUX + 4
EDGE = 2 * LANES - GROUP
DENSE = (0, BINS + 5, 2 * BINS + 5, 3 * BINS + 5)
SENT = DENSE[3] + PAD
REACH = HALO // 2
CORNER = REACH * GROUP
CHUNKS = tuple((OFF[member], OFF[member] + PAD) for member in range(CLASSES))
VMEM_LIMIT = 24 << 20

GROUPS = (
    (1, 0, ((0, 0, False), (1, 1, False))),
    (1, 1, ((4, 1, False),)),
    (2, 0, ((2, 2, False),)),
    (3, 3, ((3, 0, True), (6, 1, True), (8, 2, True), (9, 3, False))),
    (3, 2, ((5, 1, True), (7, 2, False))),
)
PAIRS = ((0, 0), (0, 1), (0, 2), (0, 3), (1, 1), (1, 2), (1, 3), (2, 2), (2, 3), (3, 3))
NG = len(GROUPS)
F32 = jnp.float32
BF16 = jnp.bfloat16
F8 = jnp.float8_e4m3fn
FINE = ((0, 80, 40, False), (1, 0, 40, False), (2, 0, -80, True), (4, -40, -80, True))
STAGES = (((3,), None), ((4,), 1), ((2,), None), ((0, 1), 0))
GAIN_SCALE = 4096.0
PEAK = 256.0
LOOK8 = 18
TOGETHER = 11


def prepare_kernel(gain, loss, blocks, tails, losses, moves, wide, turned, upper, last_rows):
    lane = lax.broadcasted_iota(jnp.int32, (PAD, LANES), 1)
    tiles = wide.shape[2] // LANES
    turned[...] = jnp.zeros_like(turned)
    slot_of = {}
    for _, _, members in GROUPS:
        for pair, _, second in members:
            if second:
                slot_of[pair] = len(slot_of)
    for pair in range(len(PAIRS)):
        wide[pair] = jnp.zeros((PAD, tiles * LANES), F32)
        wide[pair, :BINS, : BINS * BINS] = gain[pair].astype(F32)
        if pair in slot_of:
            for tile in range(tiles):
                part = wide[pair, :, tile * LANES : (tile + 1) * LANES]
                part = jnp.concatenate([part, jnp.zeros((LANES - PAD, LANES), F32)], axis=0)
                turned[slot_of[pair], tile * LANES : (tile + 1) * LANES, :] = part.T
    last_rows[...] = jnp.zeros_like(last_rows)
    for group, (_, _, members) in enumerate(GROUPS):
        for factor in range(BINS):
            halves = [jnp.zeros((PAD, LANES), F32), jnp.zeros((PAD, LANES), F32)]
            second_members = [m for m in members if m[2]]
            if second_members:
                rows = []
                for other in range(CLASSES - 1):
                    found = [m for m in second_members if m[1] == other]
                    if found:
                        piece = turned[slot_of[found[0][0]], pl.ds(factor, PAD, stride=BINS), :]
                        rows.append(piece)
                    else:
                        rows.append(jnp.zeros((PAD, LANES), F32))
                rows.append(jnp.zeros((LANES - 3 * PAD, LANES), F32))
                halves[0] = jnp.concatenate(rows, axis=0).T[:PAD]
            for pair, other, second in members:
                if second:
                    continue
                start = BINS * factor
                tile, inside = divmod(start, LANES)
                half, at = divmod(OFF[other], LANES)
                shift = (at - inside) % LANES
                first = wide[pair, :, tile * LANES : (tile + 1) * LANES]
                first = pltpu.roll(first, shift, 1) if shift else first
                if inside + BINS > LANES:
                    rest = wide[pair, :, (tile + 1) * LANES : (tile + 2) * LANES]
                    rest = pltpu.roll(rest, shift, 1) if shift else rest
                    first = jnp.where(lane < at + LANES - inside, first, rest)
                halves[half] = jnp.where((lane >= at) & (lane < at + BINS), first, halves[half])
            full = jnp.concatenate(halves, axis=1)
            blocks[group, factor * HEAD : (factor + 1) * HEAD, :] = full[:HEAD].astype(BF16)
            last_rows[group * PAD + factor : group * PAD + factor + 1, :] = full[HEAD : HEAD + 1]
    tails[...] = last_rows[...].astype(BF16)
    upper[...] = jnp.zeros_like(upper)
    for pair, (first, second) in enumerate(PAIRS):
        half, at = divmod(OFF[second], LANES)
        rates = jnp.concatenate(
            [loss[pair].astype(F32), jnp.zeros((BINS, LANES - BINS), F32)], axis=1
        )
        rates = pltpu.roll(rates, at, 1) if at else rates
        rows = slice(OFF[first], OFF[first] + BINS)
        span = slice(half * LANES, (half + 1) * LANES)
        upper[rows, span] = upper[rows, span] + rates
    whole = upper[...]
    losses[...] = (whole + whole.T)[: losses.shape[0]].astype(BF16)
    fill_moves(moves)


def fill_moves(moves):
    moves[...] = jnp.zeros_like(moves)
    for part, step in enumerate((LEV, 2 * LEV)):
        source = lax.broadcasted_iota(jnp.int32, (LANES, LANES), 0)
        target = lax.broadcasted_iota(jnp.int32, (LANES, LANES), 1)
        moves[part, :LANES, :LANES] = jnp.where(source == target - step, 1.0, 0.0).astype(BF16)
        moves[part, :LANES, LANES:] = jnp.where(source == target + step, 1.0, 0.0).astype(BF16)
        source, target = source[:GROUP], target[:GROUP]
        half = GROUP // 2
        low = (target < step) & (source == target + half - step)
        high = (target >= LANES - step) & (source == target - (LANES - step) + half)
        rows = slice(EDGE, EDGE + GROUP)
        moves[part, rows, :LANES] = jnp.where(low, 1.0, 0.0).astype(BF16)
        moves[part, rows, LANES:] = jnp.where(high, 1.0, 0.0).astype(BF16)


def prepare(gain_kernel, loss_rate):
    wide = -(-BINS * BINS // LANES) * LANES
    tail = -(-NG * PAD // 16) * 16
    rows = -(-ROWS // 16) * 16
    return pl.pallas_call(
        prepare_kernel,
        out_shape=(
            jax.ShapeDtypeStruct((NG, BINS * HEAD, 2 * LANES), BF16),
            jax.ShapeDtypeStruct((tail, 2 * LANES), BF16),
            jax.ShapeDtypeStruct((rows, 2 * LANES), BF16),
            jax.ShapeDtypeStruct((2, EDGE + LANES, 2 * LANES), BF16),
        ),
        scratch_shapes=[
            pltpu.VMEM((len(PAIRS), PAD, wide), F32),
            pltpu.VMEM((4, BINS * PAD + BINS, LANES), F32),
            pltpu.VMEM((2 * LANES, 2 * LANES), F32),
            pltpu.VMEM((tail, 2 * LANES), F32),
        ],
        compiler_params=pltpu.CompilerParams(vmem_limit_bytes=VMEM_LIMIT),
        cost_estimate=pl.CostEstimate(flops=2 * 10**9, bytes_accessed=4 << 20, transcendentals=0),
    )(gain_kernel, loss_rate)


def collide_tiles(bins, row0, blocks, tails, losses, slots, ends, sinks, emit):
    for unit in range(2):
        right = jnp.concatenate([bins[row0 + 2 * unit], bins[row0 + 2 * unit + 1]], axis=1)
        right = jnp.concatenate(
            [right, jnp.zeros((2 * LANES - ROWS, 2 * LANES), F32)], axis=0
        ).astype(BF16)
        pltpu.matmul_push_rhs(right, 0, unit)
    for unit in range(2):
        pltpu.matmul_acc_lhs(ends[unit], tails[...], 0)
    for unit in range(2):
        pltpu.matmul_acc_lhs(sinks[unit], losses[...])
    depth = len(slots[0])
    pending, count = [], 0
    parts = {t: [[jnp.zeros((HEAD, LANES), F32) for _ in range(2)] for _ in range(2)] for t in (1, 2, 3)}

    def drain():
        target, source, factor, slot = pending.pop(0)
        for unit in range(2):
            block = pltpu.matmul_pop(slots[unit][slot])
            for half in range(2):
                scale = bins[row0 + 2 * unit + half, pl.ds(OFF[source] + factor, 1), :]
                part = block[:, half * LANES : (half + 1) * LANES]
                parts[target][unit][half] = parts[target][unit][half] + part * scale

    last = [[[jnp.zeros((PAD, LANES), F32) for _ in range(2)] for _ in range(2)] for _ in range(4)]
    for unit in range(2):
        block = pltpu.matmul_pop(ends[unit])
        for group, (target, source, _) in enumerate(GROUPS):
            for half in range(2):
                scale = bins[row0 + 2 * unit + half, OFF[source] : OFF[source] + PAD, :]
                piece = block[group * PAD : (group + 1) * PAD, half * LANES : (half + 1) * LANES]
                last[target][unit][half] = last[target][unit][half] + piece * scale
    drop = [pltpu.matmul_pop(sinks[unit]) for unit in range(2)]
    for unit in range(2):
        for half in range(2):
            row = row0 + 2 * unit + half
            for member in range(CLASSES):
                rows = slice(OFF[member], OFF[member] + PAD)
                lost = drop[unit][rows, half * LANES : (half + 1) * LANES] * bins[row, rows, :]
                if member:
                    bottom = jnp.sum(last[member][unit][half], axis=0, keepdims=True)
                    bottom = jnp.concatenate([bottom, jnp.zeros((PAD - HEAD - 1, LANES), F32)], axis=0)
                    base = jnp.concatenate([-lost[:HEAD], bottom - lost[HEAD:]], axis=0)
                else:
                    base = -lost
                emit(2 * unit + half, member, None, base)
    for target in (1, 2, 3):
        order = [
            (group, source, factor)
            for factor in range(BINS)
            for group, (aim, source, _) in enumerate(GROUPS)
            if aim == target
        ]
        for group, source, factor in order:
            slot = count % depth
            count += 1
            left = blocks[group, factor * HEAD : (factor + 1) * HEAD, :]
            for unit in range(2):
                pltpu.matmul_acc_lhs(slots[unit][slot], left)
            pending.append((target, source, factor, slot))
            if len(pending) > LOOK:
                drain()
        while pending:
            drain()
        for unit in range(2):
            for half in range(2):
                emit(2 * unit + half, target, parts[target][unit][half], None)


def collide_fine(bins, row0, blocks, tails, losses, fine, scale, slots, ends, sinks, emit):
    for unit in range(2):
        right = jnp.concatenate([bins[row0 + 2 * unit], bins[row0 + 2 * unit + 1]], axis=1)
        right = jnp.concatenate(
            [right, jnp.zeros((2 * LANES - ROWS, 2 * LANES), F32)], axis=0
        ).astype(BF16)
        pltpu.matmul_push_rhs(right, 0, unit)
    for unit in range(2):
        pltpu.matmul_acc_lhs(ends[unit], tails[...], 0)
    for unit in range(2):
        pltpu.matmul_acc_lhs(sinks[unit], losses[...])
    for unit in range(2):
        rows = (row0 + 2 * unit, row0 + 2 * unit + 1)
        pltpu.matmul_push_rhs(fine_bins(bins, rows, scale, True), 1, unit)
    last = [[[jnp.zeros((PAD, LANES), F32) for _ in range(2)] for _ in range(2)] for _ in range(4)]
    for unit in range(2):
        block = pltpu.matmul_pop(ends[unit])
        for group, (target, source, _) in enumerate(GROUPS):
            for half in range(2):
                factor = bins[row0 + 2 * unit + half, OFF[source] : OFF[source] + PAD, :]
                piece = block[group * PAD : (group + 1) * PAD, half * LANES : (half + 1) * LANES]
                last[target][unit][half] = last[target][unit][half] + piece * factor
    drop = [pltpu.matmul_pop(sinks[unit]) for unit in range(2)]
    for unit in range(2):
        for half in range(2):
            row = row0 + 2 * unit + half
            for member in range(CLASSES):
                rows = slice(OFF[member], OFF[member] + PAD)
                lost = drop[unit][rows, half * LANES : (half + 1) * LANES] * bins[row, rows, :]
                if member:
                    bottom = jnp.sum(last[member][unit][half], axis=0, keepdims=True)
                    bottom = jnp.concatenate([bottom, jnp.zeros((PAD - HEAD - 1, LANES), F32)], axis=0)
                    base = jnp.concatenate([-lost[:HEAD], bottom - lost[HEAD:]], axis=0)
                else:
                    base = -lost
                emit(2 * unit + half, member, None, base)
    down = 1.0 / (scale * GAIN_SCALE)
    place = {group: index for index, (group, *_) in enumerate(FINE)}
    stages = STAGES
    depth = len(slots[0])
    sums = [
        [[jnp.zeros((HEAD, LANES), F32) for _ in range(2)] for _ in range(2)] for _ in stages
    ]
    left_over = [BINS * len(groups) for groups, _ in stages]
    pending, count = [], 0

    def drain():
        stage, source, factor, slot = pending.pop(0)
        for unit in range(2):
            block = pltpu.matmul_pop(slots[unit][slot])
            for half in range(2):
                scaled = bins[row0 + 2 * unit + half, pl.ds(OFF[source] + factor, 1), :]
                part = block[:, half * LANES : (half + 1) * LANES]
                sums[stage][unit][half] = sums[stage][unit][half] + part * scaled
        left_over[stage] -= 1
        if left_over[stage] or not stage:
            return
        target = (None, 3, 2, 1)[stage]
        for unit in range(2):
            for half in range(2):
                total = sums[stage][unit][half] * down
                if target == 3:
                    total = total + sums[0][unit][half]
                emit(2 * unit + half, target, total, None)

    for stage, (groups, staged) in enumerate(stages):
        for factor in range(BINS):
            for group in groups:
                slot = count % depth
                count += 1
                rows = slice(factor * HEAD, (factor + 1) * HEAD)
                left = fine[place[group], rows, :] if group in place else blocks[group, rows, :]
                for unit in range(2):
                    pltpu.matmul_acc_lhs(slots[unit][slot], left, staged)
                if staged == 1:
                    for unit in range(2):
                        pair = (row0 + 2 * unit, row0 + 2 * unit + 1)
                        right = fine_bins(bins, pair, scale, False)
                        pltpu.matmul_push_rhs(right, 0, unit)
                staged = None
                pending.append((stage, GROUPS[group][1], factor, slot))
                if len(pending) > LOOK8:
                    drain()
    while pending:
        drain()


def accumulators(depth, tail, rows):
    return (
        [pltpu.ACC(unit)((HEAD, 2 * LANES), F32) for unit in range(2) for _ in range(depth)]
        + [pltpu.ACC(unit)((tail, 2 * LANES), F32) for unit in range(2)]
        + [pltpu.ACC(unit)((rows, 2 * LANES), F32) for unit in range(2)]
    )


def settle(field, mask, change, row, place):
    def emit(index, member, gained, base):
        at = row(index)
        start = OFF[member]
        if base is not None and member:
            change[place(index), start : start + PAD, :] = base
            return
        if member:
            base = change[place(index), start : start + PAD, :]
            base = jnp.concatenate([base[:HEAD] + gained, base[HEAD:]], axis=0)
        part = jnp.where(mask[at, :1, :] > 0.5, base.astype(BF16).astype(F32), 0.0)
        span = slice(start, start + PAD)
        field[at, span, :] = field[at, span, :] + part

    return emit


def four_rows(bins, row0, matrices, refs, field, mask, change, fine=None, scale=None):
    depth = LOOK + 2 if fine is None else LOOK8 + 2
    slots = (refs[:depth], refs[depth : 2 * depth])
    ends, sinks = refs[2 * depth : 2 * depth + 2], refs[2 * depth + 2 :]
    emit = settle(field, mask, change, lambda index: row0 + index, lambda index: index)
    if fine is None:
        collide_tiles(bins, row0, *matrices, slots, ends, sinks, emit)
    else:
        collide_fine(bins, row0, *matrices, fine, scale, slots, ends, sinks, emit)


def one_row(bins, row, matrices, refs, field, mask, change, fine, scale):
    blocks, tails, losses = matrices
    depth = LOOK8 + 2
    slots = (refs[:depth], refs[depth : 2 * depth])
    end, sink = refs[2 * depth], refs[2 * depth + 3]
    right = bins[row]
    right = jnp.concatenate([right, jnp.zeros((2 * LANES - ROWS, LANES), F32)], axis=0)
    right = jnp.concatenate([right, jnp.zeros((2 * LANES, LANES), F32)], axis=1).astype(BF16)
    for unit in range(2):
        pltpu.matmul_push_rhs(right, 0, unit)
    pltpu.matmul_acc_lhs(end, tails[...], 0)
    pltpu.matmul_acc_lhs(sink, losses[...], 0)
    for unit in range(2):
        pltpu.matmul_push_rhs(fine_bins(bins, (row,), scale, True), 1, unit)
    emit = settle(field, mask, change, lambda index: row, lambda index: 0)
    block = pltpu.matmul_pop(end)[:, :LANES]
    last = [jnp.zeros((PAD, LANES), F32) for _ in range(CLASSES)]
    for group, (target, source, _) in enumerate(GROUPS):
        column = bins[row, OFF[source] : OFF[source] + PAD, :]
        last[target] = last[target] + block[group * PAD : (group + 1) * PAD] * column
    drop = pltpu.matmul_pop(sink)[:, :LANES]
    for member in range(CLASSES):
        span = slice(OFF[member], OFF[member] + PAD)
        base = -drop[span] * bins[row, span, :]
        if member:
            bottom = jnp.sum(last[member], axis=0, keepdims=True)
            bottom = jnp.concatenate([bottom, jnp.zeros((PAD - HEAD - 1, LANES), F32)], axis=0)
            base = jnp.concatenate([base[:HEAD], bottom + base[HEAD:]], axis=0)
        emit(0, member, None, base)
    place = {group: index for index, (group, *_) in enumerate(FINE)}
    sums = [[jnp.zeros((HEAD, LANES), F32) for _ in range(2)] for _ in STAGES]
    pending, count = [], 0

    def drain():
        stage, source, factor, unit, slot = pending.pop(0)
        part = pltpu.matmul_pop(slots[unit][slot])[:, :LANES]
        factors = bins[row, OFF[source] + factor : OFF[source] + factor + 1, :]
        sums[stage][unit] = sums[stage][unit] + part * factors

    for stage, (groups, staged) in enumerate(STAGES):
        fresh = [staged, staged]
        for factor in range(BINS):
            for group in groups:
                unit, slot = count % 2, (count // 2) % len(slots[0])
                count += 1
                rows = slice(factor * HEAD, (factor + 1) * HEAD)
                left = fine[place[group], rows, :] if group in place else blocks[group, rows, :]
                pltpu.matmul_acc_lhs(slots[unit][slot], left, fresh[unit])
                if fresh[unit] == 1:
                    pltpu.matmul_push_rhs(fine_bins(bins, (row,), scale, False), 0, unit)
                fresh[unit] = None
                pending.append((stage, GROUPS[group][1], factor, unit, slot))
                if len(pending) > 2 * LOOK8:
                    drain()
    while pending:
        drain()
    down = 1.0 / (scale * GAIN_SCALE)
    wide, *narrow = [first + second for first, second in sums]
    for target, total in zip((3, 2, 1), narrow):
        total = total * down
        emit(0, target, total + wide if target == 3 else total, None)


def weights(tile, row):
    out, centre = [], 1.0
    for axis in range(2):
        first, second = (
            jnp.broadcast_to(tile[row, pl.ds(AUX + 2 * axis + part, 1), :], (SUBLANES, LANES))
            for part in range(2)
        )
        speed = (first + second) * (1.0 / 6.0)
        rising, falling = jnp.maximum(speed, 0.0), jnp.minimum(speed, 0.0)
        centre = centre - 3.0 * (rising - falling)
        out.append(
            (
                6.0 * rising + 2.0 * falling,
                -rising,
                -2.0 * rising - 6.0 * falling,
                falling,
            )
        )
    return centre, out


def cells(value):
    return value.reshape(value.shape[0] // SUBLANES, SUBLANES, LANES)


def advance(centre, along_x, along_y, coefficients):
    middle, (for_x, for_y) = coefficients
    total = middle * centre
    for values, factors in ((along_x, for_x), (along_y, for_y)):
        for value, factor in zip(values, factors):
            total = total + factor * value
    return jnp.maximum(total, 0.0)


def shifted(value, amount):
    amount = amount % LANES
    return pltpu.roll(value, amount, value.ndim - 1) if amount else value


def travel(jobs, moves, refs, finish):
    def issue(number, job):
        row, outside, place = job
        left = jnp.concatenate([row().astype(BF16), outside().astype(BF16)], axis=1)
        for unit in range(2):
            start = EDGE - GROUP * place
            right = [moves[unit, :LANES, :], moves[unit, start : start + LANES, :]]
            pltpu.matmul_push_rhs(jnp.concatenate(right, axis=0), number % 2, unit)
            pltpu.matmul_acc_lhs(refs[2 * (number % 2) + unit], left, number % 2)

    for number in range(len(jobs) + 1):
        if number < len(jobs):
            issue(number, jobs[number])
        if number:
            one, two = (pltpu.matmul_pop(refs[2 * ((number - 1) % 2) + unit]) for unit in range(2))
            finish(number - 1, (one[:, :LANES], two[:, :LANES], one[:, LANES:], two[:, LANES:]))


def travellers():
    return [pltpu.ACC(unit)((ROWS, 2 * LANES), F32) for _ in range(2) for unit in range(2)]


def lanes():
    return lax.broadcasted_iota(jnp.int32, (SUBLANES, LANES), 1)


def put(field, bins, row, span, value, peak=None):
    if peak is not None:
        peak[...] = jnp.maximum(peak[...], jnp.max(value, axis=0))
    value = value.reshape(PAD, LANES)
    field[row, span, :] = value
    bins[row, span, :] = value.astype(BF16).astype(F32)


def clear_gap(*arrays):
    for start, stop in ((OFF[2] + PAD, OFF[3]), (OFF[3] + PAD, ROWS)):
        for array in arrays:
            for row in range(array.shape[0]):
                array[row, start:stop, :] = jnp.zeros((stop - start, LANES), F32)


def stage_kernel(
    count, order_hbm, state_hbm, courant_x_hbm, courant_y_hbm, gain_hbm, loss_hbm,
    rows, edges, low, high, gain, loss, state, courant_x, courant_y, order, arrived,
):
    rows_x = state.shape[1]
    flat = state.reshape(state.shape[0] * rows_x, LANES)
    pieces = [
        (state_hbm.at[pl.ds(member * BINS, BINS)], state.at[pl.ds(member * BINS, BINS)])
        for member in range(CLASSES)
    ]
    pieces += [(courant_x_hbm, courant_x), (courant_y_hbm, courant_y)]
    pieces += [(order_hbm, order)]
    pieces += [(gain_hbm, gain), (loss_hbm, loss)]
    copies = [
        pltpu.make_async_copy(source, target, arrived.at[number])
        for number, (source, target) in enumerate(pieces)
    ]
    for copy in copies:
        copy.start()
    for copy in copies[:-2]:
        copy.wait()
    spare = jnp.zeros((PAD - BINS, LANES), F32)
    for row in range(rows_x):
        cloudy = jnp.int32(0)
        for place in range(rows_x):
            hit = (order[0, 0, place] == row) & (place < count[0, 0])
            cloudy = cloudy | hit.astype(jnp.int32)
        for member in range(CLASSES):
            part = flat[pl.ds(member * BINS * rows_x + row, BINS, stride=rows_x), :]
            rows[row, OFF[member] : OFF[member] + BINS, :] = part
            rows[row, OFF[member] + BINS : OFF[member] + PAD, :] = spare
        for axis, courant in enumerate((courant_x, courant_y)):
            speed = courant[row : row + 1, :]
            upper = speed.astype(BF16).astype(F32)
            rows[row, AUX + 2 * axis : AUX + 2 * axis + 1, :] = upper
            rows[row, AUX + 2 * axis + 1 : AUX + 2 * axis + 2, :] = speed - upper
        rows[row, FLAG : FLAG + 1, :] = jnp.full((1, LANES), cloudy.astype(F32), F32)
    clear_gap(rows, edges)
    owner = lanes() // GROUP
    for start, stop in CHUNKS:
        left = jnp.zeros((PAD // SUBLANES, SUBLANES, LANES), F32)
        right = left
        for row in range(rows_x):
            value = cells(rows[row, start:stop, :])
            left = jnp.where(owner == row, shifted(value, GROUP * row), left)
            right = jnp.where(owner == row, shifted(value, GROUP * (row + 1)), right)
        edges[0, start:stop, :] = left.reshape(PAD, LANES)
        edges[1, start:stop, :] = right.reshape(PAD, LANES)
    low[...] = edges[0].astype(BF16)
    high[...] = edges[1].astype(BF16)
    for copy in copies[-2:]:
        copy.wait()


def pack_kernel(rows, packed, dense):
    for row in range(rows.shape[0]):
        for (start, stop), first in zip(CHUNKS, DENSE):
            dense[row, first : first + PAD, :] = rows[row, start:stop, :]
        packed[row] = dense[row].astype(BF16)


def widen_kernel(packed, before, after, around, to_right, to_left):
    rows_x = packed.shape[0]
    inner = lanes() % GROUP < GROUP // 2
    block = lanes() // CORNER
    corners = [None, None]
    for member, (start, stop) in enumerate(CHUNKS):
        near = jnp.where(
            inner,
            shifted(cells(before[start:stop].astype(F32)), -GROUP // 2),
            shifted(cells(after[start:stop].astype(F32)), GROUP // 2),
        )
        around[0, start:stop, :] = near.reshape(PAD, LANES)
        for side, first in enumerate((LANES - CORNER, 0)):
            moved = shifted(near, CORNER * member - first)
            old = corners[side]
            corners[side] = moved if old is None else jnp.where(block == member, moved, old)
    clear_gap(around)
    for index in range(HALO):
        span = slice(index * SENT, (index + 1) * SENT)
        to_right[span, :] = packed[rows_x - HALO + index]
        to_left[span, :] = packed[index]
    for target, corner in zip((to_right, to_left), corners):
        target[HALO * SENT :, :] = corner.reshape(PAD, LANES).astype(BF16)


def unpack(sent, tiles, dense, first_lane):
    for index in range(HALO):
        dense[index] = sent[index * SENT : (index + 1) * SENT, :].astype(F32)
        for (start, stop), first in zip(CHUNKS, DENSE):
            tiles[index, start:stop, :] = dense[index, first : first + PAD, :]
    corner = cells(sent[HALO * SENT :, :].astype(F32))
    for member, (start, stop) in enumerate(CHUNKS):
        moved = shifted(corner, first_lane - CORNER * member)
        tiles[HALO, start:stop, :] = moved.reshape(PAD, LANES)


def split_gains(blocks, fine):
    lane = lax.broadcasted_iota(jnp.int32, (HEAD, LANES), 1)

    @pl.loop(0, BINS // TOGETHER)
    def _(step):
        for part in range(TOGETHER):
            start = pl.multiple_of((step * TOGETHER + part) * HEAD, HEAD)
            rows = pl.ds(start, HEAD)
            for index, (group, first, second, high) in enumerate(FINE):
                gain = blocks[group, rows, :LANES].astype(F32) * GAIN_SCALE
                upper = gain.astype(F8).astype(F32)
                rest = gain - upper
                kept = lane >= PAD if high else lane < 2 * PAD
                left = jnp.where(kept, upper, shifted(upper, first)) if first else upper
                right = jnp.where(kept, rest, shifted(upper, second))
                fine[index, rows, :] = jnp.concatenate([left, right], axis=1).astype(F8)


def fine_bins(bins, rows, scale, high):
    parts = []
    for member in (1, 2) if high else (0, 1):
        span = slice(OFF[member], OFF[member] + PAD)
        halves = [bins[row, span, :] * scale for row in rows]
        if len(halves) == 1:
            halves.append(jnp.zeros_like(halves[0]))
        value = jnp.concatenate(halves, axis=1)
        upper = value.astype(F8).astype(F32)
        parts.append((upper, value - upper))
    (one, one_rest), (two, two_rest) = parts
    gap = jnp.zeros((LANES - 3 * PAD, 2 * LANES), F32)
    if high:
        order = [one_rest, one, two, gap, two_rest, one, two, gap]
    else:
        order = [one, two, one_rest, gap, one, two, two_rest, gap]
    return jnp.concatenate(order, axis=0).astype(F8)


def scale_of(peak):
    top, scale = jnp.max(peak[...]), jnp.float32(2.0**-40)
    for power in (64, 32, 16, 8, 4, 2, 1):
        larger = scale * jnp.float32(2.0**power)
        scale = jnp.where(top * larger <= PEAK, larger, scale)
    return scale


STEPS_AWAY = (-1, -2, 1, 2)


def border_columns(rows_x):
    return list(range(REACH)) + list(range(rows_x - REACH, rows_x))


def flank(edges, before, after, around, partial):
    middle, (_, for_y) = weights(around, 0)
    inside = lanes() % GROUP
    half = GROUP // 2
    for start, stop in CHUNKS:
        span = slice(start, stop)
        lower, upper = cells(before[span, :].astype(F32)), cells(after[span, :].astype(F32))
        first, last = cells(edges[0, span, :]), cells(edges[1, span, :])
        along_y = (
            jnp.where(
                inside < half + LEV,
                shifted(jnp.where(inside < half + LEV, lower, last), -LEV),
                shifted(upper, half + LEV),
            ),
            jnp.where(inside < half, lower, last),
            jnp.where(
                inside < LEV,
                shifted(lower, -half - LEV),
                shifted(jnp.where(inside < LEV, first, upper), LEV),
            ),
            jnp.where(inside < half, first, upper),
        )
        total = middle * cells(around[0, span, :])
        for value, factor in zip(along_y, for_y):
            total = total + factor * value
        partial[0, span, :] = total.reshape(PAD, LANES)
    clear_gap(partial)


def inner_kernel(
    rows, edges, before, after, around, moves, blocks, tails, losses,
    out, fine, partial, early, bins, change, mask,
):
    split_gains(blocks, fine)
    flank(edges, before, after, around, partial)
    rows_x = rows.shape[0]
    clear_gap(out, bins)
    places = [index + HALO // 2 for index in range(rows_x - HALO)]

    places += border_columns(rows_x)

    def finish(index, along_y):
        row = places[index]
        coefficients = weights(rows, row)
        within = index < rows_x - HALO
        if within:
            mask[index] = jnp.broadcast_to(rows[row, FLAG : FLAG + 1, :], mask.shape[1:])
        for start, stop in CHUNKS:
            span = slice(start, stop)
            centre = cells(rows[row, span, :])
            beside = [cells(value[span]) for value in along_y]
            if within:
                along_x = [cells(rows[row + d, span, :]) for d in STEPS_AWAY]
                put(out, bins, index, span, advance(centre, along_x, beside, coefficients))
                continue
            middle, (for_x, for_y) = coefficients
            total = middle * centre
            for value, factor in zip(beside, for_y):
                total = total + factor * value
            for d, factor in zip(STEPS_AWAY, for_x):
                if 0 <= row + d < rows_x:
                    total = total + factor * cells(rows[row + d, span, :])
            early[index - rows_x + HALO, span, :] = total.reshape(PAD, LANES)

    jobs = [(lambda row=row: rows[row], lambda: around[0], row) for row in places]
    pl.run_scoped(lambda *refs: travel(jobs, moves, refs, finish), *travellers())
    matrices = (blocks, tails, losses)
    pl.run_scoped(
        lambda *refs: four_rows(bins, 0, matrices, refs, out, mask, change),
        *accumulators(LOOK + 2, tails.shape[0], losses.shape[0]),
    )


def outer_kernel(
    rows, partial, early, around, from_left, from_right, middle, moves, fine, blocks, tails, losses,
    out_hbm, left, right, field, bins, change, mask, second, dense, out, peak, sent,
):
    rows_x = rows.shape[0]
    lane = lanes()
    outside = rows_x + HALO
    unpack(from_left, left, dense, LANES - CORNER)
    unpack(from_right, right, dense, 0)
    clear_gap(field, bins, second, left, right)
    peak[...] = jnp.zeros_like(peak)

    def column(x):
        if x < 0:
            return left, x + HALO
        if x >= rows_x:
            return right, x - rows_x
        return rows, x

    def outer_columns(x):
        if x < 0:
            return (lambda: left[HALO]), x + rows_x
        if x >= rows_x:
            return (lambda: right[HALO]), x - rows_x
        return (lambda: around[0]), x

    reach = HALO // 2
    places = list(range(-reach, 0)) + list(range(rows_x, rows_x + reach))

    def job(x):
        tile, row = column(x)
        return (lambda: tile[row], *outer_columns(x))

    def first_step(index, beside):
        x = places[index]
        tile, row = column(x)
        coefficients = weights(tile, row)
        mask[x + reach] = jnp.broadcast_to(tile[row, FLAG : FLAG + 1, :], mask.shape[1:])
        for start, stop in CHUNKS:
            span = slice(start, stop)
            centre = cells(tile[row, span, :])
            along_x = []
            for d in (-1, -2, 1, 2):
                other, at = column(x + d)
                along_x.append(cells(other[at, span, :]))
            along_y = [cells(value[span]) for value in beside]
            put(field, bins, x + reach, span, advance(centre, along_x, along_y, coefficients), peak)

    jobs = [job(x) for x in places]
    pl.run_scoped(lambda *refs: travel(jobs, moves, refs, first_step), *travellers())
    for index, x in enumerate(border_columns(rows_x)):
        _, (for_x, _) = weights(rows, x)
        mask[x + reach] = jnp.broadcast_to(rows[x, FLAG : FLAG + 1, :], mask.shape[1:])
        for start, stop in CHUNKS:
            span = slice(start, stop)
            total = cells(early[index, span, :])
            for d, factor in zip(STEPS_AWAY, for_x):
                if not 0 <= x + d < rows_x:
                    tile, row = column(x + d)
                    total = total + factor * cells(tile[row, span, :])
            put(field, bins, x + reach, span, jnp.maximum(total, 0.0), peak)
    _, (for_x, _) = weights(around, 0)
    mask[outside] = jnp.broadcast_to(around[0, FLAG : FLAG + 1, :], mask.shape[1:])
    for start, stop in CHUNKS:
        span = slice(start, stop)
        centre = cells(around[0, span, :])
        beyond = jnp.where(
            lane >= LANES // 2, cells(left[HALO, span, :]), cells(right[HALO, span, :])
        )
        along_x = (
            shifted(jnp.where(lane >= LANES - GROUP, beyond, centre), GROUP),
            shifted(jnp.where(lane >= LANES - 2 * GROUP, beyond, centre), 2 * GROUP),
            shifted(jnp.where(lane < GROUP, beyond, centre), -GROUP),
            shifted(jnp.where(lane < 2 * GROUP, beyond, centre), -2 * GROUP),
        )
        total = cells(partial[0, span, :])
        for value, factor in zip(along_x, for_x):
            total = total + factor * value
        put(field, bins, outside, span, jnp.maximum(total, 0.0), peak)
    for index in range(rows_x - HALO):
        field[index + HALO] = middle[index]
        row = index + reach
        mask[index + HALO] = jnp.broadcast_to(rows[row, FLAG : FLAG + 1, :], mask.shape[1:])
    matrices = (blocks, tails, losses)

    def first_collisions(*refs):
        scale = scale_of(peak)
        one_row(bins, outside, matrices, refs, field, mask, change, fine, scale)

        @pl.loop(0, 2)
        def _(step):
            four_rows(bins, rows_x * step, matrices, refs, field, mask, change, fine, scale)

    def second_step(x, beside):
        coefficients = weights(rows, x)
        for start, stop in CHUNKS:
            span = slice(start, stop)
            centre = cells(field[x + reach, span, :])
            along_x = [cells(field[x + reach + d, span, :]) for d in (-1, -2, 1, 2)]
            along_y = [cells(value[span]) for value in beside]
            put(second, bins, x + reach, span, advance(centre, along_x, along_y, coefficients), peak)

    def second_collisions(*refs):
        scale = scale_of(peak)

        @pl.loop(0, rows_x // 4)
        def _(step):
            row0 = reach + 4 * step
            four_rows(bins, row0, matrices, refs, second, mask, change, fine, scale)

    sizes = (tails.shape[0], losses.shape[0])
    shapes = accumulators(LOOK8 + 2, *sizes)
    pl.run_scoped(first_collisions, *shapes)
    peak[...] = jnp.zeros_like(peak)
    later = [(lambda x=x: field[x + reach], lambda: field[outside], x) for x in range(rows_x)]
    pl.run_scoped(lambda *refs: travel(later, moves, refs, second_step), *travellers())
    pl.run_scoped(second_collisions, *shapes)
    flat = out.reshape(out.shape[0] * rows_x, LANES)
    copies = []
    for member in range(CLASSES):
        for x in range(rows_x):
            span = pl.ds(member * BINS * rows_x + x, BINS, stride=rows_x)
            flat[span, :] = second[x + reach, OFF[member] : OFF[member] + BINS, :]
        part = pl.ds(member * BINS, BINS)
        copies.append(pltpu.make_async_copy(out.at[part], out_hbm.at[part], sent.at[member]))
        copies[-1].start()
    for copy in copies:
        copy.wait()


def call(kernel, outs, scratch, *arguments, scalars=0, direct=0, flops=0, stored=False):
    smem = pl.BlockSpec(memory_space=pltpu.SMEM)
    vmem = pl.BlockSpec(memory_space=pltpu.VMEM)
    hbm = pl.BlockSpec(memory_space=pltpu.HBM)
    shapes = tuple(jax.ShapeDtypeStruct(shape, dtype) for shape, dtype in outs)
    moved = sum(a.size * a.dtype.itemsize for a in arguments)
    own = [pltpu.VMEM(piece, F32) if isinstance(piece, tuple) else piece for piece in scratch]
    staged = scalars + direct
    held = [pltpu.with_memory_space_constraint(a, pltpu.HBM) for a in arguments[scalars:staged]]
    return pl.pallas_call(
        kernel,
        out_shape=shapes,
        in_specs=[smem] * scalars + [hbm] * direct + [vmem] * (len(arguments) - staged),
        out_specs=tuple(hbm if stored else vmem for _ in shapes),
        scratch_shapes=own,
        compiler_params=pltpu.CompilerParams(vmem_limit_bytes=VMEM_LIMIT),
        cost_estimate=pl.CostEstimate(flops=flops, bytes_accessed=moved, transcendentals=0),
    )(*arguments[:scalars], *held, *arguments[staged:])


def exchange(axis, upward, downward):
    size = lax.axis_size(axis)
    up = [(i, (i + 1) % size) for i in range(size)]
    down = [(j, i) for i, j in up]
    return lax.ppermute(upward, axis, up), lax.ppermute(downward, axis, down)


def per_device(bin_state, courant_x, courant_y, cloudy_order, block_count, gain_kernel, loss_rate):
    rows_x = bin_state.shape[1]
    tile = (ROWS, LANES)
    rows, edges, low, high, gain, loss = call(
        stage_kernel,
        [
            ((rows_x, *tile), F32),
            ((2, *tile), F32),
            (tile, BF16),
            (tile, BF16),
            (gain_kernel.shape, BF16),
            (loss_rate.shape, BF16),
        ],
        [
            bin_state.shape,
            courant_x.shape,
            courant_y.shape,
            pltpu.SMEM(cloudy_order.shape, jnp.int32),
            pltpu.SemaphoreType.DMA((CLASSES + 5,)),
        ],
        block_count, cloudy_order, bin_state, courant_x, courant_y, gain_kernel, loss_rate,
        scalars=1, direct=6,
    )
    before, after = exchange("gy", high, low)
    *matrices, moves = prepare(gain, loss)
    (packed,) = call(
        pack_kernel,
        [((rows_x, SENT, LANES), BF16)],
        [(rows_x, SENT, LANES)],
        rows,
    )
    message = ((HALO * SENT + PAD, LANES), BF16)
    around, to_right, to_left = call(
        widen_kernel,
        [((1, *tile), F32), message, message],
        [],
        packed, before, after,
    )
    from_left, from_right = exchange("gx", to_right, to_left)
    inner = rows_x - HALO
    middle, fine, partial, early = call(
        inner_kernel,
        [((inner, *tile), F32), ((len(FINE), BINS * HEAD, 2 * LANES), F8), ((1, *tile), F32), ((2 * REACH, *tile), F32)],
        [(inner, *tile), (4, *tile), (inner, 8, LANES)],
        rows, edges, before, after, around, moves, *matrices,
        flops=5 * 10**9,
    )
    total = rows_x + HALO + 1
    (out,) = call(
        outer_kernel,
        [(bin_state.shape, F32)],
        [
            (HALO + 1, *tile),
            (HALO + 1, *tile),
            (total, *tile),
            (total, *tile),
            (4, *tile),
            (total, 8, LANES),
            (total, *tile),
            (HALO, SENT, LANES),
            bin_state.shape,
            (SUBLANES, LANES),
            pltpu.SemaphoreType.DMA((CLASSES,)),
        ],
        rows, partial, early, around, from_left, from_right, middle, moves, fine, *matrices,
        flops=20 * 10**9,
        stored=True,
    )
    return out


def solution(mesh):
    placed = (
        P(None, "gx", "gy"),
        P("gx", "gy"),
        P("gx", "gy"),
        P("gx", "gy", None),
        P("gy", "gx"),
        P(),
        P(),
    )
    sharded = jax.shard_map(
        per_device, mesh=mesh, in_specs=placed, out_specs=P(None, "gx", "gy"), check_vma=False
    )

    def run(*arguments):
        with jax.sharding.use_abstract_mesh(mesh.abstract_mesh):
            return sharded(*arguments)

    return run
```

```python
import functools
import jax
import jax.numpy as jnp
from jax import lax
from jax.experimental import pallas as pl
from jax.experimental.pallas import tpu as pltpu
from jax.sharding import PartitionSpec as P

BINS = 33
CLASSES = 4
LEV = 4
STEPS = 2
LANES = 128
SUBLANES = 8
OFF = (0, 40, 80, 128)
ROWS = 176
PAD = 40
HEAD = 32
LOOK = 14
HALO = 2 * STEPS
GROUP = HALO * LEV
AUX = BINS
FLAG = AUX + 4
EDGE = 2 * LANES - GROUP
DENSE = (0, BINS + 5, 2 * BINS + 5, 3 * BINS + 5)
SENT = DENSE[3] + PAD
REACH = HALO // 2
CORNER = REACH * GROUP
CHUNKS = tuple((OFF[member], OFF[member] + PAD) for member in range(CLASSES))
VMEM_LIMIT = 24 << 20

GROUPS = (
    (1, 0, ((0, 0, False), (1, 1, False))),
    (1, 1, ((4, 1, False),)),
    (2, 0, ((2, 2, False),)),
    (3, 3, ((3, 0, True), (6, 1, True), (8, 2, True), (9, 3, False))),
    (3, 2, ((5, 1, True), (7, 2, False))),
)
PAIRS = ((0, 0), (0, 1), (0, 2), (0, 3), (1, 1), (1, 2), (1, 3), (2, 2), (2, 3), (3, 3))
NG = len(GROUPS)
F32 = jnp.float32
BF16 = jnp.bfloat16
F8 = jnp.float8_e4m3fn
FINE = ((0, 80, 40, False), (1, 0, 40, False), (2, 0, -80, True), (4, -40, -80, True))
STAGES = (((3,), None), ((4,), 1), ((2,), None), ((0, 1), 0))
GAIN_SCALE = 4096.0
PEAK = 256.0
LOOK8 = 18
TOGETHER = 11


def prepare_kernel(gain, loss, blocks, tails, losses, moves, wide, turned, upper, last_rows):
    lane = lax.broadcasted_iota(jnp.int32, (PAD, LANES), 1)
    tiles = wide.shape[2] // LANES
    turned[...] = jnp.zeros_like(turned)
    slot_of = {}
    for _, _, members in GROUPS:
        for pair, _, second in members:
            if second:
                slot_of[pair] = len(slot_of)
    for pair in range(len(PAIRS)):
        wide[pair] = jnp.zeros((PAD, tiles * LANES), F32)
        wide[pair, :BINS, : BINS * BINS] = gain[pair].astype(F32)
        if pair in slot_of:
            for tile in range(tiles):
                part = wide[pair, :, tile * LANES : (tile + 1) * LANES]
                part = jnp.concatenate([part, jnp.zeros((LANES - PAD, LANES), F32)], axis=0)
                turned[slot_of[pair], tile * LANES : (tile + 1) * LANES, :] = part.T
    last_rows[...] = jnp.zeros_like(last_rows)
    for group, (_, _, members) in enumerate(GROUPS):
        for factor in range(BINS):
            halves = [jnp.zeros((PAD, LANES), F32), jnp.zeros((PAD, LANES), F32)]
            second_members = [m for m in members if m[2]]
            if second_members:
                rows = []
                for other in range(CLASSES - 1):
                    found = [m for m in second_members if m[1] == other]
                    if found:
                        piece = turned[slot_of[found[0][0]], pl.ds(factor, PAD, stride=BINS), :]
                        rows.append(piece)
                    else:
                        rows.append(jnp.zeros((PAD, LANES), F32))
                rows.append(jnp.zeros((LANES - 3 * PAD, LANES), F32))
                halves[0] = jnp.concatenate(rows, axis=0).T[:PAD]
            for pair, other, second in members:
                if second:
                    continue
                start = BINS * factor
                tile, inside = divmod(start, LANES)
                half, at = divmod(OFF[other], LANES)
                shift = (at - inside) % LANES
                first = wide[pair, :, tile * LANES : (tile + 1) * LANES]
                first = pltpu.roll(first, shift, 1) if shift else first
                if inside + BINS > LANES:
                    rest = wide[pair, :, (tile + 1) * LANES : (tile + 2) * LANES]
                    rest = pltpu.roll(rest, shift, 1) if shift else rest
                    first = jnp.where(lane < at + LANES - inside, first, rest)
                halves[half] = jnp.where((lane >= at) & (lane < at + BINS), first, halves[half])
            full = jnp.concatenate(halves, axis=1)
            blocks[group, factor * HEAD : (factor + 1) * HEAD, :] = full[:HEAD].astype(BF16)
            last_rows[group * PAD + factor : group * PAD + factor + 1, :] = full[HEAD : HEAD + 1]
    tails[...] = last_rows[...].astype(BF16)
    upper[...] = jnp.zeros_like(upper)
    for pair, (first, second) in enumerate(PAIRS):
        half, at = divmod(OFF[second], LANES)
        rates = jnp.concatenate(
            [loss[pair].astype(F32), jnp.zeros((BINS, LANES - BINS), F32)], axis=1
        )
        rates = pltpu.roll(rates, at, 1) if at else rates
        rows = slice(OFF[first], OFF[first] + BINS)
        span = slice(half * LANES, (half + 1) * LANES)
        upper[rows, span] = upper[rows, span] + rates
    whole = upper[...]
    losses[...] = (whole + whole.T)[: losses.shape[0]].astype(BF16)
    fill_moves(moves)


def fill_moves(moves):
    moves[...] = jnp.zeros_like(moves)
    for part, step in enumerate((LEV, 2 * LEV)):
        source = lax.broadcasted_iota(jnp.int32, (LANES, LANES), 0)
        target = lax.broadcasted_iota(jnp.int32, (LANES, LANES), 1)
        moves[part, :LANES, :LANES] = jnp.where(source == target - step, 1.0, 0.0).astype(BF16)
        moves[part, :LANES, LANES:] = jnp.where(source == target + step, 1.0, 0.0).astype(BF16)
        source, target = source[:GROUP], target[:GROUP]
        half = GROUP // 2
        low = (target < step) & (source == target + half - step)
        high = (target >= LANES - step) & (source == target - (LANES - step) + half)
        rows = slice(EDGE, EDGE + GROUP)
        moves[part, rows, :LANES] = jnp.where(low, 1.0, 0.0).astype(BF16)
        moves[part, rows, LANES:] = jnp.where(high, 1.0, 0.0).astype(BF16)


def prepare(gain_kernel, loss_rate):
    wide = -(-BINS * BINS // LANES) * LANES
    tail = -(-NG * PAD // 16) * 16
    rows = -(-ROWS // 16) * 16
    return pl.pallas_call(
        prepare_kernel,
        out_shape=(
            jax.ShapeDtypeStruct((NG, BINS * HEAD, 2 * LANES), BF16),
            jax.ShapeDtypeStruct((tail, 2 * LANES), BF16),
            jax.ShapeDtypeStruct((rows, 2 * LANES), BF16),
            jax.ShapeDtypeStruct((2, EDGE + LANES, 2 * LANES), BF16),
        ),
        scratch_shapes=[
            pltpu.VMEM((len(PAIRS), PAD, wide), F32),
            pltpu.VMEM((4, BINS * PAD + BINS, LANES), F32),
            pltpu.VMEM((2 * LANES, 2 * LANES), F32),
            pltpu.VMEM((tail, 2 * LANES), F32),
        ],
        compiler_params=pltpu.CompilerParams(vmem_limit_bytes=VMEM_LIMIT),
        cost_estimate=pl.CostEstimate(flops=2 * 10**9, bytes_accessed=4 << 20, transcendentals=0),
    )(gain_kernel, loss_rate)


def collide_tiles(bins, row0, blocks, tails, losses, slots, ends, sinks, emit):
    for unit in range(2):
        right = jnp.concatenate([bins[row0 + 2 * unit], bins[row0 + 2 * unit + 1]], axis=1)
        right = jnp.concatenate(
            [right, jnp.zeros((2 * LANES - ROWS, 2 * LANES), F32)], axis=0
        ).astype(BF16)
        pltpu.matmul_push_rhs(right, 0, unit)
    for unit in range(2):
        pltpu.matmul_acc_lhs(ends[unit], tails[...], 0)
    for unit in range(2):
        pltpu.matmul_acc_lhs(sinks[unit], losses[...])
    depth = len(slots[0])
    pending, count = [], 0
    parts = {t: [[jnp.zeros((HEAD, LANES), F32) for _ in range(2)] for _ in range(2)] for t in (1, 2, 3)}

    def drain():
        target, source, factor, slot = pending.pop(0)
        for unit in range(2):
            block = pltpu.matmul_pop(slots[unit][slot])
            for half in range(2):
                scale = bins[row0 + 2 * unit + half, pl.ds(OFF[source] + factor, 1), :]
                part = block[:, half * LANES : (half + 1) * LANES]
                parts[target][unit][half] = parts[target][unit][half] + part * scale

    last = [[[jnp.zeros((PAD, LANES), F32) for _ in range(2)] for _ in range(2)] for _ in range(4)]
    for unit in range(2):
        block = pltpu.matmul_pop(ends[unit])
        for group, (target, source, _) in enumerate(GROUPS):
            for half in range(2):
                scale = bins[row0 + 2 * unit + half, OFF[source] : OFF[source] + PAD, :]
                piece = block[group * PAD : (group + 1) * PAD, half * LANES : (half + 1) * LANES]
                last[target][unit][half] = last[target][unit][half] + piece * scale
    drop = [pltpu.matmul_pop(sinks[unit]) for unit in range(2)]
    for unit in range(2):
        for half in range(2):
            row = row0 + 2 * unit + half
            for member in range(CLASSES):
                rows = slice(OFF[member], OFF[member] + PAD)
                lost = drop[unit][rows, half * LANES : (half + 1) * LANES] * bins[row, rows, :]
                if member:
                    bottom = jnp.sum(last[member][unit][half], axis=0, keepdims=True)
                    bottom = jnp.concatenate([bottom, jnp.zeros((PAD - HEAD - 1, LANES), F32)], axis=0)
                    base = jnp.concatenate([-lost[:HEAD], bottom - lost[HEAD:]], axis=0)
                else:
                    base = -lost
                emit(2 * unit + half, member, None, base)
    for target in (1, 2, 3):
        order = [
            (group, source, factor)
            for factor in range(BINS)
            for group, (aim, source, _) in enumerate(GROUPS)
            if aim == target
        ]
        for group, source, factor in order:
            slot = count % depth
            count += 1
            left = blocks[group, factor * HEAD : (factor + 1) * HEAD, :]
            for unit in range(2):
                pltpu.matmul_acc_lhs(slots[unit][slot], left)
            pending.append((target, source, factor, slot))
            if len(pending) > LOOK:
                drain()
        while pending:
            drain()
        for unit in range(2):
            for half in range(2):
                emit(2 * unit + half, target, parts[target][unit][half], None)


def collide_fine(bins, row0, blocks, tails, losses, fine, scale, slots, ends, sinks, emit):
    for unit in range(2):
        right = jnp.concatenate([bins[row0 + 2 * unit], bins[row0 + 2 * unit + 1]], axis=1)
        right = jnp.concatenate(
            [right, jnp.zeros((2 * LANES - ROWS, 2 * LANES), F32)], axis=0
        ).astype(BF16)
        pltpu.matmul_push_rhs(right, 0, unit)
    for unit in range(2):
        pltpu.matmul_acc_lhs(ends[unit], tails[...], 0)
    for unit in range(2):
        pltpu.matmul_acc_lhs(sinks[unit], losses[...])
    for unit in range(2):
        rows = (row0 + 2 * unit, row0 + 2 * unit + 1)
        pltpu.matmul_push_rhs(fine_bins(bins, rows, scale, True), 1, unit)
    last = [[[jnp.zeros((PAD, LANES), F32) for _ in range(2)] for _ in range(2)] for _ in range(4)]
    for unit in range(2):
        block = pltpu.matmul_pop(ends[unit])
        for group, (target, source, _) in enumerate(GROUPS):
            for half in range(2):
                factor = bins[row0 + 2 * unit + half, OFF[source] : OFF[source] + PAD, :]
                piece = block[group * PAD : (group + 1) * PAD, half * LANES : (half + 1) * LANES]
                last[target][unit][half] = last[target][unit][half] + piece * factor
    drop = [pltpu.matmul_pop(sinks[unit]) for unit in range(2)]
    for unit in range(2):
        for half in range(2):
            row = row0 + 2 * unit + half
            for member in range(CLASSES):
                rows = slice(OFF[member], OFF[member] + PAD)
                lost = drop[unit][rows, half * LANES : (half + 1) * LANES] * bins[row, rows, :]
                if member:
                    bottom = jnp.sum(last[member][unit][half], axis=0, keepdims=True)
                    bottom = jnp.concatenate([bottom, jnp.zeros((PAD - HEAD - 1, LANES), F32)], axis=0)
                    base = jnp.concatenate([-lost[:HEAD], bottom - lost[HEAD:]], axis=0)
                else:
                    base = -lost
                emit(2 * unit + half, member, None, base)
    down = 1.0 / (scale * GAIN_SCALE)
    place = {group: index for index, (group, *_) in enumerate(FINE)}
    stages = STAGES
    depth = len(slots[0])
    sums = [
        [[jnp.zeros((HEAD, LANES), F32) for _ in range(2)] for _ in range(2)] for _ in stages
    ]
    left_over = [BINS * len(groups) for groups, _ in stages]
    pending, count = [], 0

    def drain():
        stage, source, factor, slot = pending.pop(0)
        for unit in range(2):
            block = pltpu.matmul_pop(slots[unit][slot])
            for half in range(2):
                scaled = bins[row0 + 2 * unit + half, pl.ds(OFF[source] + factor, 1), :]
                part = block[:, half * LANES : (half + 1) * LANES]
                sums[stage][unit][half] = sums[stage][unit][half] + part * scaled
        left_over[stage] -= 1
        if left_over[stage] or not stage:
            return
        target = (None, 3, 2, 1)[stage]
        for unit in range(2):
            for half in range(2):
                total = sums[stage][unit][half] * down
                if target == 3:
                    total = total + sums[0][unit][half]
                emit(2 * unit + half, target, total, None)

    for stage, (groups, staged) in enumerate(stages):
        for factor in range(BINS):
            for group in groups:
                slot = count % depth
                count += 1
                rows = slice(factor * HEAD, (factor + 1) * HEAD)
                left = fine[place[group], rows, :] if group in place else blocks[group, rows, :]
                for unit in range(2):
                    pltpu.matmul_acc_lhs(slots[unit][slot], left, staged)
                if staged == 1:
                    for unit in range(2):
                        pair = (row0 + 2 * unit, row0 + 2 * unit + 1)
                        right = fine_bins(bins, pair, scale, False)
                        pltpu.matmul_push_rhs(right, 0, unit)
                staged = None
                pending.append((stage, GROUPS[group][1], factor, slot))
                if len(pending) > LOOK8:
                    drain()
    while pending:
        drain()


def accumulators(depth, tail, rows):
    return (
        [pltpu.ACC(unit)((HEAD, 2 * LANES), F32) for unit in range(2) for _ in range(depth)]
        + [pltpu.ACC(unit)((tail, 2 * LANES), F32) for unit in range(2)]
        + [pltpu.ACC(unit)((rows, 2 * LANES), F32) for unit in range(2)]
    )


def settle(field, mask, change, row, place):
    def emit(index, member, gained, base):
        at = row(index)
        start = OFF[member]
        if base is not None and member:
            change[place(index), start : start + PAD, :] = base
            return
        if member:
            base = change[place(index), start : start + PAD, :]
            base = jnp.concatenate([base[:HEAD] + gained, base[HEAD:]], axis=0)
        part = jnp.where(mask[at, :1, :] > 0.5, base.astype(BF16).astype(F32), 0.0)
        span = slice(start, start + PAD)
        field[at, span, :] = field[at, span, :] + part

    return emit


def four_rows(bins, row0, matrices, refs, field, mask, change, fine=None, scale=None):
    depth = LOOK + 2 if fine is None else LOOK8 + 2
    slots = (refs[:depth], refs[depth : 2 * depth])
    ends, sinks = refs[2 * depth : 2 * depth + 2], refs[2 * depth + 2 :]
    emit = settle(field, mask, change, lambda index: row0 + index, lambda index: index)
    if fine is None:
        collide_tiles(bins, row0, *matrices, slots, ends, sinks, emit)
    else:
        collide_fine(bins, row0, *matrices, fine, scale, slots, ends, sinks, emit)


def one_row(bins, row, matrices, refs, field, mask, change, fine, scale):
    blocks, tails, losses = matrices
    depth = LOOK8 + 2
    slots = (refs[:depth], refs[depth : 2 * depth])
    end, sink = refs[2 * depth], refs[2 * depth + 3]
    right = bins[row]
    right = jnp.concatenate([right, jnp.zeros((2 * LANES - ROWS, LANES), F32)], axis=0)
    right = jnp.concatenate([right, jnp.zeros((2 * LANES, LANES), F32)], axis=1).astype(BF16)
    for unit in range(2):
        pltpu.matmul_push_rhs(right, 0, unit)
    pltpu.matmul_acc_lhs(end, tails[...], 0)
    pltpu.matmul_acc_lhs(sink, losses[...], 0)
    for unit in range(2):
        pltpu.matmul_push_rhs(fine_bins(bins, (row,), scale, True), 1, unit)
    emit = settle(field, mask, change, lambda index: row, lambda index: 0)
    block = pltpu.matmul_pop(end)[:, :LANES]
    last = [jnp.zeros((PAD, LANES), F32) for _ in range(CLASSES)]
    for group, (target, source, _) in enumerate(GROUPS):
        column = bins[row, OFF[source] : OFF[source] + PAD, :]
        last[target] = last[target] + block[group * PAD : (group + 1) * PAD] * column
    drop = pltpu.matmul_pop(sink)[:, :LANES]
    for member in range(CLASSES):
        span = slice(OFF[member], OFF[member] + PAD)
        base = -drop[span] * bins[row, span, :]
        if member:
            bottom = jnp.sum(last[member], axis=0, keepdims=True)
            bottom = jnp.concatenate([bottom, jnp.zeros((PAD - HEAD - 1, LANES), F32)], axis=0)
            base = jnp.concatenate([base[:HEAD], bottom + base[HEAD:]], axis=0)
        emit(0, member, None, base)
    place = {group: index for index, (group, *_) in enumerate(FINE)}
    sums = [[jnp.zeros((HEAD, LANES), F32) for _ in range(2)] for _ in STAGES]
    pending, count = [], 0

    def drain():
        stage, source, factor, unit, slot = pending.pop(0)
        part = pltpu.matmul_pop(slots[unit][slot])[:, :LANES]
        factors = bins[row, OFF[source] + factor : OFF[source] + factor + 1, :]
        sums[stage][unit] = sums[stage][unit] + part * factors

    for stage, (groups, staged) in enumerate(STAGES):
        fresh = [staged, staged]
        for factor in range(BINS):
            for group in groups:
                unit, slot = count % 2, (count // 2) % len(slots[0])
                count += 1
                rows = slice(factor * HEAD, (factor + 1) * HEAD)
                left = fine[place[group], rows, :] if group in place else blocks[group, rows, :]
                pltpu.matmul_acc_lhs(slots[unit][slot], left, fresh[unit])
                if fresh[unit] == 1:
                    pltpu.matmul_push_rhs(fine_bins(bins, (row,), scale, False), 0, unit)
                fresh[unit] = None
                pending.append((stage, GROUPS[group][1], factor, unit, slot))
                if len(pending) > 2 * LOOK8:
                    drain()
    while pending:
        drain()
    down = 1.0 / (scale * GAIN_SCALE)
    wide, *narrow = [first + second for first, second in sums]
    for target, total in zip((3, 2, 1), narrow):
        total = total * down
        emit(0, target, total + wide if target == 3 else total, None)


def weights(tile, row):
    out, centre = [], 1.0
    for axis in range(2):
        first, second = (
            jnp.broadcast_to(tile[row, pl.ds(AUX + 2 * axis + part, 1), :], (SUBLANES, LANES))
            for part in range(2)
        )
        speed = (first + second) * (1.0 / 6.0)
        rising, falling = jnp.maximum(speed, 0.0), jnp.minimum(speed, 0.0)
        centre = centre - 3.0 * (rising - falling)
        out.append(
            (
                6.0 * rising + 2.0 * falling,
                -rising,
                -2.0 * rising - 6.0 * falling,
                falling,
            )
        )
    return centre, out


def cells(value):
    return value.reshape(value.shape[0] // SUBLANES, SUBLANES, LANES)


def advance(centre, along_x, along_y, coefficients):
    middle, (for_x, for_y) = coefficients
    total = middle * centre
    for values, factors in ((along_x, for_x), (along_y, for_y)):
        for value, factor in zip(values, factors):
            total = total + factor * value
    return jnp.maximum(total, 0.0)


def shifted(value, amount):
    amount = amount % LANES
    return pltpu.roll(value, amount, value.ndim - 1) if amount else value


def travel(jobs, moves, refs, finish):
    def issue(number, job):
        row, outside, place = job
        left = jnp.concatenate([row().astype(BF16), outside().astype(BF16)], axis=1)
        for unit in range(2):
            start = EDGE - GROUP * place
            right = [moves[unit, :LANES, :], moves[unit, start : start + LANES, :]]
            pltpu.matmul_push_rhs(jnp.concatenate(right, axis=0), number % 2, unit)
            pltpu.matmul_acc_lhs(refs[2 * (number % 2) + unit], left, number % 2)

    for number in range(len(jobs) + 1):
        if number < len(jobs):
            issue(number, jobs[number])
        if number:
            one, two = (pltpu.matmul_pop(refs[2 * ((number - 1) % 2) + unit]) for unit in range(2))
            finish(number - 1, (one[:, :LANES], two[:, :LANES], one[:, LANES:], two[:, LANES:]))


def travellers():
    return [pltpu.ACC(unit)((ROWS, 2 * LANES), F32) for _ in range(2) for unit in range(2)]


def lanes():
    return lax.broadcasted_iota(jnp.int32, (SUBLANES, LANES), 1)


def put(field, bins, row, span, value, peak=None):
    if peak is not None:
        peak[...] = jnp.maximum(peak[...], jnp.max(value, axis=0))
    value = value.reshape(PAD, LANES)
    field[row, span, :] = value
    bins[row, span, :] = value.astype(BF16).astype(F32)


def clear_gap(*arrays):
    for start, stop in ((OFF[2] + PAD, OFF[3]), (OFF[3] + PAD, ROWS)):
        for array in arrays:
            for row in range(array.shape[0]):
                array[row, start:stop, :] = jnp.zeros((stop - start, LANES), F32)


def stage_kernel(
    count, order_hbm, state_hbm, courant_x_hbm, courant_y_hbm, gain_hbm, loss_hbm,
    rows, edges, low, high, gain, loss, state, courant_x, courant_y, order, arrived,
):
    rows_x = state.shape[1]
    flat = state.reshape(state.shape[0] * rows_x, LANES)
    pieces = [
        (state_hbm.at[pl.ds(member * BINS, BINS)], state.at[pl.ds(member * BINS, BINS)])
        for member in range(CLASSES)
    ]
    pieces += [(courant_x_hbm, courant_x), (courant_y_hbm, courant_y)]
    pieces += [(order_hbm, order)]
    pieces += [(gain_hbm, gain), (loss_hbm, loss)]
    copies = [
        pltpu.make_async_copy(source, target, arrived.at[number])
        for number, (source, target) in enumerate(pieces)
    ]
    for copy in copies:
        copy.start()
    for copy in copies[:-2]:
        copy.wait()
    spare = jnp.zeros((PAD - BINS, LANES), F32)
    for row in range(rows_x):
        cloudy = jnp.int32(0)
        for place in range(rows_x):
            hit = (order[0, 0, place] == row) & (place < count[0, 0])
            cloudy = cloudy | hit.astype(jnp.int32)
        for member in range(CLASSES):
            part = flat[pl.ds(member * BINS * rows_x + row, BINS, stride=rows_x), :]
            rows[row, OFF[member] : OFF[member] + BINS, :] = part
            rows[row, OFF[member] + BINS : OFF[member] + PAD, :] = spare
        for axis, courant in enumerate((courant_x, courant_y)):
            speed = courant[row : row + 1, :]
            upper = speed.astype(BF16).astype(F32)
            rows[row, AUX + 2 * axis : AUX + 2 * axis + 1, :] = upper
            rows[row, AUX + 2 * axis + 1 : AUX + 2 * axis + 2, :] = speed - upper
        rows[row, FLAG : FLAG + 1, :] = jnp.full((1, LANES), cloudy.astype(F32), F32)
    clear_gap(rows, edges)
    owner = lanes() // GROUP
    for start, stop in CHUNKS:
        left = jnp.zeros((PAD // SUBLANES, SUBLANES, LANES), F32)
        right = left
        for row in range(rows_x):
            value = cells(rows[row, start:stop, :])
            left = jnp.where(owner == row, shifted(value, GROUP * row), left)
            right = jnp.where(owner == row, shifted(value, GROUP * (row + 1)), right)
        edges[0, start:stop, :] = left.reshape(PAD, LANES)
        edges[1, start:stop, :] = right.reshape(PAD, LANES)
    low[...] = edges[0].astype(BF16)
    high[...] = edges[1].astype(BF16)
    for copy in copies[-2:]:
        copy.wait()


def pack_kernel(rows, packed, dense):
    for row in range(rows.shape[0]):
        for (start, stop), first in zip(CHUNKS, DENSE):
            dense[row, first : first + PAD, :] = rows[row, start:stop, :]
        packed[row] = dense[row].astype(BF16)


def widen_kernel(packed, before, after, around, to_right, to_left):
    rows_x = packed.shape[0]
    inner = lanes() % GROUP < GROUP // 2
    block = lanes() // CORNER
    corners = [None, None]
    for member, (start, stop) in enumerate(CHUNKS):
        near = jnp.where(
            inner,
            shifted(cells(before[start:stop].astype(F32)), -GROUP // 2),
            shifted(cells(after[start:stop].astype(F32)), GROUP // 2),
        )
        around[0, start:stop, :] = near.reshape(PAD, LANES)
        for side, first in enumerate((LANES - CORNER, 0)):
            moved = shifted(near, CORNER * member - first)
            old = corners[side]
            corners[side] = moved if old is None else jnp.where(block == member, moved, old)
    clear_gap(around)
    for index in range(HALO):
        span = slice(index * SENT, (index + 1) * SENT)
        to_right[span, :] = packed[rows_x - HALO + index]
        to_left[span, :] = packed[index]
    for target, corner in zip((to_right, to_left), corners):
        target[HALO * SENT :, :] = corner.reshape(PAD, LANES).astype(BF16)


def unpack(sent, tiles, dense, first_lane):
    for index in range(HALO):
        dense[index] = sent[index * SENT : (index + 1) * SENT, :].astype(F32)
        for (start, stop), first in zip(CHUNKS, DENSE):
            tiles[index, start:stop, :] = dense[index, first : first + PAD, :]
    corner = cells(sent[HALO * SENT :, :].astype(F32))
    for member, (start, stop) in enumerate(CHUNKS):
        moved = shifted(corner, first_lane - CORNER * member)
        tiles[HALO, start:stop, :] = moved.reshape(PAD, LANES)


def split_gains(blocks, fine):
    lane = lax.broadcasted_iota(jnp.int32, (HEAD, LANES), 1)

    @pl.loop(0, BINS // TOGETHER)
    def _(step):
        for part in range(TOGETHER):
            start = pl.multiple_of((step * TOGETHER + part) * HEAD, HEAD)
            rows = pl.ds(start, HEAD)
            for index, (group, first, second, high) in enumerate(FINE):
                gain = blocks[group, rows, :LANES].astype(F32) * GAIN_SCALE
                upper = gain.astype(F8).astype(F32)
                rest = gain - upper
                kept = lane >= PAD if high else lane < 2 * PAD
                left = jnp.where(kept, upper, shifted(upper, first)) if first else upper
                right = jnp.where(kept, rest, shifted(upper, second))
                fine[index, rows, :] = jnp.concatenate([left, right], axis=1).astype(F8)


def fine_bins(bins, rows, scale, high):
    parts = []
    for member in (1, 2) if high else (0, 1):
        span = slice(OFF[member], OFF[member] + PAD)
        halves = [bins[row, span, :] * scale for row in rows]
        if len(halves) == 1:
            halves.append(jnp.zeros_like(halves[0]))
        value = jnp.concatenate(halves, axis=1)
        upper = value.astype(F8).astype(F32)
        parts.append((upper, value - upper))
    (one, one_rest), (two, two_rest) = parts
    gap = jnp.zeros((LANES - 3 * PAD, 2 * LANES), F32)
    if high:
        order = [one_rest, one, two, gap, two_rest, one, two, gap]
    else:
        order = [one, two, one_rest, gap, one, two, two_rest, gap]
    return jnp.concatenate(order, axis=0).astype(F8)


def scale_of(peak):
    top, scale = jnp.max(peak[...]), jnp.float32(2.0**-40)
    for power in (64, 32, 16, 8, 4, 2, 1):
        larger = scale * jnp.float32(2.0**power)
        scale = jnp.where(top * larger <= PEAK, larger, scale)
    return scale


STEPS_AWAY = (-1, -2, 1, 2)


def border_columns(rows_x):
    return list(range(REACH)) + list(range(rows_x - REACH, rows_x))


def flank(edges, before, after, around, partial):
    middle, (_, for_y) = weights(around, 0)
    inside = lanes() % GROUP
    half = GROUP // 2
    for start, stop in CHUNKS:
        span = slice(start, stop)
        lower, upper = cells(before[span, :].astype(F32)), cells(after[span, :].astype(F32))
        first, last = cells(edges[0, span, :]), cells(edges[1, span, :])
        along_y = (
            jnp.where(
                inside < half + LEV,
                shifted(jnp.where(inside < half + LEV, lower, last), -LEV),
                shifted(upper, half + LEV),
            ),
            jnp.where(inside < half, lower, last),
            jnp.where(
                inside < LEV,
                shifted(lower, -half - LEV),
                shifted(jnp.where(inside < LEV, first, upper), LEV),
            ),
            jnp.where(inside < half, first, upper),
        )
        total = middle * cells(around[0, span, :])
        for value, factor in zip(along_y, for_y):
            total = total + factor * value
        partial[0, span, :] = total.reshape(PAD, LANES)
    clear_gap(partial)


def inner_kernel(
    rows, edges, before, after, around, moves, blocks, tails, losses,
    out, fine, partial, early, bins, change, mask,
):
    split_gains(blocks, fine)
    flank(edges, before, after, around, partial)
    rows_x = rows.shape[0]
    clear_gap(out, bins)
    places = [index + HALO // 2 for index in range(rows_x - HALO)]

    places += border_columns(rows_x)

    def finish(index, along_y):
        row = places[index]
        coefficients = weights(rows, row)
        within = index < rows_x - HALO
        if within:
            mask[index] = jnp.broadcast_to(rows[row, FLAG : FLAG + 1, :], mask.shape[1:])
        for start, stop in CHUNKS:
            span = slice(start, stop)
            centre = cells(rows[row, span, :])
            beside = [cells(value[span]) for value in along_y]
            if within:
                along_x = [cells(rows[row + d, span, :]) for d in STEPS_AWAY]
                put(out, bins, index, span, advance(centre, along_x, beside, coefficients))
                continue
            middle, (for_x, for_y) = coefficients
            total = middle * centre
            for value, factor in zip(beside, for_y):
                total = total + factor * value
            for d, factor in zip(STEPS_AWAY, for_x):
                if 0 <= row + d < rows_x:
                    total = total + factor * cells(rows[row + d, span, :])
            early[index - rows_x + HALO, span, :] = total.reshape(PAD, LANES)

    jobs = [(lambda row=row: rows[row], lambda: around[0], row) for row in places]
    pl.run_scoped(lambda *refs: travel(jobs, moves, refs, finish), *travellers())
    matrices = (blocks, tails, losses)
    pl.run_scoped(
        lambda *refs: four_rows(bins, 0, matrices, refs, out, mask, change),
        *accumulators(LOOK + 2, tails.shape[0], losses.shape[0]),
    )


def outer_kernel(
    rows, partial, early, around, from_left, from_right, middle, moves, fine, blocks, tails, losses,
    out_hbm, left, right, field, bins, change, mask, second, dense, out, peak, sent,
):
    rows_x = rows.shape[0]
    lane = lanes()
    outside = rows_x + HALO
    unpack(from_left, left, dense, LANES - CORNER)
    unpack(from_right, right, dense, 0)
    clear_gap(field, bins, second, left, right)
    peak[...] = jnp.zeros_like(peak)

    def column(x):
        if x < 0:
            return left, x + HALO
        if x >= rows_x:
            return right, x - rows_x
        return rows, x

    def outer_columns(x):
        if x < 0:
            return (lambda: left[HALO]), x + rows_x
        if x >= rows_x:
            return (lambda: right[HALO]), x - rows_x
        return (lambda: around[0]), x

    reach = HALO // 2
    places = list(range(-reach, 0)) + list(range(rows_x, rows_x + reach))

    def job(x):
        tile, row = column(x)
        return (lambda: tile[row], *outer_columns(x))

    def first_step(index, beside):
        x = places[index]
        tile, row = column(x)
        coefficients = weights(tile, row)
        mask[x + reach] = jnp.broadcast_to(tile[row, FLAG : FLAG + 1, :], mask.shape[1:])
        for start, stop in CHUNKS:
            span = slice(start, stop)
            centre = cells(tile[row, span, :])
            along_x = []
            for d in (-1, -2, 1, 2):
                other, at = column(x + d)
                along_x.append(cells(other[at, span, :]))
            along_y = [cells(value[span]) for value in beside]
            put(field, bins, x + reach, span, advance(centre, along_x, along_y, coefficients), peak)

    jobs = [job(x) for x in places]
    pl.run_scoped(lambda *refs: travel(jobs, moves, refs, first_step), *travellers())
    for index, x in enumerate(border_columns(rows_x)):
        _, (for_x, _) = weights(rows, x)
        mask[x + reach] = jnp.broadcast_to(rows[x, FLAG : FLAG + 1, :], mask.shape[1:])
        for start, stop in CHUNKS:
            span = slice(start, stop)
            total = cells(early[index, span, :])
            for d, factor in zip(STEPS_AWAY, for_x):
                if not 0 <= x + d < rows_x:
                    tile, row = column(x + d)
                    total = total + factor * cells(tile[row, span, :])
            put(field, bins, x + reach, span, jnp.maximum(total, 0.0), peak)
    _, (for_x, _) = weights(around, 0)
    mask[outside] = jnp.broadcast_to(around[0, FLAG : FLAG + 1, :], mask.shape[1:])
    for start, stop in CHUNKS:
        span = slice(start, stop)
        centre = cells(around[0, span, :])
        beyond = jnp.where(
            lane >= LANES // 2, cells(left[HALO, span, :]), cells(right[HALO, span, :])
        )
        along_x = (
            shifted(jnp.where(lane >= LANES - GROUP, beyond, centre), GROUP),
            shifted(jnp.where(lane >= LANES - 2 * GROUP, beyond, centre), 2 * GROUP),
            shifted(jnp.where(lane < GROUP, beyond, centre), -GROUP),
            shifted(jnp.where(lane < 2 * GROUP, beyond, centre), -2 * GROUP),
        )
        total = cells(partial[0, span, :])
        for value, factor in zip(along_x, for_x):
            total = total + factor * value
        put(field, bins, outside, span, jnp.maximum(total, 0.0), peak)
    for index in range(rows_x - HALO):
        field[index + HALO] = middle[index]
        row = index + reach
        mask[index + HALO] = jnp.broadcast_to(rows[row, FLAG : FLAG + 1, :], mask.shape[1:])
    matrices = (blocks, tails, losses)

    def first_collisions(*refs):
        scale = scale_of(peak)
        one_row(bins, outside, matrices, refs, field, mask, change, fine, scale)

        @pl.loop(0, 2)
        def _(step):
            four_rows(bins, rows_x * step, matrices, refs, field, mask, change, fine, scale)

    def second_step(x, beside):
        coefficients = weights(rows, x)
        for start, stop in CHUNKS:
            span = slice(start, stop)
            centre = cells(field[x + reach, span, :])
            along_x = [cells(field[x + reach + d, span, :]) for d in (-1, -2, 1, 2)]
            along_y = [cells(value[span]) for value in beside]
            put(second, bins, x + reach, span, advance(centre, along_x, along_y, coefficients), peak)

    def second_collisions(*refs):
        scale = scale_of(peak)

        @pl.loop(0, rows_x // 4)
        def _(step):
            row0 = reach + 4 * step
            four_rows(bins, row0, matrices, refs, second, mask, change, fine, scale)

    sizes = (tails.shape[0], losses.shape[0])
    shapes = accumulators(LOOK8 + 2, *sizes)
    pl.run_scoped(first_collisions, *shapes)
    peak[...] = jnp.zeros_like(peak)
    later = [(lambda x=x: field[x + reach], lambda: field[outside], x) for x in range(rows_x)]
    pl.run_scoped(lambda *refs: travel(later, moves, refs, second_step), *travellers())
    pl.run_scoped(second_collisions, *shapes)
    flat = out.reshape(out.shape[0] * rows_x, LANES)
    copies = []
    for member in range(CLASSES):
        for x in range(rows_x):
            span = pl.ds(member * BINS * rows_x + x, BINS, stride=rows_x)
            flat[span, :] = second[x + reach, OFF[member] : OFF[member] + BINS, :]
        part = pl.ds(member * BINS, BINS)
        copies.append(pltpu.make_async_copy(out.at[part], out_hbm.at[part], sent.at[member]))
        copies[-1].start()
    for copy in copies:
        copy.wait()


def call(kernel, outs, scratch, *arguments, scalars=0, direct=0, flops=0, stored=False):
    smem = pl.BlockSpec(memory_space=pltpu.SMEM)
    vmem = pl.BlockSpec(memory_space=pltpu.VMEM)
    hbm = pl.BlockSpec(memory_space=pltpu.HBM)
    shapes = tuple(jax.ShapeDtypeStruct(shape, dtype) for shape, dtype in outs)
    moved = sum(a.size * a.dtype.itemsize for a in arguments)
    own = [pltpu.VMEM(piece, F32) if isinstance(piece, tuple) else piece for piece in scratch]
    staged = scalars + direct
    held = [pltpu.with_memory_space_constraint(a, pltpu.HBM) for a in arguments[scalars:staged]]
    return pl.pallas_call(
        kernel,
        out_shape=shapes,
        in_specs=[smem] * scalars + [hbm] * direct + [vmem] * (len(arguments) - staged),
        out_specs=tuple(hbm if stored else vmem for _ in shapes),
        scratch_shapes=own,
        compiler_params=pltpu.CompilerParams(vmem_limit_bytes=VMEM_LIMIT),
        cost_estimate=pl.CostEstimate(flops=flops, bytes_accessed=moved, transcendentals=0),
    )(*arguments[:scalars], *held, *arguments[staged:])


def exchange(axis, upward, downward):
    size = lax.axis_size(axis)
    up = [(i, (i + 1) % size) for i in range(size)]
    down = [(j, i) for i, j in up]
    return lax.ppermute(upward, axis, up), lax.ppermute(downward, axis, down)


def per_device(bin_state, courant_x, courant_y, cloudy_order, block_count, gain_kernel, loss_rate):
    rows_x = bin_state.shape[1]
    tile = (ROWS, LANES)
    roomy = ((CLASSES - 1) * BINS + PAD, *bin_state.shape[1:])
    rows, edges, low, high, gain, loss = call(
        stage_kernel,
        [
            ((rows_x, *tile), F32),
            ((2, *tile), F32),
            (tile, BF16),
            (tile, BF16),
            (gain_kernel.shape, BF16),
            (loss_rate.shape, BF16),
        ],
        [
            roomy,
            courant_x.shape,
            courant_y.shape,
            pltpu.SMEM(cloudy_order.shape, jnp.int32),
            pltpu.SemaphoreType.DMA((CLASSES + 5,)),
        ],
        block_count, cloudy_order, bin_state, courant_x, courant_y, gain_kernel, loss_rate,
        scalars=1, direct=6,
    )
    before, after = exchange("gy", high, low)
    *matrices, moves = prepare(gain, loss)
    (packed,) = call(
        pack_kernel,
        [((rows_x, SENT, LANES), BF16)],
        [(rows_x, SENT, LANES)],
        rows,
    )
    message = ((HALO * SENT + PAD, LANES), BF16)
    around, to_right, to_left = call(
        widen_kernel,
        [((1, *tile), F32), message, message],
        [],
        packed, before, after,
    )
    from_left, from_right = exchange("gx", to_right, to_left)
    inner = rows_x - HALO
    middle, fine, partial, early = call(
        inner_kernel,
        [((inner, *tile), F32), ((len(FINE), BINS * HEAD, 2 * LANES), F8), ((1, *tile), F32), ((2 * REACH, *tile), F32)],
        [(inner, *tile), (4, *tile), (inner, 8, LANES)],
        rows, edges, before, after, around, moves, *matrices,
        flops=5 * 10**9,
    )
    total = rows_x + HALO + 1
    (out,) = call(
        outer_kernel,
        [(bin_state.shape, F32)],
        [
            (HALO + 1, *tile),
            (HALO + 1, *tile),
            (total, *tile),
            (total, *tile),
            (4, *tile),
            (total, 8, LANES),
            (total, *tile),
            (HALO, SENT, LANES),
            roomy,
            (SUBLANES, LANES),
            pltpu.SemaphoreType.DMA((CLASSES,)),
        ],
        rows, partial, early, around, from_left, from_right, middle, moves, fine, *matrices,
        flops=20 * 10**9,
        stored=True,
    )
    return out


def solution(mesh):
    placed = (
        P(None, "gx", "gy"),
        P("gx", "gy"),
        P("gx", "gy"),
        P("gx", "gy", None),
        P("gy", "gx"),
        P(),
        P(),
    )
    sharded = jax.shard_map(
        per_device, mesh=mesh, in_specs=placed, out_specs=P(None, "gx", "gy"), check_vma=False
    )

    def run(*arguments):
        with jax.sharding.use_abstract_mesh(mesh.abstract_mesh):
            return sharded(*arguments)

    return run
```
